512 devices in a mesh: gy: 32 (over z, x), gx: 16 (over y, core).
Axes of the slice: x: 4, y: 8, z: 8, core: 2. Of those that a mesh axis runs over, the one named last changes fastest.
Arguments:
- ensemble: float32 [64, 256, 2048], P(None, 'gy', 'gx'), may hold values from -6 to 6
- flow: float32 [3, 256, 2048], P(None, 'gy', 'gx')
- obs_cell: int32 [32, 16, 4], P('gy', 'gx'), may hold values from 0 to 1023
- obs_value: float32 [32, 16, 4], P('gy', 'gx'), may hold values from -6 to 6
- obs_var: float32 [32, 16, 4], P('gy', 'gx'), may hold values from 4 to 16
Outputs:
- analysis: float32 [64, 256, 2048], P(None, 'gy', 'gx')
The draws below stay inside these ranges and needn't reach their ends.
All inputs are finite; a program needn't handle non-finite values.
Results may differ from the reference program's by a relative error of at most 0.0001.
Values sent between devices are 32-bit elements; how exact they have to be, the bound alone decides.
A program may use at most 64 MiB of HBM per device.

```python
import math
import jax
import jax.numpy as jnp
from jax import lax

M = 64
CY = 8
CX = 128
OBS_DEV = 4
NY = 256
NX = 2048
N_GY = 32
N_GX = 16


def draw_flow(key, part):
    keys = jax.random.split(key, 3)
    level = jax.random.uniform(keys[0], (NY, NX), jnp.float32, jnp.log(0.02), jnp.log(0.2))
    diffusivity = jnp.exp(level)
    along = jax.random.uniform(keys[1], (NY, NX), jnp.float32, -0.2, 0.2)
    across = jax.random.uniform(keys[2], (NY, NX), jnp.float32, -0.2, 0.2)
    return jnp.stack([diffusivity, along, across]).astype(jnp.float32)


def set_ends(entries, key, least, high):
    index_at = [jax.random.randint(jax.random.fold_in(key, axis), (), 0, length) for axis, length in enumerate(entries.shape)]
    longest = entries.shape.index(max(entries.shape))
    neighbour = index_at[:longest] + [(index_at[longest] + 1) % entries.shape[longest]] + index_at[longest + 1:]
    return entries.at[tuple(index_at)].set(least).at[tuple(neighbour)].set(high)


def steps_of(stream_key, extent, shards, smallest, high):
    level, own = 1.0, jax.random.fold_in(stream_key, 6)
    for dim, shards_of in shards:
        heights = jnp.exp(jax.random.uniform(jax.random.fold_in(own, dim), (shards_of,), jnp.float32, smallest / len(shards), high / len(shards)))
        level = level * jnp.repeat(heights, extent[dim] // shards_of).reshape([-1 if axis == dim else 1 for axis in range(len(extent))])
    return level


def noise(key, shape, scale, limit, cuts=(), held_as=jnp.bfloat16):
    level = steps_of(key, shape, cuts, -0.22, 0.18) if cuts else 1.0
    result = jax.random.normal(key, shape, jnp.float32) * scale * level
    return jnp.minimum(jnp.maximum(result, -limit), limit).astype(held_as)


def setup_inputs(seed: int = 0) -> dict:
    arg_keys = jax.random.split(jax.random.key(seed), 6)
    ensemble = noise(arg_keys[0], (M, NY, NX), 1.0, 6.0, ((1, 32), (2, 16)), jnp.float32)
    flow = draw_flow(jax.random.fold_in(arg_keys[5], 71), 0)
    obs_cell = set_ends(jax.random.randint(arg_keys[2], (N_GY, N_GX, OBS_DEV), 0, CY * CX), jax.random.fold_in(arg_keys[2], 1), 0, (CY * CX) - 1).astype(jnp.int32)
    obs_value = noise(arg_keys[3], (N_GY, N_GX, OBS_DEV), 1.0, 6.0, ((0, 32), (1, 16)), jnp.float32)
    obs_var = jnp.clip(jnp.exp(math.log(16.0) - 1.3862944 * jax.random.uniform(arg_keys[4], (N_GY, N_GX, OBS_DEV), jnp.float32) ** steps_of(arg_keys[4], (N_GY, N_GX, OBS_DEV), ((0, 32), (1, 16)), -0.2, 0.2)), 4.0, 16.0)
    return {"ensemble": ensemble, "flow": flow, "obs_cell": obs_cell, "obs_value": obs_value, "obs_var": obs_var}


def prediction_update(state_grid, flow):
    padded = jnp.pad(state_grid, 1)
    north = padded[:-2, 1:-1]
    south = padded[2:, 1:-1]
    west = padded[1:-1, :-2]
    east = padded[1:-1, 2:]
    spread = flow[0] * (north + south + west + east - 4.0 * state_grid)
    return state_grid + spread - 0.5 * flow[1] * (east - west) - 0.5 * flow[2] * (south - north)

def tri_solve(matrix, rhs, lower, flipped):
    return lax.linalg.triangular_solve(matrix, rhs, left_side=True, lower=lower, transpose_a=flipped)

def reference(ensemble, flow, obs_cell, obs_value, obs_var):

    def ensemble_sample(state_grid):
        return prediction_update(prediction_update(state_grid, flow), flow)
    predicted_state = lax.map(ensemble_sample, ensemble)
    ensemble_average = lax.optimization_barrier(jnp.mean(predicted_state, axis=0))
    member_deviation = predicted_state - ensemble_average
    tile_row = lax.broadcasted_iota(jnp.int32, obs_cell.shape, 0)
    tile_col = lax.broadcasted_iota(jnp.int32, obs_cell.shape, 1)
    rows = (tile_row * CY + obs_cell // CX).reshape(-1).astype(jnp.int32)
    cols = (tile_col * CX + obs_cell % CX).reshape(-1).astype(jnp.int32)
    factor = lax.rsqrt(obs_var.reshape(-1))
    scaled = member_deviation[:, rows, cols] * factor
    innovation = (obs_value.reshape(-1) - ensemble_average[rows, cols]) * factor
    eye = jnp.eye(M, dtype=jnp.float32)
    gram = jnp.dot(scaled, scaled.T, precision=lax.Precision.HIGHEST) + (M - 1.0) * eye
    target = jnp.dot(scaled, innovation, precision=lax.Precision.HIGHEST)
    lower = jnp.linalg.cholesky(gram)
    inverse = tri_solve(lower, eye, True, True)
    weights = jnp.dot(inverse, jnp.dot(inverse.T, target, precision=lax.Precision.HIGHEST), precision=lax.Precision.HIGHEST)
    transform = jnp.sqrt(M - 1.0) * inverse + weights[:, None]
    update = jnp.dot(transform.T, member_deviation.reshape(M, -1), precision=lax.Precision.HIGHEST)
    return ensemble_average + update.reshape(member_deviation.shape)
```

```python
import functools
import math

import jax
import jax.numpy as jnp
from jax import lax
from jax.experimental import pallas as pl
from jax.experimental.pallas import tpu as pltpu
from jax.sharding import PartitionSpec as P

MESH = pl.DeviceIdType.MESH
M = 64
CY = 8
CX = 128
F32 = jnp.float32
BF16 = jnp.bfloat16
NX4 = 4


def iota(shape, dim):
    return lax.broadcasted_iota(jnp.int32, shape, dim)


def step(x, n, s, w, e, k, hu, hv):
    return x + k * (n + s + w + e - 4.0 * x) - hu * (e - w) - hv * (s - n)


def forecast_kernel(
    ngy, ngx,
    x_hbm, flow_hbm, cell_hbm, val_hbm, var_hbm,
    gram_ref, hilo_ref, mean_ref,
    xb, fl, cells, vals, varis, qs, sb, hb, hl, hr, kb, yb, rf, rz, rx,
    load_sem, halo_send, halo_recv, gx_send, gx_recv, z_send, z_recv, x_send, x_recv,
):
    gy = lax.axis_index("gy")
    gx = lax.axis_index("gx")
    nz = ngy // NX4
    up, down = lax.rem(gy + ngy - 1, ngy), lax.rem(gy + 1, ngy)
    left, right = lax.rem(gx + ngx - 1, ngx), lax.rem(gx + 1, ngx)
    zpos = gy // NX4
    xpos = lax.rem(gy, NX4)
    z_partners = [(lax.rem(gy + NX4 * i, ngy), gx) for i in range(1, nz)]
    x_partners = [(zpos * NX4 + lax.rem(xpos + i, NX4), gx) for i in range(1, NX4)]
    gx_partners = [(gy, lax.rem(gx + i, ngx)) for i in range(1, ngx)]
    halo_partners = [
        (up, gx), (down, gx), (gy, left), (gy, right),
        (up, left), (up, right), (down, left), (down, right),
    ]

    loads = [
        pltpu.make_async_copy(x_hbm, xb, load_sem.at[0]),
        pltpu.make_async_copy(flow_hbm, fl, load_sem.at[1]),
        pltpu.make_async_copy(cell_hbm, cells, load_sem.at[2]),
        pltpu.make_async_copy(val_hbm, vals, load_sem.at[3]),
        pltpu.make_async_copy(var_hbm, varis, load_sem.at[4]),
    ]
    for copy in loads:
        copy.start()
    barrier = pltpu.get_barrier_semaphore()
    partners = halo_partners + gx_partners + z_partners + x_partners
    for partner in partners:
        pl.semaphore_signal(barrier, inc=1, device_id=partner, device_id_type=MESH)

    lane = iota((8, CX), 1)
    sub = iota((8, CX), 0)
    edge = (lane <= 1) | (lane >= CX - 2)
    s0, s7 = sub == 0, sub == 7
    l0, l127 = lane == 0, lane == CX - 1

    for copy in loads:
        copy.wait()

    def pack(half):
        def body(i, q):
            for j in range(8):
                m = i * 8 + j
                q = q + pltpu.roll(jnp.where(edge, xb[half * 32 + m], 0.0), 4 * m, 1)
            return q
        return lax.fori_loop(0, 4, body, jnp.zeros((8, CX), F32))

    qa, qb = pack(0), pack(1)
    qs[pl.ds(0, 8), :] = qa
    qs[pl.ds(8, 8), :] = qb
    qc = jnp.where(edge, fl[0], 0.0)
    for i in range(1, 3):
        qc = qc + pltpu.roll(jnp.where(edge, fl[i], 0.0), 4 * i, 1)
    qs[pl.ds(16, 8), :] = qc
    sb[pl.ds(0, M), :] = xb[:, 0, :]
    sb[pl.ds(64, M), :] = xb[:, 1, :]
    sb[pl.ds(136, M), :] = xb[:, 6, :]
    sb[pl.ds(200, M), :] = xb[:, 7, :]
    for i in range(3):
        sb[pl.ds(128 + i, 1), :] = fl[i, 0:1, :]
        sb[pl.ds(131 + i, 1), :] = fl[i, 7:8, :]

    pl.semaphore_wait(barrier, len(partners))

    def remote(src, dst, index, target, send=halo_send, recv=halo_recv):
        return pltpu.make_async_remote_copy(
            src_ref=src, dst_ref=dst, send_sem=send.at[index], recv_sem=recv.at[index],
            device_id=target, device_id_type=MESH,
        )

    halos = [
        remote(sb.at[pl.ds(0, 136), :], hb.at[pl.ds(0, 136), :], 0, (up, gx)),
        remote(sb.at[pl.ds(128, 136), :], hb.at[pl.ds(376, 136), :], 1, (down, gx)),
        remote(qs.at[pl.ds(0, 16), :], kb.at[0], 4, (up, left)),
        remote(qs.at[pl.ds(0, 16), :], kb.at[1], 5, (up, right)),
        remote(qs.at[pl.ds(0, 16), :], kb.at[2], 6, (down, left)),
        remote(qs.at[pl.ds(0, 16), :], kb.at[3], 7, (down, right)),
        remote(qs, hr, 2, (gy, left)),
        remote(qs, hl, 3, (gy, right)),
    ]
    for copy in halos:
        copy.start()
    for copy in halos:
        copy.wait_recv()

    has_up, has_down = gy > 0, gy < ngy - 1
    has_left, has_right = gx > 0, gx < ngx - 1

    def on(flag):
        return jnp.full((8, CX), jnp.where(flag, 1, 0), jnp.int32) > 0

    quad = lane & 3
    west_side = quad >= 2
    hmask = ((sub >= 6) & on(has_up)) | ((sub <= 1) & on(has_down))
    cmask = (west_side & on(has_left)) | ((quad <= 1) & on(has_right))
    kmask = hmask & cmask

    k, hu, hv = fl[0], 0.5 * fl[1], 0.5 * fl[2]

    def flow_rows(i):
        lower = jnp.broadcast_to(hb[pl.ds(128 + i, 1), :], (8, CX))
        upper = jnp.broadcast_to(hb[pl.ds(376 + 3 + i, 1), :], (8, CX))
        return jnp.where(hmask, jnp.where(s7, upper, jnp.where(s0, lower, 0.0)), 0.0)

    def flow_cols(i):
        west = jnp.broadcast_to(hl[pl.ds(16, 8), (4 * i - 1) % CX:(4 * i - 1) % CX + 1], (8, CX))
        east = jnp.broadcast_to(hr[pl.ds(16, 8), 4 * i:4 * i + 1], (8, CX))
        return jnp.where(cmask, jnp.where(west_side, west, east), 0.0)

    kh, uh, vh = flow_rows(0), 0.5 * flow_rows(1), 0.5 * flow_rows(2)
    kc, uc, vc = flow_cols(0), 0.5 * flow_cols(1), 0.5 * flow_cols(2)
    west_cell = quad == 3

    total = jnp.zeros((8, CX), F32)
    for half in range(2):
        q = (qa, qb)[half]
        rows = pl.ds(8 * half, 8)
        ring = jnp.where(cmask, jnp.where(west_side, hl[rows, :], hr[rows, :]), 0.0)
        corner_w = jnp.where(s7, kb[3, rows, :], kb[1, rows, :])
        corner_e = jnp.where(s7, kb[2, rows, :], kb[0, rows, :])
        corner = jnp.where(kmask & (s0 | s7), jnp.where(west_side, corner_w, corner_e), 0.0)
        n = pltpu.roll(jnp.where(s7, corner, ring), 1, 0)
        s = pltpu.roll(jnp.where(s0, corner, ring), 7, 0)
        w = jnp.where(west_cell, pltpu.roll(ring, 1, 1), pltpu.roll(q, 1, 1))
        e = jnp.where(west_cell, pltpu.roll(q, CX - 1, 1), pltpu.roll(ring, CX - 1, 1))
        ring1 = step(ring, n, s, w, e, kc, uc, vc)

        def body(i, acc):
            for j in range(4):
                m = i * 4 + j
                shift = lax.rem(CX - 4 * m, CX)
                member = half * 32 + m
                x = xb[member]
                h = jnp.where(hmask, hb[pl.ds(member, 8, stride=M), :], 0.0)
                ex = pltpu.roll(ring, shift, 1)
                ek = pltpu.roll(corner, shift, 1)
                ey = pltpu.roll(ring1, shift, 1)
                y = step(
                    x,
                    pltpu.roll(jnp.where(s7, h, x), 1, 0), pltpu.roll(jnp.where(s0, h, x), 7, 0),
                    pltpu.roll(jnp.where(l127, ex, x), 1, 1), pltpu.roll(jnp.where(l0, ex, x), CX - 1, 1),
                    k, hu, hv,
                )
                yh = step(
                    h,
                    pltpu.roll(jnp.where(s7, x, h), 1, 0), pltpu.roll(jnp.where(s0, x, h), 7, 0),
                    pltpu.roll(jnp.where(l127, ek, h), 1, 1), pltpu.roll(jnp.where(l0, ek, h), CX - 1, 1),
                    kh, uh, vh,
                )
                z = step(
                    y,
                    pltpu.roll(jnp.where(s7, yh, y), 1, 0), pltpu.roll(jnp.where(s0, yh, y), 7, 0),
                    pltpu.roll(jnp.where(l127, ey, y), 1, 1), pltpu.roll(jnp.where(l0, ey, y), CX - 1, 1),
                    k, hu, hv,
                )
                yb[pl.ds(member * 8, 8), :] = z
                acc = acc + z
            return acc

        total = lax.fori_loop(0, 8, body, total)
    mean = total * (1.0 / M)
    mean_ref[...] = mean

    lane64 = iota((M, CX), 1)
    diag64 = lane64 == iota((M, CX), 0)
    sub4 = iota((4, CX), 0)
    picked, value, variance = [], jnp.zeros((4, CX), F32), jnp.ones((4, CX), F32)
    for j in range(4):
        cell = cells[0, 0, j]
        row, col = lax.shift_right_logical(cell, 7), cell & (CX - 1)
        line = yb[pl.ds(row, M, stride=8), :]
        column = jnp.sum(jnp.where(lane64 == col, line, 0.0), axis=1, keepdims=True)
        picked.append(jnp.sum(jnp.where(diag64, column, 0.0), axis=0, keepdims=True))
        value = jnp.where(sub4 == j, vals[0, 0, j], value)
        variance = jnp.where(sub4 == j, varis[0, 0, j], variance)
    picked = jnp.concatenate(picked, axis=0)
    cell_mean = jnp.sum(picked, axis=1, keepdims=True) * (1.0 / M)
    factor = lax.rsqrt(variance)
    lane4 = iota((4, CX), 1)
    obs = jnp.where(lane4 < M - 1, picked, value)
    obs = jnp.where(lane4 < M, (obs - cell_mean) * factor, 0.0)
    rf[gx] = obs[0:2] + pltpu.roll(obs[2:4], M, 1)

    gx_copies = [
        pltpu.make_async_remote_copy(
            src_ref=rf.at[gx], dst_ref=rf.at[gx], send_sem=gx_send, recv_sem=gx_recv,
            device_id=partner, device_id_type=MESH,
        )
        for partner in gx_partners
    ]
    for copy in gx_copies:
        copy.start()

    for r in range(CY):
        line = yb[pl.ds(r, M, stride=8), :] - mean[r:r + 1, :]
        high = line.astype(BF16)
        hilo_ref[pl.ds(0, M), pl.ds(r * CX, CX)] = high
        hilo_ref[pl.ds(M, M), pl.ds(r * CX, CX)] = (line - high.astype(F32)).astype(BF16)

    def wait_all(buffer, count, sem):
        piece = buffer.at[pl.ds(0, count)]
        pltpu.make_async_copy(piece, piece, sem).wait()

    wait_all(rf, ngx - 1, gx_recv)
    gathered = jnp.concatenate([rf[i] for i in range(ngx)], axis=0)
    lane32 = iota((2 * ngx, CX), 1)
    rows = jnp.concatenate(
        [jnp.where(lane32 < M, gathered, 0.0), jnp.where(lane32 < M, pltpu.roll(gathered, M, 1), 0.0)], axis=0
    )
    gram = jnp.dot(rows.T, rows, precision=lax.Precision.HIGHEST, preferred_element_type=F32)
    rz[zpos] = gram[0:32] + pltpu.roll(gram[32:64], M, 1)

    z_copies = [
        pltpu.make_async_remote_copy(
            src_ref=rz.at[zpos], dst_ref=rz.at[zpos], send_sem=z_send, recv_sem=z_recv,
            device_id=partner, device_id_type=MESH,
        )
        for partner in z_partners
    ]
    for copy in z_copies:
        copy.start()
    wait_all(rz, nz - 1, z_recv)
    part = rz[0]
    for i in range(1, nz):
        part = part + rz[i]
    rx[xpos] = part
    x_copies = [
        pltpu.make_async_remote_copy(
            src_ref=rx.at[xpos], dst_ref=rx.at[xpos], send_sem=x_send, recv_sem=x_recv,
            device_id=partner, device_id_type=MESH,
        )
        for partner in x_partners
    ]
    for copy in x_copies:
        copy.start()
    wait_all(rx, NX4 - 1, x_recv)
    gram_ref[...] = (rx[0] + rx[1]) + (rx[2] + rx[3])

    for copy in halos:
        copy.wait_send()
    wait_all(rf, ngx - 1, gx_send)
    wait_all(rz, nz - 1, z_send)
    wait_all(rx, NX4 - 1, x_send)


def analysis_kernel(gram_ref, hilo_ref, mean_ref, out_ref):
    lane = iota((8, CX), 1)
    sub = iota((8, CX), 0)
    packed = gram_ref[...]
    shifted = pltpu.roll(packed, M, 1)
    blocks = [packed[8 * i:8 * i + 8] for i in range(4)] + [shifted[8 * i:8 * i + 8] for i in range(4)]
    blocks = [jnp.where(lane < M - 1, b, 0.0) for b in blocks]
    row_sums = [jnp.sum(b, axis=1, keepdims=True) for b in blocks]
    last = sub == 7
    target_row = blocks[7][7:8] + jnp.where(lane[0:1] == M - 1, -row_sums[7][7:8], 0.0)
    blocks[7] = jnp.where(last, 0.0, blocks[7])
    row_sums[7] = jnp.where(last[:, 0:1], 0.0, row_sums[7])
    col_sum = functools.reduce(jnp.add, blocks)
    col_sum = jnp.sum(col_sum, axis=0, keepdims=True)
    all_sum = jnp.sum(functools.reduce(jnp.add, row_sums), axis=0, keepdims=True)
    blocks = [jnp.where(lane == M - 1, -r, b) for b, r in zip(blocks, row_sums)]
    blocks[7] = jnp.where(last, jnp.where(lane == M - 1, all_sum, -col_sum), blocks[7])
    eyes = [lane == sub + 8 * i for i in range(8)]
    blocks = [jnp.where(e, b + (M - 1.0), b) for e, b in zip(eyes, blocks)]
    diagonals = [jnp.where(e, b, 0.0) for e, b in zip(eyes, blocks)]
    scale_row = lax.rsqrt(jnp.sum(functools.reduce(jnp.add, diagonals), axis=0, keepdims=True) + jnp.where(lane[0:1] < M, 0.0, 1.0))
    scale_col = [lax.rsqrt(jnp.sum(d, axis=1, keepdims=True)) for d in diagonals]
    a = [
        jnp.where(lane == sub + (M + 8 * i), scale_col[i], jnp.where(lane < M, blocks[i] * scale_col[i] * scale_row, 0.0))
        for i in range(8)
    ]

    lower = [None] * 8
    for p in range(16):
        b, o = p // 2, 4 * (p % 2)
        cols = {
            (t, i): jnp.broadcast_to(a[i][:, 4 * p + t:4 * p + t + 1], (8, CX)) for t in range(4) for i in range(b, 8)
        }
        d = {
            (s, t): jnp.broadcast_to(cols[t, b][o + s:o + s + 1, :], (8, CX)) for s in range(4) for t in range(s + 1)
        }
        r = [jnp.broadcast_to(a[b][o + s:o + s + 1, :], (8, CX)) for s in range(4)]

        det = d[0, 0] * d[1, 1] - d[1, 0] * d[1, 0]
        inv = 1.0 / det
        i00, i10, i11 = d[1, 1] * inv, -d[1, 0] * inv, d[0, 0] * inv
        e00 = i00 * d[2, 0] + i10 * d[2, 1]
        e10 = i10 * d[2, 0] + i11 * d[2, 1]
        e01 = i00 * d[3, 0] + i10 * d[3, 1]
        e11 = i10 * d[3, 0] + i11 * d[3, 1]
        c00 = d[2, 2] - (d[2, 0] * e00 + d[2, 1] * e10)
        c10 = d[3, 2] - (d[3, 0] * e00 + d[3, 1] * e10)
        c11 = d[3, 3] - (d[3, 0] * e01 + d[3, 1] * e11)
        r2 = r[2] - (e00 * r[0] + e10 * r[1])
        r3 = r[3] - (e01 * r[0] + e11 * r[1])
        det2 = c00 * c11 - c10 * c10
        if p < 15:
            u0 = i00 * r[0] + i10 * r[1]
            u1 = i10 * r[0] + i11 * r[1]
            inv2 = 1.0 / det2
            z2 = (c11 * r2 - c10 * r3) * inv2
            z3 = (c00 * r3 - c10 * r2) * inv2
            z0 = u0 - (e00 * z2 + e01 * z3)
            z1 = u1 - (e10 * z2 + e11 * z3)
            z = (z0, z1, z2, z3)
            for i in range(b if o == 0 else b + 1, 8):
                update = (cols[0, i] * z[0] + cols[1, i] * z[1]) + (cols[2, i] * z[2] + cols[3, i] * z[3])
                new = a[i] - update
                a[i] = jnp.where(sub >= 4, new, a[i]) if i == b else new
        n0 = r[0] * lax.rsqrt(d[0, 0])
        n1 = (d[0, 0] * r[1] - d[1, 0] * r[0]) * lax.rsqrt(d[0, 0] * det)
        n2 = r2 * lax.rsqrt(c00)
        n3 = (c00 * r3 - c10 * r2) * lax.rsqrt(c00 * det2)
        rows = jnp.where(sub == o, n0, jnp.where(sub == o + 1, n1, jnp.where(sub == o + 2, n2, n3)))
        lower[b] = rows if o == 0 else jnp.where(sub >= 4, rows, lower[b])
    lower = [pltpu.roll(jnp.where(lane >= M, v, 0.0), M, 1) for v in lower]
    heads = [jnp.sum(v * target_row, axis=1, keepdims=True) for v in lower]
    weight = jnp.sum(functools.reduce(jnp.add, [v * h for v, h in zip(lower, heads)]), axis=0, keepdims=True)
    root = math.sqrt(M - 1.0)
    mix = jnp.concatenate([root * v + weight for v in lower], axis=0)
    high = mix.astype(BF16).astype(F32)
    low = mix - high
    pair = jnp.where(iota((M, CX), 1) < M, high, pltpu.roll(high, M, 1)).astype(BF16)
    low_pair = jnp.where(iota((M, CX), 1) < M, low, pltpu.roll(low, M, 1)).astype(BF16)
    left = jnp.concatenate([pair, low_pair], axis=1)
    for r in range(0, CY, 2):
        cols = pl.ds(r * CX, 2 * CX)
        block = hilo_ref[:, cols]
        right = jnp.concatenate([block, block], axis=0)
        res = jnp.dot(left, right, preferred_element_type=F32)
        out_ref[:, r, :] = res[:, :CX] + mean_ref[r:r + 1, :]
        out_ref[:, r + 1, :] = res[:, CX:] + mean_ref[r + 1:r + 2, :]


def body(ngy, ngx, ensemble, flow, obs_cell, obs_value, obs_var):
    vmem = pl.BlockSpec(memory_space=pltpu.VMEM)
    hbm = pl.BlockSpec(memory_space=pl.ANY)
    dma = pltpu.SemaphoreType.DMA
    gram, hilo, mean = pl.pallas_call(
        functools.partial(forecast_kernel, ngy, ngx),
        out_shape=(
            jax.ShapeDtypeStruct((32, CX), F32),
            jax.ShapeDtypeStruct((2 * M, CY * CX), BF16),
            jax.ShapeDtypeStruct((CY, CX), F32),
        ),
        in_specs=[hbm] * 5,
        out_specs=(vmem,) * 3,
        scratch_shapes=[
            pltpu.VMEM((M, CY, CX), F32),
            pltpu.VMEM((3, CY, CX), F32),
            pltpu.SMEM((1, 1, 4), jnp.int32),
            pltpu.SMEM((1, 1, 4), F32),
            pltpu.SMEM((1, 1, 4), F32),
            pltpu.VMEM((24, CX), F32),
            pltpu.VMEM((264, CX), F32),
            pltpu.VMEM((512, CX), F32),
            pltpu.VMEM((24, CX), F32),
            pltpu.VMEM((24, CX), F32),
            pltpu.VMEM((4, 16, CX), F32),
            pltpu.VMEM((512, CX), F32),
            pltpu.VMEM((ngx, 2, CX), F32),
            pltpu.VMEM((ngy // NX4, 32, CX), F32),
            pltpu.VMEM((NX4, 32, CX), F32),
            dma((5,)), dma((8,)), dma((8,)),
            dma, dma, dma, dma, dma, dma,
        ],
        compiler_params=pltpu.CompilerParams(collective_id=0, has_side_effects=True),
        name="forecast",
    )(ensemble, flow, obs_cell, obs_value, obs_var)
    return pl.pallas_call(
        analysis_kernel,
        out_shape=jax.ShapeDtypeStruct((M, CY, CX), F32),
        in_specs=[vmem] * 3,
        out_specs=vmem,
        name="analysis",
    )(gram, hilo, mean)


def solution(mesh):
    tile = P("gy", "gx", None)
    return jax.shard_map(
        functools.partial(body, mesh.shape["gy"], mesh.shape["gx"]),
        mesh=mesh,
        in_specs=(P(None, "gy", "gx"), P(None, "gy", "gx"), tile, tile, tile),
        out_specs=P(None, "gy", "gx"),
        check_vma=False,
    )
```

```python
import functools
import math

import jax
import jax.numpy as jnp
from jax import lax
from jax.experimental import pallas as pl
from jax.experimental.pallas import tpu as pltpu
from jax.sharding import PartitionSpec as P

MESH = pl.DeviceIdType.MESH
M = 64
CY = 8
CX = 128
F32 = jnp.float32
BF16 = jnp.bfloat16
NX4 = 4


def iota(shape, dim):
    return lax.broadcasted_iota(jnp.int32, shape, dim)


def step(x, n, s, w, e, k, hu, hv):
    return x + k * (n + s + w + e - 4.0 * x) - hu * (e - w) - hv * (s - n)


def forecast_kernel(
    ngy, ngx,
    x_hbm, flow_hbm, cell_hbm, val_hbm, var_hbm,
    gram_ref, hilo_ref, mean_ref,
    xb, fl, cells, vals, varis, qs, sb, hb, hl, hr, kb, yb, rf,
    load_sem, halo_send, halo_recv, gx_send, gx_recv,
):
    gy = lax.axis_index("gy")
    gx = lax.axis_index("gx")
    up, down = gy - 1, gy + 1
    has_up, has_down = gy > 0, gy < ngy - 1
    left, right = lax.rem(gx + ngx - 1, ngx), lax.rem(gx + 1, ngx)
    gx_partners = [(gy, lax.rem(gx + i, ngx)) for i in range(1, ngx)]

    loads = [
        pltpu.make_async_copy(x_hbm, xb, load_sem.at[0]),
        pltpu.make_async_copy(flow_hbm, fl, load_sem.at[1]),
        pltpu.make_async_copy(cell_hbm, cells, load_sem.at[2]),
        pltpu.make_async_copy(val_hbm, vals, load_sem.at[3]),
        pltpu.make_async_copy(var_hbm, varis, load_sem.at[4]),
    ]
    for copy in loads:
        copy.start()
    barrier = pltpu.get_barrier_semaphore()

    def greet(partners):
        for partner in partners:
            pl.semaphore_signal(barrier, inc=1, device_id=partner, device_id_type=MESH)

    @pl.when(has_up)
    def _():
        greet([(up, gx), (up, left), (up, right)])

    @pl.when(has_down)
    def _():
        greet([(down, gx), (down, left), (down, right)])

    greet(gx_partners)

    lane = iota((8, CX), 1)
    sub = iota((8, CX), 0)
    edge = (lane <= 1) | (lane >= CX - 2)
    s0, s7 = sub == 0, sub == 7
    l0, l127 = lane == 0, lane == CX - 1

    for copy in loads:
        copy.wait()

    def pack(half):
        def body(i, q):
            for j in range(8):
                m = i * 8 + j
                q = q + pltpu.roll(jnp.where(edge, xb[half * 32 + m], 0.0), 4 * m, 1)
            return q
        return lax.fori_loop(0, 4, body, jnp.zeros((8, CX), F32))

    qa, qb = pack(0), pack(1)
    qs[pl.ds(0, 8), :] = qa
    qs[pl.ds(8, 8), :] = qb
    qc = jnp.where(edge, fl[0], 0.0)
    for i in range(1, 3):
        qc = qc + pltpu.roll(jnp.where(edge, fl[i], 0.0), 4 * i, 1)
    qs[pl.ds(16, 8), :] = qc
    sb[pl.ds(0, M), :] = xb[:, 0, :]
    sb[pl.ds(64, M), :] = xb[:, 1, :]
    sb[pl.ds(136, M), :] = xb[:, 6, :]
    sb[pl.ds(200, M), :] = xb[:, 7, :]
    for i in range(3):
        sb[pl.ds(128 + i, 1), :] = fl[i, 0:1, :]
        sb[pl.ds(131 + i, 1), :] = fl[i, 7:8, :]

    @pl.when(has_up & has_down)
    def _():
        pl.semaphore_wait(barrier, ngx + 5)

    @pl.when(jnp.logical_not(has_up & has_down))
    def _():
        pl.semaphore_wait(barrier, ngx + 2)


    def remote(src, dst, index, target, send=halo_send, recv=halo_recv):
        return pltpu.make_async_remote_copy(
            src_ref=src, dst_ref=dst, send_sem=send.at[index], recv_sem=recv.at[index],
            device_id=target, device_id_type=MESH,
        )

    up_halos = [
        remote(sb.at[pl.ds(0, 136), :], hb.at[pl.ds(0, 136), :], 0, (up, gx)),
        remote(qs.at[pl.ds(0, 16), :], kb.at[0], 4, (up, left)),
        remote(qs.at[pl.ds(0, 16), :], kb.at[1], 5, (up, right)),
    ]
    down_halos = [
        remote(sb.at[pl.ds(128, 136), :], hb.at[pl.ds(376, 136), :], 1, (down, gx)),
        remote(qs.at[pl.ds(0, 16), :], kb.at[2], 6, (down, left)),
        remote(qs.at[pl.ds(0, 16), :], kb.at[3], 7, (down, right)),
    ]
    side_halos = [remote(qs, hr, 2, (gy, left)), remote(qs, hl, 3, (gy, right))]

    @pl.when(has_up)
    def _():
        for copy in up_halos:
            copy.start()

    @pl.when(has_down)
    def _():
        for copy in down_halos:
            copy.start()

    for copy in side_halos:
        copy.start()
    for copy in side_halos:
        copy.wait_recv()

    @pl.when(has_up)
    def _():
        for copy in down_halos:
            copy.wait_recv()

    @pl.when(has_down)
    def _():
        for copy in up_halos:
            copy.wait_recv()

    has_left, has_right = gx > 0, gx < ngx - 1

    def on(flag):
        return jnp.full((8, CX), jnp.where(flag, 1, 0), jnp.int32) > 0

    quad = lane & 3
    west_side = quad >= 2
    hmask = ((sub >= 6) & on(has_up)) | ((sub <= 1) & on(has_down))
    cmask = (west_side & on(has_left)) | ((quad <= 1) & on(has_right))
    kmask = hmask & cmask

    k, hu, hv = fl[0], 0.5 * fl[1], 0.5 * fl[2]

    def flow_rows(i):
        lower = jnp.broadcast_to(hb[pl.ds(128 + i, 1), :], (8, CX))
        upper = jnp.broadcast_to(hb[pl.ds(376 + 3 + i, 1), :], (8, CX))
        return jnp.where(hmask, jnp.where(s7, upper, jnp.where(s0, lower, 0.0)), 0.0)

    def flow_cols(i):
        west = jnp.broadcast_to(hl[pl.ds(16, 8), (4 * i - 1) % CX:(4 * i - 1) % CX + 1], (8, CX))
        east = jnp.broadcast_to(hr[pl.ds(16, 8), 4 * i:4 * i + 1], (8, CX))
        return jnp.where(cmask, jnp.where(west_side, west, east), 0.0)

    kh, uh, vh = flow_rows(0), 0.5 * flow_rows(1), 0.5 * flow_rows(2)
    kc, uc, vc = flow_cols(0), 0.5 * flow_cols(1), 0.5 * flow_cols(2)
    west_cell = quad == 3

    total = jnp.zeros((8, CX), F32)
    for half in range(2):
        q = (qa, qb)[half]
        rows = pl.ds(8 * half, 8)
        ring = jnp.where(cmask, jnp.where(west_side, hl[rows, :], hr[rows, :]), 0.0)
        corner_w = jnp.where(s7, kb[3, rows, :], kb[1, rows, :])
        corner_e = jnp.where(s7, kb[2, rows, :], kb[0, rows, :])
        corner = jnp.where(kmask & (s0 | s7), jnp.where(west_side, corner_w, corner_e), 0.0)
        n = pltpu.roll(jnp.where(s7, corner, ring), 1, 0)
        s = pltpu.roll(jnp.where(s0, corner, ring), 7, 0)
        w = jnp.where(west_cell, pltpu.roll(ring, 1, 1), pltpu.roll(q, 1, 1))
        e = jnp.where(west_cell, pltpu.roll(q, CX - 1, 1), pltpu.roll(ring, CX - 1, 1))
        ring1 = step(ring, n, s, w, e, kc, uc, vc)

        def body(i, acc):
            for j in range(4):
                m = i * 4 + j
                shift = lax.rem(CX - 4 * m, CX)
                member = half * 32 + m
                x = xb[member]
                h = jnp.where(hmask, hb[pl.ds(member, 8, stride=M), :], 0.0)
                ex = pltpu.roll(ring, shift, 1)
                ek = pltpu.roll(corner, shift, 1)
                ey = pltpu.roll(ring1, shift, 1)
                y = step(
                    x,
                    pltpu.roll(jnp.where(s7, h, x), 1, 0), pltpu.roll(jnp.where(s0, h, x), 7, 0),
                    pltpu.roll(jnp.where(l127, ex, x), 1, 1), pltpu.roll(jnp.where(l0, ex, x), CX - 1, 1),
                    k, hu, hv,
                )
                yh = step(
                    h,
                    pltpu.roll(jnp.where(s7, x, h), 1, 0), pltpu.roll(jnp.where(s0, x, h), 7, 0),
                    pltpu.roll(jnp.where(l127, ek, h), 1, 1), pltpu.roll(jnp.where(l0, ek, h), CX - 1, 1),
                    kh, uh, vh,
                )
                z = step(
                    y,
                    pltpu.roll(jnp.where(s7, yh, y), 1, 0), pltpu.roll(jnp.where(s0, yh, y), 7, 0),
                    pltpu.roll(jnp.where(l127, ey, y), 1, 1), pltpu.roll(jnp.where(l0, ey, y), CX - 1, 1),
                    k, hu, hv,
                )
                yb[pl.ds(member * 8, 8), :] = z
                acc = acc + z
            return acc

        total = lax.fori_loop(0, 8, body, total)
    mean = total * (1.0 / M)
    mean_ref[...] = mean

    lane64 = iota((M, CX), 1)
    diag64 = lane64 == iota((M, CX), 0)
    sub4 = iota((4, CX), 0)
    picked, value, variance = [], jnp.zeros((4, CX), F32), jnp.ones((4, CX), F32)
    for j in range(4):
        cell = cells[0, 0, j]
        row, col = lax.shift_right_logical(cell, 7), cell & (CX - 1)
        line = yb[pl.ds(row, M, stride=8), :]
        column = jnp.sum(jnp.where(lane64 == col, line, 0.0), axis=1, keepdims=True)
        picked.append(jnp.sum(jnp.where(diag64, column, 0.0), axis=0, keepdims=True))
        value = jnp.where(sub4 == j, vals[0, 0, j], value)
        variance = jnp.where(sub4 == j, varis[0, 0, j], variance)
    picked = jnp.concatenate(picked, axis=0)
    cell_mean = jnp.sum(picked, axis=1, keepdims=True) * (1.0 / M)
    factor = lax.rsqrt(variance)
    lane4 = iota((4, CX), 1)
    obs = jnp.where(lane4 < M - 1, picked, value)
    obs = jnp.where(lane4 < M, (obs - cell_mean) * factor, 0.0)
    rf[gx] = obs[0:2] + pltpu.roll(obs[2:4], M, 1)

    gx_copies = [
        pltpu.make_async_remote_copy(
            src_ref=rf.at[gx], dst_ref=rf.at[gx], send_sem=gx_send, recv_sem=gx_recv,
            device_id=partner, device_id_type=MESH,
        )
        for partner in gx_partners
    ]
    for copy in gx_copies:
        copy.start()

    for r in range(CY):
        line = yb[pl.ds(r, M, stride=8), :] - mean[r:r + 1, :]
        high = line.astype(BF16)
        hilo_ref[pl.ds(0, M), pl.ds(r * CX, CX)] = high
        hilo_ref[pl.ds(M, M), pl.ds(r * CX, CX)] = (line - high.astype(F32)).astype(BF16)

    wait_all(rf, ngx - 1, gx_recv)
    gathered = jnp.concatenate([rf[i] for i in range(ngx)], axis=0)
    lane32 = iota((2 * ngx, CX), 1)
    rows = jnp.concatenate(
        [jnp.where(lane32 < M, gathered, 0.0), jnp.where(lane32 < M, pltpu.roll(gathered, M, 1), 0.0)], axis=0
    )
    gram = jnp.dot(rows.T, rows, precision=lax.Precision.HIGHEST, preferred_element_type=F32)
    gram_ref[...] = gram[0:32] + pltpu.roll(gram[32:64], M, 1)

    for copy in side_halos:
        copy.wait_send()

    @pl.when(has_up)
    def _():
        for copy in up_halos:
            copy.wait_send()

    @pl.when(has_down)
    def _():
        for copy in down_halos:
            copy.wait_send()

    wait_all(rf, ngx - 1, gx_send)


def wait_all(buffer, count, sem):
    piece = buffer.at[pl.ds(0, count)]
    pltpu.make_async_copy(piece, piece, sem).wait()


def sum_kernel(ngy, part_ref, gram_ref, rz, rx, z_send, z_recv, x_send, x_recv):
    gy = lax.axis_index("gy")
    gx = lax.axis_index("gx")
    nz = ngy // NX4
    zpos = gy // NX4
    xpos = lax.rem(gy, NX4)
    z_partners = [(lax.rem(gy + NX4 * i, ngy), gx) for i in range(1, nz)]
    x_partners = [(zpos * NX4 + lax.rem(xpos + i, NX4), gx) for i in range(1, NX4)]
    barrier = pltpu.get_barrier_semaphore()
    for partner in z_partners + x_partners:
        pl.semaphore_signal(barrier, inc=1, device_id=partner, device_id_type=MESH)
    rz[zpos] = part_ref[...]
    pl.semaphore_wait(barrier, nz + NX4 - 2)

    def spread(buffer, slot, partners, send, recv):
        for partner in partners:
            pltpu.make_async_remote_copy(
                src_ref=buffer.at[slot], dst_ref=buffer.at[slot], send_sem=send, recv_sem=recv,
                device_id=partner, device_id_type=MESH,
            ).start()

    spread(rz, zpos, z_partners, z_send, z_recv)
    wait_all(rz, nz - 1, z_recv)
    part = rz[0]
    for i in range(1, nz):
        part = part + rz[i]
    rx[xpos] = part
    spread(rx, xpos, x_partners, x_send, x_recv)
    wait_all(rx, NX4 - 1, x_recv)
    gram_ref[...] = (rx[0] + rx[1]) + (rx[2] + rx[3])
    wait_all(rz, nz - 1, z_send)
    wait_all(rx, NX4 - 1, x_send)


def analysis_kernel(gram_ref, hilo_ref, mean_ref, out_ref):
    lane = iota((8, CX), 1)
    sub = iota((8, CX), 0)
    packed = gram_ref[...]
    shifted = pltpu.roll(packed, M, 1)
    blocks = [packed[8 * i:8 * i + 8] for i in range(4)] + [shifted[8 * i:8 * i + 8] for i in range(4)]
    blocks = [jnp.where(lane < M - 1, b, 0.0) for b in blocks]
    row_sums = [jnp.sum(b, axis=1, keepdims=True) for b in blocks]
    last = sub == 7
    target_row = blocks[7][7:8] + jnp.where(lane[0:1] == M - 1, -row_sums[7][7:8], 0.0)
    blocks[7] = jnp.where(last, 0.0, blocks[7])
    row_sums[7] = jnp.where(last[:, 0:1], 0.0, row_sums[7])
    col_sum = functools.reduce(jnp.add, blocks)
    col_sum = jnp.sum(col_sum, axis=0, keepdims=True)
    all_sum = jnp.sum(functools.reduce(jnp.add, row_sums), axis=0, keepdims=True)
    blocks = [jnp.where(lane == M - 1, -r, b) for b, r in zip(blocks, row_sums)]
    blocks[7] = jnp.where(last, jnp.where(lane == M - 1, all_sum, -col_sum), blocks[7])
    eyes = [lane == sub + 8 * i for i in range(8)]
    blocks = [jnp.where(e, b + (M - 1.0), b) for e, b in zip(eyes, blocks)]
    diagonals = [jnp.where(e, b, 0.0) for e, b in zip(eyes, blocks)]
    scale_row = lax.rsqrt(jnp.sum(functools.reduce(jnp.add, diagonals), axis=0, keepdims=True) + jnp.where(lane[0:1] < M, 0.0, 1.0))
    scale_col = [lax.rsqrt(jnp.sum(d, axis=1, keepdims=True)) for d in diagonals]
    a = [
        jnp.where(lane == sub + (M + 8 * i), scale_col[i], jnp.where(lane < M, blocks[i] * scale_col[i] * scale_row, 0.0))
        for i in range(8)
    ]

    lower = [None] * 8
    for p in range(16):
        b, o = p // 2, 4 * (p % 2)
        cols = {
            (t, i): jnp.broadcast_to(a[i][:, 4 * p + t:4 * p + t + 1], (8, CX)) for t in range(4) for i in range(b, 8)
        }
        d = {
            (s, t): jnp.broadcast_to(cols[t, b][o + s:o + s + 1, :], (8, CX)) for s in range(4) for t in range(s + 1)
        }
        r = [jnp.broadcast_to(a[b][o + s:o + s + 1, :], (8, CX)) for s in range(4)]

        det = d[0, 0] * d[1, 1] - d[1, 0] * d[1, 0]
        inv = 1.0 / det
        i00, i10, i11 = d[1, 1] * inv, -d[1, 0] * inv, d[0, 0] * inv
        e00 = i00 * d[2, 0] + i10 * d[2, 1]
        e10 = i10 * d[2, 0] + i11 * d[2, 1]
        e01 = i00 * d[3, 0] + i10 * d[3, 1]
        e11 = i10 * d[3, 0] + i11 * d[3, 1]
        c00 = d[2, 2] - (d[2, 0] * e00 + d[2, 1] * e10)
        c10 = d[3, 2] - (d[3, 0] * e00 + d[3, 1] * e10)
        c11 = d[3, 3] - (d[3, 0] * e01 + d[3, 1] * e11)
        r2 = r[2] - (e00 * r[0] + e10 * r[1])
        r3 = r[3] - (e01 * r[0] + e11 * r[1])
        det2 = c00 * c11 - c10 * c10
        if p < 15:
            u0 = i00 * r[0] + i10 * r[1]
            u1 = i10 * r[0] + i11 * r[1]
            inv2 = 1.0 / det2
            z2 = (c11 * r2 - c10 * r3) * inv2
            z3 = (c00 * r3 - c10 * r2) * inv2
            z0 = u0 - (e00 * z2 + e01 * z3)
            z1 = u1 - (e10 * z2 + e11 * z3)
            z = (z0, z1, z2, z3)
            for i in range(b if o == 0 else b + 1, 8):
                update = (cols[0, i] * z[0] + cols[1, i] * z[1]) + (cols[2, i] * z[2] + cols[3, i] * z[3])
                new = a[i] - update
                a[i] = jnp.where(sub >= 4, new, a[i]) if i == b else new
        n0 = r[0] * lax.rsqrt(d[0, 0])
        n1 = (d[0, 0] * r[1] - d[1, 0] * r[0]) * lax.rsqrt(d[0, 0] * det)
        n2 = r2 * lax.rsqrt(c00)
        n3 = (c00 * r3 - c10 * r2) * lax.rsqrt(c00 * det2)
        rows = jnp.where(sub == o, n0, jnp.where(sub == o + 1, n1, jnp.where(sub == o + 2, n2, n3)))
        lower[b] = rows if o == 0 else jnp.where(sub >= 4, rows, lower[b])
    lower = [pltpu.roll(jnp.where(lane >= M, v, 0.0), M, 1) for v in lower]
    heads = [jnp.sum(v * target_row, axis=1, keepdims=True) for v in lower]
    weight = jnp.sum(functools.reduce(jnp.add, [v * h for v, h in zip(lower, heads)]), axis=0, keepdims=True)
    root = math.sqrt(M - 1.0)
    mix = jnp.concatenate([root * v + weight for v in lower], axis=0)
    high = mix.astype(BF16).astype(F32)
    low = mix - high
    pair = jnp.where(iota((M, CX), 1) < M, high, pltpu.roll(high, M, 1)).astype(BF16)
    low_pair = jnp.where(iota((M, CX), 1) < M, low, pltpu.roll(low, M, 1)).astype(BF16)
    left = jnp.concatenate([pair, low_pair], axis=1)
    for r in range(0, CY, 2):
        cols = pl.ds(r * CX, 2 * CX)
        block = hilo_ref[:, cols]
        right = jnp.concatenate([block, block], axis=0)
        res = jnp.dot(left, right, preferred_element_type=F32)
        out_ref[:, r, :] = res[:, :CX] + mean_ref[r:r + 1, :]
        out_ref[:, r + 1, :] = res[:, CX:] + mean_ref[r + 1:r + 2, :]


def near(array):
    return pltpu.with_memory_space_constraint(array, pltpu.VMEM)


def body(ngy, ngx, ensemble, flow, obs_cell, obs_value, obs_var):
    vmem = pl.BlockSpec(memory_space=pltpu.VMEM)
    hbm = pl.BlockSpec(memory_space=pl.ANY)
    dma = pltpu.SemaphoreType.DMA
    part, hilo, mean = pl.pallas_call(
        functools.partial(forecast_kernel, ngy, ngx),
        out_shape=(
            pltpu.VMEM((32, CX), F32),
            pltpu.VMEM((2 * M, CY * CX), BF16),
            pltpu.VMEM((CY, CX), F32),
        ),
        in_specs=[hbm] * 5,
        out_specs=(vmem,) * 3,
        scratch_shapes=[
            pltpu.VMEM((M, CY, CX), F32),
            pltpu.VMEM((3, CY, CX), F32),
            pltpu.SMEM((1, 1, 4), jnp.int32),
            pltpu.SMEM((1, 1, 4), F32),
            pltpu.SMEM((1, 1, 4), F32),
            pltpu.VMEM((24, CX), F32),
            pltpu.VMEM((264, CX), F32),
            pltpu.VMEM((512, CX), F32),
            pltpu.VMEM((24, CX), F32),
            pltpu.VMEM((24, CX), F32),
            pltpu.VMEM((4, 16, CX), F32),
            pltpu.VMEM((512, CX), F32),
            pltpu.VMEM((ngx, 2, CX), F32),
            dma((5,)), dma((8,)), dma((8,)), dma, dma,
        ],
        compiler_params=pltpu.CompilerParams(collective_id=0, has_side_effects=True),
        name="forecast",
    )(ensemble, flow, obs_cell, obs_value, obs_var)
    gram = pl.pallas_call(
        functools.partial(sum_kernel, ngy),
        out_shape=pltpu.VMEM((32, CX), F32),
        in_specs=[vmem],
        out_specs=vmem,
        scratch_shapes=[
            pltpu.VMEM((ngy // NX4, 32, CX), F32),
            pltpu.VMEM((NX4, 32, CX), F32),
            dma, dma, dma, dma,
        ],
        compiler_params=pltpu.CompilerParams(collective_id=1, has_side_effects=True),
        name="sums",
    )(near(part))
    return pl.pallas_call(
        analysis_kernel,
        out_shape=jax.ShapeDtypeStruct((M, CY, CX), F32),
        in_specs=[vmem] * 3,
        out_specs=vmem,
        name="analysis",
    )(near(gram), near(hilo), near(mean))


def solution(mesh):
    tile = P("gy", "gx", None)
    return jax.shard_map(
        functools.partial(body, mesh.shape["gy"], mesh.shape["gx"]),
        mesh=mesh,
        in_specs=(P(None, "gy", "gx"), P(None, "gy", "gx"), tile, tile, tile),
        out_specs=P(None, "gy", "gx"),
        check_vma=False,
    )
```

```python
import functools
import math

import jax
import jax.numpy as jnp
from jax import lax
from jax.experimental import pallas as pl
from jax.experimental.pallas import tpu as pltpu
from jax.sharding import PartitionSpec as P

MESH = pl.DeviceIdType.MESH
M = 64
CY = 8
CX = 128
F32 = jnp.float32
BF16 = jnp.bfloat16
NX4 = 4


def iota(shape, dim):
    return lax.broadcasted_iota(jnp.int32, shape, dim)


def step(x, n, s, w, e, k, hu, hv):
    return x + k * (n + s + w + e - 4.0 * x) - hu * (e - w) - hv * (s - n)


def forecast_kernel(
    ngy, ngx,
    x_hbm, flow_hbm, cell_hbm, val_hbm, var_hbm,
    gram_ref, hilo_ref, mean_ref,
    xb, xr, yr, zr, fl, cf, cells, vals, varis, qs, fs, hu_rows, hd_rows, hl, hr, kb, fh, zc, rf,
    load_sem, halo_send, halo_recv, flow_send, flow_recv, gx_send, gx_recv,
):
    gy = lax.axis_index("gy")
    gx = lax.axis_index("gx")
    up, down = gy - 1, gy + 1
    has_up, has_down = gy > 0, gy < ngy - 1
    left, right = lax.rem(gx + ngx - 1, ngx), lax.rem(gx + 1, ngx)
    gx_partners = [(gy, lax.rem(gx + i, ngx)) for i in range(1, ngx)]

    row_loads = [pltpu.make_async_copy(x_hbm.at[:, r, :], xr.at[r + 1], load_sem.at[5 + r]) for r in (0, 1, 6, 7, 2, 3, 4, 5)]
    flow_load = pltpu.make_async_copy(flow_hbm, fl, load_sem.at[1])
    loads = [
        pltpu.make_async_copy(x_hbm, xb, load_sem.at[0]),
        pltpu.make_async_copy(cell_hbm, cells, load_sem.at[2]),
        pltpu.make_async_copy(val_hbm, vals, load_sem.at[3]),
        pltpu.make_async_copy(var_hbm, varis, load_sem.at[4]),
    ]
    flow_load.start()
    for copy in row_loads + loads:
        copy.start()
    barrier = pltpu.get_barrier_semaphore()

    def greet(partners):
        for partner in partners:
            pl.semaphore_signal(barrier, inc=1, device_id=partner, device_id_type=MESH)

    @pl.when(has_up)
    def _():
        greet([(up, gx), (up, left), (up, right)])

    @pl.when(has_down)
    def _():
        greet([(down, gx), (down, left), (down, right)])

    greet(gx_partners)

    lane = iota((8, CX), 1)
    sub = iota((8, CX), 0)
    edge = (lane <= 1) | (lane >= CX - 2)
    s0, s7 = sub == 0, sub == 7
    l0, l127 = lane == 0, lane == CX - 1
    quad = lane & 3
    q0, q1, q3 = quad == 0, quad == 1, quad == 3
    west_side = quad >= 2

    def remote(src, dst, index, target, send=halo_send, recv=halo_recv):
        return pltpu.make_async_remote_copy(
            src_ref=src, dst_ref=dst, send_sem=send.at[index], recv_sem=recv.at[index],
            device_id=target, device_id_type=MESH,
        )

    up_flow = [remote(fs.at[0], fh.at[0], 0, (up, gx), flow_send, flow_recv)]
    down_flow = [remote(fs.at[0], fh.at[1], 1, (down, gx), flow_send, flow_recv)]
    side_flow = [
        remote(fs.at[1], fh.at[2], 2, (gy, left), flow_send, flow_recv),
        remote(fs.at[1], fh.at[3], 3, (gy, right), flow_send, flow_recv),
    ]
    up_rows = [remote(xr.at[pl.ds(1, 2)], hd_rows, 0, (up, gx))]
    down_rows = [remote(xr.at[pl.ds(7, 2)], hu_rows, 1, (down, gx))]
    up_corners = [remote(qs, kb.at[0], 4, (up, left)), remote(qs, kb.at[1], 5, (up, right))]
    down_corners = [remote(qs, kb.at[2], 6, (down, left)), remote(qs, kb.at[3], 7, (down, right))]
    side_halos = [remote(qs, hr, 2, (gy, left)), remote(qs, hl, 3, (gy, right))]

    def start(up_copies, down_copies, side_copies=()):
        @pl.when(has_up)
        def _():
            for copy in up_copies:
                copy.start()

        @pl.when(has_down)
        def _():
            for copy in down_copies:
                copy.start()

        for copy in side_copies:
            copy.start()

    def received(up_copies, down_copies, side_copies=()):
        for copy in side_copies:
            copy.wait_recv()

        @pl.when(has_up)
        def _():
            for copy in down_copies:
                copy.wait_recv()

        @pl.when(has_down)
        def _():
            for copy in up_copies:
                copy.wait_recv()

    def sent(up_copies, down_copies, side_copies=()):
        for copy in side_copies:
            copy.wait_send()

        @pl.when(has_up)
        def _():
            for copy in up_copies:
                copy.wait_send()

        @pl.when(has_down)
        def _():
            for copy in down_copies:
                copy.wait_send()

    flow_load.wait()
    qc = jnp.where(edge, fl[0], 0.0)
    for i in range(1, 3):
        qc = qc + pltpu.roll(jnp.where(edge, fl[i], 0.0), 4 * i, 1)
    fs[1] = qc
    for i in range(3):
        fs[0, pl.ds(i, 1), :] = fl[i, 0:1, :]
        fs[0, pl.ds(3 + i, 1), :] = fl[i, 7:8, :]
    for copy in row_loads[:4]:
        copy.wait()

    @pl.when(has_up & has_down)
    def _():
        pl.semaphore_wait(barrier, ngx + 5)

    @pl.when(jnp.logical_not(has_up & has_down))
    def _():
        pl.semaphore_wait(barrier, ngx + 2)

    start(up_rows, down_rows)
    start(up_flow, down_flow, side_flow)
    for copy in row_loads[4:] + loads:
        copy.wait()

    def pack(half):
        def body(i, q):
            for j in range(8):
                m = i * 8 + j
                q = q + pltpu.roll(jnp.where(edge, xb[half * 32 + m], 0.0), lax.rem(CX - 4 * m, CX), 1)
            return q
        return lax.fori_loop(0, 4, body, jnp.zeros((8, CX), F32))

    qa, qb = pack(0), pack(1)
    qs[pl.ds(0, 8), :] = qa
    qs[pl.ds(8, 8), :] = qb
    start(up_corners, down_corners, side_halos)

    def weights(f0, f1, f2):
        hu, hv = 0.5 * f1, 0.5 * f2
        return 1.0 - 4.0 * f0, f0 + hv, f0 - hv, f0 + hu, f0 - hu

    own = weights(fl[0], fl[1], fl[2])
    a0, an, as_, aw, ae = own
    aw_in, ae_in = jnp.where(l0, 0.0, aw), jnp.where(l127, 0.0, ae)
    for i, v in enumerate((a0, an, as_, aw_in, ae_in)):
        cf[i] = v

    blank = jnp.zeros((M, CX), F32)
    xr[0] = blank
    xr[9] = blank
    yr[0] = blank
    yr[9] = blank

    def inner(source, target, shift):
        def body(r, carry):
            c = [jnp.broadcast_to(cf[i, pl.ds(r, 1), :], (8, CX)) for i in range(5)]
            for b in range(8):
                rows = pl.ds(8 * b, 8)
                x = source[r + 1, rows, :]
                target[r + shift, rows, :] = (
                    (c[0] * x + c[1] * source[r, rows, :]) + (c[2] * source[r + 2, rows, :] + c[3] * pltpu.roll(x, 1, 1))
                    + c[4] * pltpu.roll(x, CX - 1, 1)
                )
            return carry
        lax.fori_loop(0, CY, body, 0)

    inner(xr, yr, 1)
    inner(yr, zr, 0)

    def col(v, l):
        return jnp.broadcast_to(v[:, l:l + 1], (8, CX))

    c_edge = jnp.where(q0, col(aw, 0), jnp.where(q3, col(ae, CX - 1), 0.0))
    a0_edge = jnp.where(q0, col(a0, 0), col(a0, CX - 1))
    an_edge = jnp.where(s0, 0.0, jnp.where(q0, col(an, 0), col(an, CX - 1)))
    as_edge = jnp.where(s7, 0.0, jnp.where(q0, col(as_, 0), col(as_, CX - 1)))
    c_next = jnp.where(q1, col(aw, 1), col(ae, CX - 2))

    has_left, has_right = gx > 0, gx < ngx - 1

    def on(flag):
        return jnp.full((8, CX), jnp.where(flag, 1, 0), jnp.int32) > 0

    hmask = (s7 & on(has_up)) | (s0 & on(has_down))
    cmask = (west_side & on(has_left)) | ((quad <= 1) & on(has_right))

    received(up_flow, down_flow, side_flow)

    def flow_cols(i):
        west, east = col(fh[3], (4 * i - 1) % CX), col(fh[2], 4 * i)
        return jnp.where(cmask, jnp.where(west_side, west, east), 0.0)

    kc, uc, vc = flow_cols(0), 0.5 * flow_cols(1), 0.5 * flow_cols(2)

    def outer_row(tile, offset, flag):
        fields = [jnp.where(on(flag), jnp.broadcast_to(tile[offset + i:offset + i + 1, :], (8, CX)), 0.0) for i in range(3)]
        return weights(*fields)

    def line(v, r):
        return jnp.broadcast_to(v[r:r + 1, :], (8, CX))

    def outside(above):
        if above:
            t0, tn, ts, tw, te = outer_row(fh[1], 3, has_up)
            r, near, far, cross, toward = 0, line(an, 0), tn, ts, line(an, 1)
        else:
            t0, tn, ts, tw, te = outer_row(fh[0], 0, has_down)
            r, near, far, cross, toward = 7, line(as_, 7), ts, tn, line(as_, 6)
        west = near * jnp.where(l0, 0.0, tw) + line(aw_in, r) * pltpu.roll(near, 1, 1)
        east = near * jnp.where(l127, 0.0, te) + line(ae_in, r) * pltpu.roll(near, CX - 1, 1)
        corner = jnp.where(q0, col(near * tw, 0), jnp.where(q3, col(near * te, CX - 1), 0.0))
        return (near * (t0 + line(a0, r)), near * far, near * cross, west, east, toward * near), corner

    above, corner_above = outside(True)
    below, corner_below = outside(False)
    c_corner = jnp.where(s0, corner_above, jnp.where(s7, corner_below, 0.0))

    received(up_corners, down_corners, side_halos)
    west_cell = q3
    for half in range(2):
        q = (qa, qb)[half]
        rows = pl.ds(8 * half, 8)
        ring = jnp.where(cmask, jnp.where(west_side, hl[rows, :], hr[rows, :]), 0.0)
        corner_w = jnp.where(s7, kb[3, rows, :], kb[1, rows, :])
        corner_e = jnp.where(s7, kb[2, rows, :], kb[0, rows, :])
        corner = jnp.where(hmask & cmask, jnp.where(west_side, corner_w, corner_e), 0.0)
        n = pltpu.roll(jnp.where(s7, corner, ring), 1, 0)
        s = pltpu.roll(jnp.where(s0, corner, ring), 7, 0)
        ring_w, ring_e = pltpu.roll(ring, 1, 1), pltpu.roll(ring, CX - 1, 1)
        w = jnp.where(west_cell, ring_w, pltpu.roll(q, 1, 1))
        e = jnp.where(west_cell, pltpu.roll(q, CX - 1, 1), ring_e)
        ring1 = step(ring, n, s, w, e, kc, uc, vc)
        x1 = jnp.where(q0, ring_w, ring_e)
        y1 = jnp.where(q0, pltpu.roll(ring1, 1, 1), pltpu.roll(ring1, CX - 1, 1))
        outer = jnp.where(s0, pltpu.roll(corner, 1, 0), pltpu.roll(corner, 7, 0))
        outer = jnp.where(q0, pltpu.roll(outer, 1, 1), pltpu.roll(outer, CX - 1, 1))
        d = c_edge * x1
        at_edge = a0_edge * d + an_edge * pltpu.roll(d, 1, 0) + as_edge * pltpu.roll(d, 7, 0) + c_edge * y1 + c_corner * outer
        inside = c_next * jnp.where(q1, pltpu.roll(d, 1, 1), pltpu.roll(d, CX - 1, 1))
        zc[half] = jnp.where(q0 | q3, at_edge, inside)

    received(up_rows, down_rows)

    def add_rows(flag, c, near_row, far_row, r, r_in):
        @pl.when(flag)
        def _():
            for b in range(8):
                rows = pl.ds(8 * b, 8)
                p = near_row[rows, :]
                zr[r, rows, :] = zr[r, rows, :] + (
                    (c[0] * p + c[1] * far_row[rows, :]) + (c[2] * xr[r + 1, rows, :] + c[3] * pltpu.roll(p, 1, 1))
                    + c[4] * pltpu.roll(p, CX - 1, 1)
                )
                zr[r_in, rows, :] = zr[r_in, rows, :] + c[5] * p

    add_rows(has_up, above, hu_rows.at[1], hu_rows.at[0], 0, 1)
    add_rows(has_down, below, hd_rows.at[0], hd_rows.at[1], 7, 6)

    def add_columns(r, carry):
        lines = [jnp.broadcast_to(zc[half, pl.ds(r, 1), :], (8, CX)) for half in range(2)]
        for b in range(8):
            rows = pl.ds(8 * b, 8)
            spread = pltpu.roll(lines[b // 4], 32 * (b % 4), 1, stride=4, stride_axis=0)
            zr[r, rows, :] = zr[r, rows, :] + jnp.where(edge, spread, 0.0)
        return carry

    lax.fori_loop(0, CY, add_columns, 0)

    lane64 = iota((M, CX), 1)
    diag64 = lane64 == iota((M, CX), 0)
    ones = jnp.zeros((1, CX), F32)
    picked = []
    for j in range(4):
        cell = cells[0, 0, j]
        row, place = lax.shift_right_logical(cell, 7), cell & (CX - 1)
        column = jnp.sum(jnp.where(lane64 == place, zr[row], 0.0), axis=1, keepdims=True)
        column = jnp.broadcast_to(column, (M, CX))
        average = jnp.sum(column, axis=0, keepdims=True) * (1.0 / M)
        factor = lax.rsqrt(ones + varis[0, 0, j])
        values = jnp.sum(jnp.where(diag64, column, 0.0), axis=0, keepdims=True)
        values = jnp.where(iota((1, CX), 1) < M - 1, values, ones + vals[0, 0, j])
        picked.append(jnp.where(iota((1, CX), 1) < M, (values - average) * factor, 0.0))
    rf[gx] = jnp.concatenate(
        [picked[0] + pltpu.roll(picked[2], M, 1), picked[1] + pltpu.roll(picked[3], M, 1)], axis=0
    )

    gx_copies = [
        pltpu.make_async_remote_copy(
            src_ref=rf.at[gx], dst_ref=rf.at[gx], send_sem=gx_send, recv_sem=gx_recv,
            device_id=partner, device_id_type=MESH,
        )
        for partner in gx_partners
    ]
    for copy in gx_copies:
        copy.start()

    for r in range(CY):
        field = zr[r]
        mean = jnp.sum(field, axis=0, keepdims=True) * (1.0 / M)
        mean_ref[pl.ds(r, 1), :] = mean
        field = field - mean
        high = field.astype(BF16)
        hilo_ref[pl.ds(0, M), pl.ds(r * CX, CX)] = high
        hilo_ref[pl.ds(M, M), pl.ds(r * CX, CX)] = (field - high.astype(F32)).astype(BF16)

    wait_all(rf, ngx - 1, gx_recv)
    gathered = jnp.concatenate([rf[i] for i in range(ngx)], axis=0)
    lane32 = iota((2 * ngx, CX), 1)
    rows = jnp.concatenate(
        [jnp.where(lane32 < M, gathered, 0.0), jnp.where(lane32 < M, pltpu.roll(gathered, M, 1), 0.0)], axis=0
    )
    gram = jnp.dot(rows.T, rows, precision=lax.Precision.HIGHEST, preferred_element_type=F32)
    gram_ref[...] = gram[0:32] + pltpu.roll(gram[32:64], M, 1)

    sent(up_rows, down_rows)
    sent(up_flow, down_flow, side_flow)
    sent(up_corners, down_corners, side_halos)
    wait_all(rf, ngx - 1, gx_send)


def wait_all(buffer, count, sem):
    piece = buffer.at[pl.ds(0, count)]
    pltpu.make_async_copy(piece, piece, sem).wait()


def sum_kernel(ngy, part_ref, gram_ref, rz, rx, z_send, z_recv, x_send, x_recv):
    gy = lax.axis_index("gy")
    gx = lax.axis_index("gx")
    nz = ngy // NX4
    zpos = gy // NX4
    xpos = lax.rem(gy, NX4)
    z_partners = [(lax.rem(gy + NX4 * i, ngy), gx) for i in range(1, nz)]
    x_partners = [(zpos * NX4 + lax.rem(xpos + i, NX4), gx) for i in range(1, NX4)]
    barrier = pltpu.get_barrier_semaphore()
    for partner in z_partners + x_partners:
        pl.semaphore_signal(barrier, inc=1, device_id=partner, device_id_type=MESH)
    rz[zpos] = part_ref[...]
    pl.semaphore_wait(barrier, nz + NX4 - 2)

    def spread(buffer, slot, partners, send, recv):
        for partner in partners:
            pltpu.make_async_remote_copy(
                src_ref=buffer.at[slot], dst_ref=buffer.at[slot], send_sem=send, recv_sem=recv,
                device_id=partner, device_id_type=MESH,
            ).start()

    spread(rz, zpos, z_partners, z_send, z_recv)
    wait_all(rz, nz - 1, z_recv)
    part = rz[0]
    for i in range(1, nz):
        part = part + rz[i]
    rx[xpos] = part
    spread(rx, xpos, x_partners, x_send, x_recv)
    wait_all(rx, NX4 - 1, x_recv)
    gram_ref[...] = (rx[0] + rx[1]) + (rx[2] + rx[3])
    wait_all(rz, nz - 1, z_send)
    wait_all(rx, NX4 - 1, x_send)


def analysis_kernel(gram_ref, hilo_ref, mean_ref, out_ref):
    lane = iota((8, CX), 1)
    sub = iota((8, CX), 0)
    packed = gram_ref[...]
    shifted = pltpu.roll(packed, M, 1)
    blocks = [packed[8 * i:8 * i + 8] for i in range(4)] + [shifted[8 * i:8 * i + 8] for i in range(4)]
    blocks = [jnp.where(lane < M - 1, b, 0.0) for b in blocks]
    row_sums = [jnp.sum(b, axis=1, keepdims=True) for b in blocks]
    last = sub == 7
    target_row = blocks[7][7:8] + jnp.where(lane[0:1] == M - 1, -row_sums[7][7:8], 0.0)
    blocks[7] = jnp.where(last, 0.0, blocks[7])
    row_sums[7] = jnp.where(last[:, 0:1], 0.0, row_sums[7])
    col_sum = functools.reduce(jnp.add, blocks)
    col_sum = jnp.sum(col_sum, axis=0, keepdims=True)
    all_sum = jnp.sum(functools.reduce(jnp.add, row_sums), axis=0, keepdims=True)
    blocks = [jnp.where(lane == M - 1, -r, b) for b, r in zip(blocks, row_sums)]
    blocks[7] = jnp.where(last, jnp.where(lane == M - 1, all_sum, -col_sum), blocks[7])
    eyes = [lane == sub + 8 * i for i in range(8)]
    blocks = [jnp.where(e, b + (M - 1.0), b) for e, b in zip(eyes, blocks)]
    diagonals = [jnp.where(e, b, 0.0) for e, b in zip(eyes, blocks)]
    scale_row = lax.rsqrt(jnp.sum(functools.reduce(jnp.add, diagonals), axis=0, keepdims=True) + jnp.where(lane[0:1] < M, 0.0, 1.0))
    scale_col = [lax.rsqrt(jnp.sum(d, axis=1, keepdims=True)) for d in diagonals]
    a = [
        jnp.where(lane == sub + (M + 8 * i), scale_col[i], jnp.where(lane < M, blocks[i] * scale_col[i] * scale_row, 0.0))
        for i in range(8)
    ]

    lower = [None] * 8
    for p in range(16):
        b, o = p // 2, 4 * (p % 2)
        cols = {
            (t, i): jnp.broadcast_to(a[i][:, 4 * p + t:4 * p + t + 1], (8, CX)) for t in range(4) for i in range(b, 8)
        }
        d = {
            (s, t): jnp.broadcast_to(cols[t, b][o + s:o + s + 1, :], (8, CX)) for s in range(4) for t in range(s + 1)
        }
        r = [jnp.broadcast_to(a[b][o + s:o + s + 1, :], (8, CX)) for s in range(4)]

        det = d[0, 0] * d[1, 1] - d[1, 0] * d[1, 0]
        inv = 1.0 / det
        i00, i10, i11 = d[1, 1] * inv, -d[1, 0] * inv, d[0, 0] * inv
        e00 = i00 * d[2, 0] + i10 * d[2, 1]
        e10 = i10 * d[2, 0] + i11 * d[2, 1]
        e01 = i00 * d[3, 0] + i10 * d[3, 1]
        e11 = i10 * d[3, 0] + i11 * d[3, 1]
        c00 = d[2, 2] - (d[2, 0] * e00 + d[2, 1] * e10)
        c10 = d[3, 2] - (d[3, 0] * e00 + d[3, 1] * e10)
        c11 = d[3, 3] - (d[3, 0] * e01 + d[3, 1] * e11)
        r2 = r[2] - (e00 * r[0] + e10 * r[1])
        r3 = r[3] - (e01 * r[0] + e11 * r[1])
        det2 = c00 * c11 - c10 * c10
        if p < 15:
            u0 = i00 * r[0] + i10 * r[1]
            u1 = i10 * r[0] + i11 * r[1]
            inv2 = 1.0 / det2
            z2 = (c11 * r2 - c10 * r3) * inv2
            z3 = (c00 * r3 - c10 * r2) * inv2
            z0 = u0 - (e00 * z2 + e01 * z3)
            z1 = u1 - (e10 * z2 + e11 * z3)
            z = (z0, z1, z2, z3)
            for i in range(b if o == 0 else b + 1, 8):
                update = (cols[0, i] * z[0] + cols[1, i] * z[1]) + (cols[2, i] * z[2] + cols[3, i] * z[3])
                new = a[i] - update
                a[i] = jnp.where(sub >= 4, new, a[i]) if i == b else new
        n0 = r[0] * lax.rsqrt(d[0, 0])
        n1 = (d[0, 0] * r[1] - d[1, 0] * r[0]) * lax.rsqrt(d[0, 0] * det)
        n2 = r2 * lax.rsqrt(c00)
        n3 = (c00 * r3 - c10 * r2) * lax.rsqrt(c00 * det2)
        rows = jnp.where(sub == o, n0, jnp.where(sub == o + 1, n1, jnp.where(sub == o + 2, n2, n3)))
        lower[b] = rows if o == 0 else jnp.where(sub >= 4, rows, lower[b])
    lower = [pltpu.roll(jnp.where(lane >= M, v, 0.0), M, 1) for v in lower]
    heads = [jnp.sum(v * target_row, axis=1, keepdims=True) for v in lower]
    weight = jnp.sum(functools.reduce(jnp.add, [v * h for v, h in zip(lower, heads)]), axis=0, keepdims=True)
    root = math.sqrt(M - 1.0)
    mix = jnp.concatenate([root * v + weight for v in lower], axis=0)
    high = mix.astype(BF16).astype(F32)
    low = mix - high
    pair = jnp.where(iota((M, CX), 1) < M, high, pltpu.roll(high, M, 1)).astype(BF16)
    low_pair = jnp.where(iota((M, CX), 1) < M, low, pltpu.roll(low, M, 1)).astype(BF16)
    left = jnp.concatenate([pair, low_pair], axis=1)
    for r in range(0, CY, 2):
        cols = pl.ds(r * CX, 2 * CX)
        block = hilo_ref[:, cols]
        right = jnp.concatenate([block, block], axis=0)
        res = jnp.dot(left, right, preferred_element_type=F32)
        out_ref[:, r, :] = res[:, :CX] + mean_ref[r:r + 1, :]
        out_ref[:, r + 1, :] = res[:, CX:] + mean_ref[r + 1:r + 2, :]


def near(array):
    return pltpu.with_memory_space_constraint(array, pltpu.VMEM)


def body(ngy, ngx, ensemble, flow, obs_cell, obs_value, obs_var):
    vmem = pl.BlockSpec(memory_space=pltpu.VMEM)
    hbm = pl.BlockSpec(memory_space=pl.ANY)
    dma = pltpu.SemaphoreType.DMA
    part, hilo, mean = pl.pallas_call(
        functools.partial(forecast_kernel, ngy, ngx),
        out_shape=(
            pltpu.VMEM((32, CX), F32),
            pltpu.VMEM((2 * M, CY * CX), BF16),
            pltpu.VMEM((CY, CX), F32),
        ),
        in_specs=[hbm] * 5,
        out_specs=(vmem,) * 3,
        scratch_shapes=[
            pltpu.VMEM((M, CY, CX), F32),
            pltpu.VMEM((CY + 2, M, CX), F32),
            pltpu.VMEM((CY + 2, M, CX), F32),
            pltpu.VMEM((CY, M, CX), F32),
            pltpu.VMEM((3, CY, CX), F32),
            pltpu.VMEM((5, CY, CX), F32),
            pltpu.SMEM((1, 1, 4), jnp.int32),
            pltpu.SMEM((1, 1, 4), F32),
            pltpu.SMEM((1, 1, 4), F32),
            pltpu.VMEM((16, CX), F32),
            pltpu.VMEM((2, 8, CX), F32),
            pltpu.VMEM((2, M, CX), F32),
            pltpu.VMEM((2, M, CX), F32),
            pltpu.VMEM((16, CX), F32),
            pltpu.VMEM((16, CX), F32),
            pltpu.VMEM((4, 16, CX), F32),
            pltpu.VMEM((4, 8, CX), F32),
            pltpu.VMEM((2, 8, CX), F32),
            pltpu.VMEM((ngx, 2, CX), F32),
            dma((13,)), dma((8,)), dma((8,)), dma((4,)), dma((4,)), dma, dma,
        ],
        compiler_params=pltpu.CompilerParams(collective_id=0, has_side_effects=True),
        name="forecast",
    )(ensemble, flow, obs_cell, obs_value, obs_var)
    gram = pl.pallas_call(
        functools.partial(sum_kernel, ngy),
        out_shape=pltpu.VMEM((32, CX), F32),
        in_specs=[vmem],
        out_specs=vmem,
        scratch_shapes=[
            pltpu.VMEM((ngy // NX4, 32, CX), F32),
            pltpu.VMEM((NX4, 32, CX), F32),
            dma, dma, dma, dma,
        ],
        compiler_params=pltpu.CompilerParams(collective_id=1, has_side_effects=True),
        name="sums",
    )(near(part))
    return pl.pallas_call(
        analysis_kernel,
        out_shape=jax.ShapeDtypeStruct((M, CY, CX), F32),
        in_specs=[vmem] * 3,
        out_specs=vmem,
        name="analysis",
    )(near(gram), near(hilo), near(mean))


def solution(mesh):
    tile = P("gy", "gx", None)
    return jax.shard_map(
        functools.partial(body, mesh.shape["gy"], mesh.shape["gx"]),
        mesh=mesh,
        in_specs=(P(None, "gy", "gx"), P(None, "gy", "gx"), tile, tile, tile),
        out_specs=P(None, "gy", "gx"),
        check_vma=False,
    )
```

```python
import functools
import math

import jax
import jax.numpy as jnp
from jax import lax
from jax.experimental import pallas as pl
from jax.experimental.pallas import tpu as pltpu
from jax.sharding import PartitionSpec as P

MESH = pl.DeviceIdType.MESH
M = 64
CY = 8
CX = 128
F32 = jnp.float32
BF16 = jnp.bfloat16
NX4 = 4


def iota(shape, dim):
    return lax.broadcasted_iota(jnp.int32, shape, dim)


def step(x, n, s, w, e, k, hu, hv):
    return x + k * (n + s + w + e - 4.0 * x) - hu * (e - w) - hv * (s - n)


def forecast_kernel(
    ngy, ngx,
    x_hbm, flow_hbm, cell_hbm, val_hbm, var_hbm,
    gram_ref, hilo_ref, mean_ref,
    xb, xr, yr, zr, fl, cf, cells, vals, varis, qs, fs, hu_rows, hd_rows, hl, hr, kb, fh, zc, rf,
    load_sem, halo_send, halo_recv, flow_send, flow_recv, gx_send, gx_recv,
):
    gy = lax.axis_index("gy")
    gx = lax.axis_index("gx")
    up, down = gy - 1, gy + 1
    has_up, has_down = gy > 0, gy < ngy - 1
    left, right = lax.rem(gx + ngx - 1, ngx), lax.rem(gx + 1, ngx)
    gx_partners = [(gy, lax.rem(gx + i, ngx)) for i in sorted(range(1, ngx), key=lambda i: -min(i, ngx - i))]

    row_loads = [pltpu.make_async_copy(x_hbm.at[:, r, :], xr.at[r + 1], load_sem.at[5 + r]) for r in (0, 1, 6, 7, 2, 3, 4, 5)]
    flow_load = pltpu.make_async_copy(flow_hbm, fl, load_sem.at[1])
    loads = [
        pltpu.make_async_copy(x_hbm, xb, load_sem.at[0]),
        pltpu.make_async_copy(cell_hbm, cells, load_sem.at[2]),
        pltpu.make_async_copy(val_hbm, vals, load_sem.at[3]),
        pltpu.make_async_copy(var_hbm, varis, load_sem.at[4]),
    ]
    flow_load.start()
    for copy in row_loads + loads:
        copy.start()
    barrier = pltpu.get_barrier_semaphore()

    def greet(partners):
        for partner in partners:
            pl.semaphore_signal(barrier, inc=1, device_id=partner, device_id_type=MESH)

    @pl.when(has_up)
    def _():
        greet([(up, gx), (up, left), (up, right)])

    @pl.when(has_down)
    def _():
        greet([(down, gx), (down, left), (down, right)])

    greet(gx_partners)

    lane = iota((8, CX), 1)
    sub = iota((8, CX), 0)
    edge = (lane <= 1) | (lane >= CX - 2)
    s0, s7 = sub == 0, sub == 7
    l0, l127 = lane == 0, lane == CX - 1
    quad = lane & 3
    q0, q1, q3 = quad == 0, quad == 1, quad == 3
    west_side = quad >= 2

    def remote(src, dst, index, target, send=halo_send, recv=halo_recv):
        return pltpu.make_async_remote_copy(
            src_ref=src, dst_ref=dst, send_sem=send.at[index], recv_sem=recv.at[index],
            device_id=target, device_id_type=MESH,
        )

    up_flow = [remote(fs.at[0], fh.at[0], 0, (up, gx), flow_send, flow_recv)]
    down_flow = [remote(fs.at[0], fh.at[1], 1, (down, gx), flow_send, flow_recv)]
    side_flow = [
        remote(fs.at[1], fh.at[2], 2, (gy, left), flow_send, flow_recv),
        remote(fs.at[1], fh.at[3], 3, (gy, right), flow_send, flow_recv),
    ]
    up_rows = [remote(xr.at[pl.ds(1, 2)], hd_rows, 0, (up, gx))]
    down_rows = [remote(xr.at[pl.ds(7, 2)], hu_rows, 1, (down, gx))]
    up_corners = [remote(qs, kb.at[0], 4, (up, left)), remote(qs, kb.at[1], 5, (up, right))]
    down_corners = [remote(qs, kb.at[2], 6, (down, left)), remote(qs, kb.at[3], 7, (down, right))]
    side_halos = [remote(qs, hr, 2, (gy, left)), remote(qs, hl, 3, (gy, right))]

    def start(up_copies, down_copies, side_copies=()):
        @pl.when(has_up)
        def _():
            for copy in up_copies:
                copy.start()

        @pl.when(has_down)
        def _():
            for copy in down_copies:
                copy.start()

        for copy in side_copies:
            copy.start()

    def received(up_copies, down_copies, side_copies=()):
        for copy in side_copies:
            copy.wait_recv()

        @pl.when(has_up)
        def _():
            for copy in down_copies:
                copy.wait_recv()

        @pl.when(has_down)
        def _():
            for copy in up_copies:
                copy.wait_recv()

    def sent(up_copies, down_copies, side_copies=()):
        for copy in side_copies:
            copy.wait_send()

        @pl.when(has_up)
        def _():
            for copy in up_copies:
                copy.wait_send()

        @pl.when(has_down)
        def _():
            for copy in down_copies:
                copy.wait_send()

    flow_load.wait()
    qc = jnp.where(edge, fl[0], 0.0)
    for i in range(1, 3):
        qc = qc + pltpu.roll(jnp.where(edge, fl[i], 0.0), 4 * i, 1)
    fs[1] = qc
    for i in range(3):
        fs[0, pl.ds(i, 1), :] = fl[i, 0:1, :]
        fs[0, pl.ds(3 + i, 1), :] = fl[i, 7:8, :]
    for copy in row_loads[:4]:
        copy.wait()

    @pl.when(has_up & has_down)
    def _():
        pl.semaphore_wait(barrier, ngx + 5)

    @pl.when(jnp.logical_not(has_up & has_down))
    def _():
        pl.semaphore_wait(barrier, ngx + 2)

    start(up_rows, down_rows)
    start(up_flow, down_flow, side_flow)
    for copy in row_loads[4:] + loads:
        copy.wait()

    def pack(half):
        def body(i, q):
            for j in range(8):
                m = i * 8 + j
                q = q + pltpu.roll(jnp.where(edge, xb[half * 32 + m], 0.0), lax.rem(CX - 4 * m, CX), 1)
            return q
        return lax.fori_loop(0, 4, body, jnp.zeros((8, CX), F32))

    qa, qb = pack(0), pack(1)
    qs[pl.ds(0, 8), :] = qa
    qs[pl.ds(8, 8), :] = qb
    start(up_corners, down_corners, side_halos)

    def weights(f0, f1, f2):
        hu, hv = 0.5 * f1, 0.5 * f2
        return 1.0 - 4.0 * f0, f0 + hv, f0 - hv, f0 + hu, f0 - hu

    own = weights(fl[0], fl[1], fl[2])
    a0, an, as_, aw, ae = own
    aw_in, ae_in = jnp.where(l0, 0.0, aw), jnp.where(l127, 0.0, ae)
    for i, v in enumerate((a0, an, as_, aw_in, ae_in)):
        cf[i] = v

    blank = jnp.zeros((M, CX), F32)
    xr[0] = blank
    xr[9] = blank
    yr[0] = blank
    yr[9] = blank

    def inner(source, target, shift):
        def body(r, carry):
            c = [jnp.broadcast_to(cf[i, pl.ds(r, 1), :], (8, CX)) for i in range(5)]
            for b in range(8):
                rows = pl.ds(8 * b, 8)
                x = source[r + 1, rows, :]
                target[r + shift, rows, :] = (
                    (c[0] * x + c[1] * source[r, rows, :]) + (c[2] * source[r + 2, rows, :] + c[3] * pltpu.roll(x, 1, 1))
                    + c[4] * pltpu.roll(x, CX - 1, 1)
                )
            return carry
        lax.fori_loop(0, CY, body, 0)

    inner(xr, yr, 1)
    inner(yr, zr, 0)

    def col(v, l):
        return jnp.broadcast_to(v[:, l:l + 1], (8, CX))

    c_edge = jnp.where(q0, col(aw, 0), jnp.where(q3, col(ae, CX - 1), 0.0))
    a0_edge = jnp.where(q0, col(a0, 0), col(a0, CX - 1))
    an_edge = jnp.where(s0, 0.0, jnp.where(q0, col(an, 0), col(an, CX - 1)))
    as_edge = jnp.where(s7, 0.0, jnp.where(q0, col(as_, 0), col(as_, CX - 1)))
    c_next = jnp.where(q1, col(aw, 1), col(ae, CX - 2))

    has_left, has_right = gx > 0, gx < ngx - 1

    def on(flag):
        return jnp.full((8, CX), jnp.where(flag, 1, 0), jnp.int32) > 0

    hmask = (s7 & on(has_up)) | (s0 & on(has_down))
    cmask = (west_side & on(has_left)) | ((quad <= 1) & on(has_right))

    received(up_flow, down_flow, side_flow)

    def flow_cols(i):
        west, east = col(fh[3], (4 * i - 1) % CX), col(fh[2], 4 * i)
        return jnp.where(cmask, jnp.where(west_side, west, east), 0.0)

    kc, uc, vc = flow_cols(0), 0.5 * flow_cols(1), 0.5 * flow_cols(2)

    def outer_row(tile, offset, flag):
        fields = [jnp.where(on(flag), jnp.broadcast_to(tile[offset + i:offset + i + 1, :], (8, CX)), 0.0) for i in range(3)]
        return weights(*fields)

    def line(v, r):
        return jnp.broadcast_to(v[r:r + 1, :], (8, CX))

    def outside(above):
        if above:
            t0, tn, ts, tw, te = outer_row(fh[1], 3, has_up)
            r, near, far, cross, toward = 0, line(an, 0), tn, ts, line(an, 1)
        else:
            t0, tn, ts, tw, te = outer_row(fh[0], 0, has_down)
            r, near, far, cross, toward = 7, line(as_, 7), ts, tn, line(as_, 6)
        west = near * jnp.where(l0, 0.0, tw) + line(aw_in, r) * pltpu.roll(near, 1, 1)
        east = near * jnp.where(l127, 0.0, te) + line(ae_in, r) * pltpu.roll(near, CX - 1, 1)
        corner = jnp.where(q0, col(near * tw, 0), jnp.where(q3, col(near * te, CX - 1), 0.0))
        return (near * (t0 + line(a0, r)), near * far, near * cross, west, east, toward * near), corner

    above, corner_above = outside(True)
    below, corner_below = outside(False)
    c_corner = jnp.where(s0, corner_above, jnp.where(s7, corner_below, 0.0))

    received(up_corners, down_corners, side_halos)
    west_cell = q3
    for half in range(2):
        q = (qa, qb)[half]
        rows = pl.ds(8 * half, 8)
        ring = jnp.where(cmask, jnp.where(west_side, hl[rows, :], hr[rows, :]), 0.0)
        corner_w = jnp.where(s7, kb[3, rows, :], kb[1, rows, :])
        corner_e = jnp.where(s7, kb[2, rows, :], kb[0, rows, :])
        corner = jnp.where(hmask & cmask, jnp.where(west_side, corner_w, corner_e), 0.0)
        n = pltpu.roll(jnp.where(s7, corner, ring), 1, 0)
        s = pltpu.roll(jnp.where(s0, corner, ring), 7, 0)
        ring_w, ring_e = pltpu.roll(ring, 1, 1), pltpu.roll(ring, CX - 1, 1)
        w = jnp.where(west_cell, ring_w, pltpu.roll(q, 1, 1))
        e = jnp.where(west_cell, pltpu.roll(q, CX - 1, 1), ring_e)
        ring1 = step(ring, n, s, w, e, kc, uc, vc)
        x1 = jnp.where(q0, ring_w, ring_e)
        y1 = jnp.where(q0, pltpu.roll(ring1, 1, 1), pltpu.roll(ring1, CX - 1, 1))
        outer = jnp.where(s0, pltpu.roll(corner, 1, 0), pltpu.roll(corner, 7, 0))
        outer = jnp.where(q0, pltpu.roll(outer, 1, 1), pltpu.roll(outer, CX - 1, 1))
        d = c_edge * x1
        at_edge = a0_edge * d + an_edge * pltpu.roll(d, 1, 0) + as_edge * pltpu.roll(d, 7, 0) + c_edge * y1 + c_corner * outer
        inside = c_next * jnp.where(q1, pltpu.roll(d, 1, 1), pltpu.roll(d, CX - 1, 1))
        zc[half] = jnp.where(q0 | q3, at_edge, inside)

    received(up_rows, down_rows)

    def add_rows(flag, c, near_row, far_row, r, r_in):
        @pl.when(flag)
        def _():
            for b in range(8):
                rows = pl.ds(8 * b, 8)
                p = near_row[rows, :]
                zr[r, rows, :] = zr[r, rows, :] + (
                    (c[0] * p + c[1] * far_row[rows, :]) + (c[2] * xr[r + 1, rows, :] + c[3] * pltpu.roll(p, 1, 1))
                    + c[4] * pltpu.roll(p, CX - 1, 1)
                )
                zr[r_in, rows, :] = zr[r_in, rows, :] + c[5] * p

    add_rows(has_up, above, hu_rows.at[1], hu_rows.at[0], 0, 1)
    add_rows(has_down, below, hd_rows.at[0], hd_rows.at[1], 7, 6)

    def add_columns(r, carry):
        lines = [jnp.broadcast_to(zc[half, pl.ds(r, 1), :], (8, CX)) for half in range(2)]
        for b in range(8):
            rows = pl.ds(8 * b, 8)
            spread = pltpu.roll(lines[b // 4], 32 * (b % 4), 1, stride=4, stride_axis=0)
            zr[r, rows, :] = zr[r, rows, :] + jnp.where(edge, spread, 0.0)
        return carry

    lax.fori_loop(0, CY, add_columns, 0)

    lane64 = iota((M, CX), 1)
    diag64 = lane64 == iota((M, CX), 0)
    ones = jnp.zeros((1, CX), F32)
    picked = []
    for j in range(4):
        cell = cells[0, 0, j]
        row, place = lax.shift_right_logical(cell, 7), cell & (CX - 1)
        column = jnp.sum(jnp.where(lane64 == place, zr[row], 0.0), axis=1, keepdims=True)
        column = jnp.broadcast_to(column, (M, CX))
        average = jnp.sum(column, axis=0, keepdims=True) * (1.0 / M)
        factor = lax.rsqrt(ones + varis[0, 0, j])
        values = jnp.sum(jnp.where(diag64, column, 0.0), axis=0, keepdims=True)
        values = jnp.where(iota((1, CX), 1) < M - 1, values, ones + vals[0, 0, j])
        picked.append(jnp.where(iota((1, CX), 1) < M, (values - average) * factor, 0.0))
    rf[gx] = jnp.concatenate(
        [picked[0] + pltpu.roll(picked[2], M, 1), picked[1] + pltpu.roll(picked[3], M, 1)], axis=0
    )

    gx_copies = [
        pltpu.make_async_remote_copy(
            src_ref=rf.at[gx], dst_ref=rf.at[gx], send_sem=gx_send, recv_sem=gx_recv,
            device_id=partner, device_id_type=MESH,
        )
        for partner in gx_partners
    ]
    for copy in gx_copies:
        copy.start()

    for r in range(CY):
        field = zr[r]
        mean = jnp.sum(field, axis=0, keepdims=True) * (1.0 / M)
        mean_ref[pl.ds(r, 1), :] = mean
        field = field - mean
        high = field.astype(BF16)
        hilo_ref[pl.ds(0, M), pl.ds(r * CX, CX)] = high
        hilo_ref[pl.ds(M, M), pl.ds(r * CX, CX)] = (field - high.astype(F32)).astype(BF16)

    wait_all(rf, ngx - 1, gx_recv)
    gathered = jnp.concatenate([rf[i] for i in range(ngx)], axis=0)
    lane32 = iota((2 * ngx, CX), 1)
    rows = jnp.concatenate(
        [jnp.where(lane32 < M, gathered, 0.0), jnp.where(lane32 < M, pltpu.roll(gathered, M, 1), 0.0)], axis=0
    )
    gram = jnp.dot(rows.T, rows, precision=lax.Precision.HIGHEST, preferred_element_type=F32)
    gram_ref[...] = gram[0:32] + pltpu.roll(gram[32:64], M, 1)

    sent(up_rows, down_rows)
    sent(up_flow, down_flow, side_flow)
    sent(up_corners, down_corners, side_halos)
    wait_all(rf, ngx - 1, gx_send)


def wait_all(buffer, count, sem):
    piece = buffer.at[pl.ds(0, count)]
    pltpu.make_async_copy(piece, piece, sem).wait()


def sum_kernel(ngy, part_ref, gram_ref, rz, rx, z_send, z_recv, x_send, x_recv):
    gy = lax.axis_index("gy")
    gx = lax.axis_index("gx")
    nz = ngy // NX4
    zpos = gy // NX4
    xpos = lax.rem(gy, NX4)
    core = lax.rem(gx, 2)
    other = gx + 1 - 2 * core
    z_partners = [(lax.rem(gy + NX4 * i, ngy), gx) for i in range(1, nz)]
    x_partners = [(zpos * NX4 + lax.rem(xpos + i, NX4), g) for i in (2, 1, 3) for g in (gx, other)] + [(gy, other)]
    barrier = pltpu.get_barrier_semaphore()
    for partner in z_partners + x_partners:
        pl.semaphore_signal(barrier, inc=1, device_id=partner, device_id_type=MESH)
    rz[zpos] = part_ref[pl.ds(pl.multiple_of(16 * core, 16), 16), :]
    pl.semaphore_wait(barrier, nz - 1 + 2 * NX4 - 1)

    def spread(buffer, slot, partners, send, recv):
        for partner in partners:
            pltpu.make_async_remote_copy(
                src_ref=buffer.at[slot], dst_ref=buffer.at[slot], send_sem=send, recv_sem=recv,
                device_id=partner, device_id_type=MESH,
            ).start()

    spread(rz, zpos, z_partners, z_send, z_recv)
    wait_all(rz, nz - 1, z_recv)
    half = rz[0]
    for i in range(1, nz):
        half = half + rz[i]
    rx[2 * xpos + core] = half
    spread(rx, 2 * xpos + core, x_partners, x_send, x_recv)
    wait_all(rx, 2 * NX4 - 1, x_recv)
    for c in range(2):
        gram_ref[pl.ds(16 * c, 16), :] = (rx[c] + rx[2 + c]) + (rx[4 + c] + rx[6 + c])
    wait_all(rz, nz - 1, z_send)
    wait_all(rx, 2 * NX4 - 1, x_send)


def analysis_kernel(gram_ref, hilo_ref, mean_ref, out_ref):
    lane = iota((8, CX), 1)
    sub = iota((8, CX), 0)
    packed = gram_ref[...]
    shifted = pltpu.roll(packed, M, 1)
    blocks = [packed[8 * i:8 * i + 8] for i in range(4)] + [shifted[8 * i:8 * i + 8] for i in range(4)]
    blocks = [jnp.where(lane < M - 1, b, 0.0) for b in blocks]
    row_sums = [jnp.sum(b, axis=1, keepdims=True) for b in blocks]
    eyes = [lane == sub + 8 * i for i in range(8)]
    diagonals = [jnp.where(e, b, 0.0) for e, b in zip(eyes, blocks)]
    last = sub == 7
    target_row = blocks[7][7:8] + jnp.where(lane[0:1] == M - 1, -row_sums[7][7:8], 0.0)
    blocks[7] = jnp.where(last, 0.0, blocks[7])
    row_sums[7] = jnp.where(last[:, 0:1], 0.0, row_sums[7])
    col_sum = functools.reduce(jnp.add, blocks)
    col_sum = jnp.sum(col_sum, axis=0, keepdims=True)
    all_sum = jnp.sum(functools.reduce(jnp.add, row_sums), axis=0, keepdims=True)
    blocks = [jnp.where(lane == M - 1, -r, b) for b, r in zip(blocks, row_sums)]
    blocks[7] = jnp.where(last, jnp.where(lane == M - 1, all_sum, -col_sum), blocks[7])
    scale_row = jnp.sum(functools.reduce(jnp.add, diagonals), axis=0, keepdims=True)
    scale_row = lax.rsqrt((M - 1.0) + jnp.where(lane[0:1] == M - 1, all_sum, scale_row))
    scale_col = [jnp.sum(d, axis=1, keepdims=True) for d in diagonals]
    scale_col[7] = jnp.where(last[:, 0:1], all_sum, scale_col[7])
    scale_col = [lax.rsqrt((M - 1.0) + c) for c in scale_col]
    blocks = [jnp.where(e, b + (M - 1.0), b) for e, b in zip(eyes, blocks)]
    a = [
        jnp.where(lane == sub + (M + 8 * i), scale_col[i], jnp.where(lane < M, blocks[i] * scale_col[i] * scale_row, 0.0))
        for i in range(8)
    ]

    lower = [None] * 8
    for p in range(16):
        b, o = p // 2, 4 * (p % 2)
        cols = {
            (t, i): jnp.broadcast_to(a[i][:, 4 * p + t:4 * p + t + 1], (8, CX)) for t in range(4) for i in range(b, 8)
        }
        d = {
            (s, t): jnp.broadcast_to(cols[t, b][o + s:o + s + 1, :], (8, CX)) for s in range(4) for t in range(s + 1)
        }
        r = [jnp.broadcast_to(a[b][o + s:o + s + 1, :], (8, CX)) for s in range(4)]

        det = d[0, 0] * d[1, 1] - d[1, 0] * d[1, 0]
        inv = 1.0 / det
        i00, i10, i11 = d[1, 1] * inv, -d[1, 0] * inv, d[0, 0] * inv
        e00 = i00 * d[2, 0] + i10 * d[2, 1]
        e10 = i10 * d[2, 0] + i11 * d[2, 1]
        e01 = i00 * d[3, 0] + i10 * d[3, 1]
        e11 = i10 * d[3, 0] + i11 * d[3, 1]
        c00 = d[2, 2] - (d[2, 0] * e00 + d[2, 1] * e10)
        c10 = d[3, 2] - (d[3, 0] * e00 + d[3, 1] * e10)
        c11 = d[3, 3] - (d[3, 0] * e01 + d[3, 1] * e11)
        r2 = r[2] - (e00 * r[0] + e10 * r[1])
        r3 = r[3] - (e01 * r[0] + e11 * r[1])
        det2 = c00 * c11 - c10 * c10
        if p < 15:
            u0 = i00 * r[0] + i10 * r[1]
            u1 = i10 * r[0] + i11 * r[1]
            inv2 = 1.0 / det2
            z2 = (c11 * r2 - c10 * r3) * inv2
            z3 = (c00 * r3 - c10 * r2) * inv2
            z0 = u0 - (e00 * z2 + e01 * z3)
            z1 = u1 - (e10 * z2 + e11 * z3)
            z = (z0, z1, z2, z3)
            for i in range(b if o == 0 else b + 1, 8):
                update = (cols[0, i] * z[0] + cols[1, i] * z[1]) + (cols[2, i] * z[2] + cols[3, i] * z[3])
                new = a[i] - update
                a[i] = jnp.where(sub >= 4, new, a[i]) if i == b else new
        n0 = r[0] * lax.rsqrt(d[0, 0])
        n1 = (d[0, 0] * r[1] - d[1, 0] * r[0]) * lax.rsqrt(d[0, 0] * det)
        n2 = r2 * lax.rsqrt(c00)
        n3 = (c00 * r3 - c10 * r2) * lax.rsqrt(c00 * det2)
        rows = jnp.where(sub == o, n0, jnp.where(sub == o + 1, n1, jnp.where(sub == o + 2, n2, n3)))
        lower[b] = rows if o == 0 else jnp.where(sub >= 4, rows, lower[b])
    lower = [pltpu.roll(jnp.where(lane >= M, v, 0.0), M, 1) for v in lower]
    heads = [jnp.sum(v * target_row, axis=1, keepdims=True) for v in lower]
    weight = jnp.sum(functools.reduce(jnp.add, [v * h for v, h in zip(lower, heads)]), axis=0, keepdims=True)
    root = math.sqrt(M - 1.0)
    mix = jnp.concatenate([root * v + weight for v in lower], axis=0)
    high = mix.astype(BF16).astype(F32)
    low = mix - high
    pair = jnp.where(iota((M, CX), 1) < M, high, pltpu.roll(high, M, 1)).astype(BF16)
    low_pair = jnp.where(iota((M, CX), 1) < M, low, pltpu.roll(low, M, 1)).astype(BF16)
    left = jnp.concatenate([pair, low_pair], axis=1)
    for r in range(0, CY, 2):
        cols = pl.ds(r * CX, 2 * CX)
        block = hilo_ref[:, cols]
        right = jnp.concatenate([block, block], axis=0)
        res = jnp.dot(left, right, preferred_element_type=F32)
        out_ref[:, r, :] = res[:, :CX] + mean_ref[r:r + 1, :]
        out_ref[:, r + 1, :] = res[:, CX:] + mean_ref[r + 1:r + 2, :]


def near(array):
    return pltpu.with_memory_space_constraint(array, pltpu.VMEM)


def body(ngy, ngx, ensemble, flow, obs_cell, obs_value, obs_var):
    vmem = pl.BlockSpec(memory_space=pltpu.VMEM)
    hbm = pl.BlockSpec(memory_space=pl.ANY)
    dma = pltpu.SemaphoreType.DMA
    part, hilo, mean = pl.pallas_call(
        functools.partial(forecast_kernel, ngy, ngx),
        out_shape=(
            pltpu.VMEM((32, CX), F32),
            pltpu.VMEM((2 * M, CY * CX), BF16),
            pltpu.VMEM((CY, CX), F32),
        ),
        in_specs=[hbm] * 5,
        out_specs=(vmem,) * 3,
        scratch_shapes=[
            pltpu.VMEM((M, CY, CX), F32),
            pltpu.VMEM((CY + 2, M, CX), F32),
            pltpu.VMEM((CY + 2, M, CX), F32),
            pltpu.VMEM((CY, M, CX), F32),
            pltpu.VMEM((3, CY, CX), F32),
            pltpu.VMEM((5, CY, CX), F32),
            pltpu.SMEM((1, 1, 4), jnp.int32),
            pltpu.SMEM((1, 1, 4), F32),
            pltpu.SMEM((1, 1, 4), F32),
            pltpu.VMEM((16, CX), F32),
            pltpu.VMEM((2, 8, CX), F32),
            pltpu.VMEM((2, M, CX), F32),
            pltpu.VMEM((2, M, CX), F32),
            pltpu.VMEM((16, CX), F32),
            pltpu.VMEM((16, CX), F32),
            pltpu.VMEM((4, 16, CX), F32),
            pltpu.VMEM((4, 8, CX), F32),
            pltpu.VMEM((2, 8, CX), F32),
            pltpu.VMEM((ngx, 2, CX), F32),
            dma((13,)), dma((8,)), dma((8,)), dma((4,)), dma((4,)), dma, dma,
        ],
        compiler_params=pltpu.CompilerParams(collective_id=0, has_side_effects=True),
        name="forecast",
    )(ensemble, flow, obs_cell, obs_value, obs_var)
    gram = pl.pallas_call(
        functools.partial(sum_kernel, ngy),
        out_shape=pltpu.VMEM((32, CX), F32),
        in_specs=[vmem],
        out_specs=vmem,
        scratch_shapes=[
            pltpu.VMEM((ngy // NX4, 16, CX), F32),
            pltpu.VMEM((2 * NX4, 16, CX), F32),
            dma, dma, dma, dma,
        ],
        compiler_params=pltpu.CompilerParams(collective_id=1, has_side_effects=True),
        name="sums",
    )(near(part))
    return pl.pallas_call(
        analysis_kernel,
        out_shape=jax.ShapeDtypeStruct((M, CY, CX), F32),
        in_specs=[vmem] * 3,
        out_specs=vmem,
        name="analysis",
    )(near(gram), near(hilo), near(mean))


def solution(mesh):
    tile = P("gy", "gx", None)
    return jax.shard_map(
        functools.partial(body, mesh.shape["gy"], mesh.shape["gx"]),
        mesh=mesh,
        in_specs=(P(None, "gy", "gx"), P(None, "gy", "gx"), tile, tile, tile),
        out_specs=P(None, "gy", "gx"),
        check_vma=False,
    )
```

```python
import functools
import math

import jax
import jax.numpy as jnp
from jax import lax
from jax.experimental import pallas as pl
from jax.experimental.pallas import tpu as pltpu
from jax.sharding import PartitionSpec as P

MESH = pl.DeviceIdType.MESH
M = 64
CY = 8
CX = 128
F32 = jnp.float32
BF16 = jnp.bfloat16
NX4 = 4


def iota(shape, dim):
    return lax.broadcasted_iota(jnp.int32, shape, dim)


def step(x, n, s, w, e, k, hu, hv):
    return x + k * (n + s + w + e - 4.0 * x) - hu * (e - w) - hv * (s - n)


def forecast_kernel(
    ngy, ngx,
    x_hbm, flow_hbm, cell_hbm, val_hbm, var_hbm,
    gram_ref, hilo_ref, mean_ref,
    xb, xr, yr, zr, fl, cf, cells, vals, varis, qs, fs, hu_rows, hd_rows, hl, hr, kb, fh, zc, rf,
    load_sem, halo_send, halo_recv, flow_send, flow_recv, gx_send, gx_recv,
):
    gy = lax.axis_index("gy")
    gx = lax.axis_index("gx")
    up, down = gy - 1, gy + 1
    has_up, has_down = gy > 0, gy < ngy - 1
    left, right = lax.rem(gx + ngx - 1, ngx), lax.rem(gx + 1, ngx)
    gx_partners = [(gy, lax.rem(gx + i, ngx)) for i in sorted(range(1, ngx), key=lambda i: -min(i, ngx - i))]

    row_loads = [pltpu.make_async_copy(x_hbm.at[:, r, :], xr.at[r + 1], load_sem.at[5 + r]) for r in (0, 1, 6, 7, 2, 3, 4, 5)]
    flow_load = pltpu.make_async_copy(flow_hbm, fl, load_sem.at[1])
    loads = [
        pltpu.make_async_copy(x_hbm, xb, load_sem.at[0]),
        pltpu.make_async_copy(cell_hbm, cells, load_sem.at[2]),
        pltpu.make_async_copy(val_hbm, vals, load_sem.at[3]),
        pltpu.make_async_copy(var_hbm, varis, load_sem.at[4]),
    ]
    flow_load.start()
    for copy in row_loads + loads:
        copy.start()
    barrier = pltpu.get_barrier_semaphore()

    def greet(partners):
        for partner in partners:
            pl.semaphore_signal(barrier, inc=1, device_id=partner, device_id_type=MESH)

    @pl.when(has_up)
    def _():
        greet([(up, gx), (up, left), (up, right)])

    @pl.when(has_down)
    def _():
        greet([(down, gx), (down, left), (down, right)])

    greet(gx_partners)

    lane = iota((8, CX), 1)
    sub = iota((8, CX), 0)
    edge = (lane <= 1) | (lane >= CX - 2)
    s0, s7 = sub == 0, sub == 7
    l0, l127 = lane == 0, lane == CX - 1
    quad = lane & 3
    q0, q1, q3 = quad == 0, quad == 1, quad == 3
    west_side = quad >= 2

    def remote(src, dst, index, target, send=halo_send, recv=halo_recv):
        return pltpu.make_async_remote_copy(
            src_ref=src, dst_ref=dst, send_sem=send.at[index], recv_sem=recv.at[index],
            device_id=target, device_id_type=MESH,
        )

    up_flow = [remote(fs.at[0], fh.at[0], 0, (up, gx), flow_send, flow_recv)]
    down_flow = [remote(fs.at[0], fh.at[1], 1, (down, gx), flow_send, flow_recv)]
    side_flow = [
        remote(fs.at[1], fh.at[2], 2, (gy, left), flow_send, flow_recv),
        remote(fs.at[1], fh.at[3], 3, (gy, right), flow_send, flow_recv),
    ]
    up_rows = [remote(xr.at[pl.ds(1, 2)], hd_rows, 0, (up, gx))]
    down_rows = [remote(xr.at[pl.ds(7, 2)], hu_rows, 1, (down, gx))]
    up_corners = [remote(qs, kb.at[0], 4, (up, left)), remote(qs, kb.at[1], 5, (up, right))]
    down_corners = [remote(qs, kb.at[2], 6, (down, left)), remote(qs, kb.at[3], 7, (down, right))]
    side_halos = [remote(qs, hr, 2, (gy, left)), remote(qs, hl, 3, (gy, right))]

    def start(up_copies, down_copies, side_copies=()):
        @pl.when(has_up)
        def _():
            for copy in up_copies:
                copy.start()

        @pl.when(has_down)
        def _():
            for copy in down_copies:
                copy.start()

        for copy in side_copies:
            copy.start()

    def received(up_copies, down_copies, side_copies=()):
        for copy in side_copies:
            copy.wait_recv()

        @pl.when(has_up)
        def _():
            for copy in down_copies:
                copy.wait_recv()

        @pl.when(has_down)
        def _():
            for copy in up_copies:
                copy.wait_recv()

    def sent(up_copies, down_copies, side_copies=()):
        for copy in side_copies:
            copy.wait_send()

        @pl.when(has_up)
        def _():
            for copy in up_copies:
                copy.wait_send()

        @pl.when(has_down)
        def _():
            for copy in down_copies:
                copy.wait_send()

    flow_load.wait()
    qc = jnp.where(edge, fl[0], 0.0)
    for i in range(1, 3):
        qc = qc + pltpu.roll(jnp.where(edge, fl[i], 0.0), 4 * i, 1)
    fs[1] = qc
    for i in range(3):
        fs[0, pl.ds(i, 1), :] = fl[i, 0:1, :]
        fs[0, pl.ds(3 + i, 1), :] = fl[i, 7:8, :]
    for copy in row_loads[:4]:
        copy.wait()

    @pl.when(has_up & has_down)
    def _():
        pl.semaphore_wait(barrier, ngx + 5)

    @pl.when(jnp.logical_not(has_up & has_down))
    def _():
        pl.semaphore_wait(barrier, ngx + 2)

    start(up_rows, down_rows)
    start(up_flow, down_flow, side_flow)
    for copy in row_loads[4:] + loads:
        copy.wait()

    def pack(half):
        def body(i, q):
            for j in range(8):
                m = i * 8 + j
                q = q + pltpu.roll(jnp.where(edge, xb[half * 32 + m], 0.0), lax.rem(CX - 4 * m, CX), 1)
            return q
        return lax.fori_loop(0, 4, body, jnp.zeros((8, CX), F32))

    qa, qb = pack(0), pack(1)
    qs[pl.ds(0, 8), :] = qa
    qs[pl.ds(8, 8), :] = qb
    start(up_corners, down_corners, side_halos)

    def weights(f0, f1, f2):
        hu, hv = 0.5 * f1, 0.5 * f2
        return 1.0 - 4.0 * f0, f0 + hv, f0 - hv, f0 + hu, f0 - hu

    own = weights(fl[0], fl[1], fl[2])
    a0, an, as_, aw, ae = own
    aw_in, ae_in = jnp.where(l0, 0.0, aw), jnp.where(l127, 0.0, ae)
    for i, v in enumerate((a0, an, as_, aw_in, ae_in)):
        cf[i] = v

    blank = jnp.zeros((M, CX), F32)
    xr[0] = blank
    xr[9] = blank
    yr[0] = blank
    yr[9] = blank

    def inner(source, target, shift):
        def body(r, carry):
            c = [jnp.broadcast_to(cf[i, pl.ds(r, 1), :], (8, CX)) for i in range(5)]
            for b in range(8):
                rows = pl.ds(8 * b, 8)
                x = source[r + 1, rows, :]
                target[r + shift, rows, :] = (
                    (c[0] * x + c[1] * source[r, rows, :]) + (c[2] * source[r + 2, rows, :] + c[3] * pltpu.roll(x, 1, 1))
                    + c[4] * pltpu.roll(x, CX - 1, 1)
                )
            return carry
        lax.fori_loop(0, CY, body, 0)

    inner(xr, yr, 1)
    inner(yr, zr, 0)

    def col(v, l):
        return jnp.broadcast_to(v[:, l:l + 1], (8, CX))

    c_edge = jnp.where(q0, col(aw, 0), jnp.where(q3, col(ae, CX - 1), 0.0))
    a0_edge = jnp.where(q0, col(a0, 0), col(a0, CX - 1))
    an_edge = jnp.where(s0, 0.0, jnp.where(q0, col(an, 0), col(an, CX - 1)))
    as_edge = jnp.where(s7, 0.0, jnp.where(q0, col(as_, 0), col(as_, CX - 1)))
    c_next = jnp.where(q1, col(aw, 1), col(ae, CX - 2))

    has_left, has_right = gx > 0, gx < ngx - 1

    def on(flag):
        return jnp.full((8, CX), jnp.where(flag, 1, 0), jnp.int32) > 0

    hmask = (s7 & on(has_up)) | (s0 & on(has_down))
    cmask = (west_side & on(has_left)) | ((quad <= 1) & on(has_right))

    received(up_flow, down_flow, side_flow)

    def flow_cols(i):
        west, east = col(fh[3], (4 * i - 1) % CX), col(fh[2], 4 * i)
        return jnp.where(cmask, jnp.where(west_side, west, east), 0.0)

    kc, uc, vc = flow_cols(0), 0.5 * flow_cols(1), 0.5 * flow_cols(2)

    def outer_row(tile, offset, flag):
        fields = [jnp.where(on(flag), jnp.broadcast_to(tile[offset + i:offset + i + 1, :], (8, CX)), 0.0) for i in range(3)]
        return weights(*fields)

    def line(v, r):
        return jnp.broadcast_to(v[r:r + 1, :], (8, CX))

    def outside(above):
        if above:
            t0, tn, ts, tw, te = outer_row(fh[1], 3, has_up)
            r, near, far, cross, toward = 0, line(an, 0), tn, ts, line(an, 1)
        else:
            t0, tn, ts, tw, te = outer_row(fh[0], 0, has_down)
            r, near, far, cross, toward = 7, line(as_, 7), ts, tn, line(as_, 6)
        west = near * jnp.where(l0, 0.0, tw) + line(aw_in, r) * pltpu.roll(near, 1, 1)
        east = near * jnp.where(l127, 0.0, te) + line(ae_in, r) * pltpu.roll(near, CX - 1, 1)
        corner = jnp.where(q0, col(near * tw, 0), jnp.where(q3, col(near * te, CX - 1), 0.0))
        return (near * (t0 + line(a0, r)), near * far, near * cross, west, east, toward * near), corner

    above, corner_above = outside(True)
    below, corner_below = outside(False)
    c_corner = jnp.where(s0, corner_above, jnp.where(s7, corner_below, 0.0))

    received(up_corners, down_corners, side_halos)
    west_cell = q3
    for half in range(2):
        q = (qa, qb)[half]
        rows = pl.ds(8 * half, 8)
        ring = jnp.where(cmask, jnp.where(west_side, hl[rows, :], hr[rows, :]), 0.0)
        corner_w = jnp.where(s7, kb[3, rows, :], kb[1, rows, :])
        corner_e = jnp.where(s7, kb[2, rows, :], kb[0, rows, :])
        corner = jnp.where(hmask & cmask, jnp.where(west_side, corner_w, corner_e), 0.0)
        n = pltpu.roll(jnp.where(s7, corner, ring), 1, 0)
        s = pltpu.roll(jnp.where(s0, corner, ring), 7, 0)
        ring_w, ring_e = pltpu.roll(ring, 1, 1), pltpu.roll(ring, CX - 1, 1)
        w = jnp.where(west_cell, ring_w, pltpu.roll(q, 1, 1))
        e = jnp.where(west_cell, pltpu.roll(q, CX - 1, 1), ring_e)
        ring1 = step(ring, n, s, w, e, kc, uc, vc)
        x1 = jnp.where(q0, ring_w, ring_e)
        y1 = jnp.where(q0, pltpu.roll(ring1, 1, 1), pltpu.roll(ring1, CX - 1, 1))
        outer = jnp.where(s0, pltpu.roll(corner, 1, 0), pltpu.roll(corner, 7, 0))
        outer = jnp.where(q0, pltpu.roll(outer, 1, 1), pltpu.roll(outer, CX - 1, 1))
        d = c_edge * x1
        at_edge = a0_edge * d + an_edge * pltpu.roll(d, 1, 0) + as_edge * pltpu.roll(d, 7, 0) + c_edge * y1 + c_corner * outer
        inside = c_next * jnp.where(q1, pltpu.roll(d, 1, 1), pltpu.roll(d, CX - 1, 1))
        zc[half] = jnp.where(q0 | q3, at_edge, inside)

    received(up_rows, down_rows)

    def add_rows(flag, c, near_row, far_row, r, r_in):
        @pl.when(flag)
        def _():
            for b in range(8):
                rows = pl.ds(8 * b, 8)
                p = near_row[rows, :]
                zr[r, rows, :] = zr[r, rows, :] + (
                    (c[0] * p + c[1] * far_row[rows, :]) + (c[2] * xr[r + 1, rows, :] + c[3] * pltpu.roll(p, 1, 1))
                    + c[4] * pltpu.roll(p, CX - 1, 1)
                )
                zr[r_in, rows, :] = zr[r_in, rows, :] + c[5] * p

    add_rows(has_up, above, hu_rows.at[1], hu_rows.at[0], 0, 1)
    add_rows(has_down, below, hd_rows.at[0], hd_rows.at[1], 7, 6)

    def add_columns(r, carry):
        lines = [jnp.broadcast_to(zc[half, pl.ds(r, 1), :], (8, CX)) for half in range(2)]
        for b in range(8):
            rows = pl.ds(8 * b, 8)
            spread = pltpu.roll(lines[b // 4], 32 * (b % 4), 1, stride=4, stride_axis=0)
            zr[r, rows, :] = zr[r, rows, :] + jnp.where(edge, spread, 0.0)
        return carry

    lax.fori_loop(0, CY, add_columns, 0)

    lane64 = iota((M, CX), 1)
    diag64 = lane64 == iota((M, CX), 0)
    ones = jnp.zeros((1, CX), F32)
    picked = []
    for j in range(4):
        cell = cells[0, 0, j]
        row, place = lax.shift_right_logical(cell, 7), cell & (CX - 1)
        column = jnp.sum(jnp.where(lane64 == place, zr[row], 0.0), axis=1, keepdims=True)
        column = jnp.broadcast_to(column, (M, CX))
        average = jnp.sum(column, axis=0, keepdims=True) * (1.0 / M)
        factor = lax.rsqrt(ones + varis[0, 0, j])
        values = jnp.sum(jnp.where(diag64, column, 0.0), axis=0, keepdims=True)
        values = jnp.where(iota((1, CX), 1) < M - 1, values, ones + vals[0, 0, j])
        picked.append(jnp.where(iota((1, CX), 1) < M, (values - average) * factor, 0.0))
    rf[gx] = jnp.concatenate(
        [picked[0] + pltpu.roll(picked[2], M, 1), picked[1] + pltpu.roll(picked[3], M, 1)], axis=0
    )

    gx_copies = [
        pltpu.make_async_remote_copy(
            src_ref=rf.at[gx], dst_ref=rf.at[gx], send_sem=gx_send, recv_sem=gx_recv,
            device_id=partner, device_id_type=MESH,
        )
        for partner in gx_partners
    ]
    for copy in gx_copies:
        copy.start()

    for r in range(CY):
        field = zr[r]
        mean = jnp.sum(field, axis=0, keepdims=True) * (1.0 / M)
        mean_ref[pl.ds(r, 1), :] = mean
        field = field - mean
        high = field.astype(BF16)
        hilo_ref[pl.ds(0, M), pl.ds(r * CX, CX)] = high
        hilo_ref[pl.ds(M, M), pl.ds(r * CX, CX)] = (field - high.astype(F32)).astype(BF16)

    wait_all(rf, ngx - 1, gx_recv)
    gathered = jnp.concatenate([rf[i] for i in range(ngx)], axis=0)
    lane32 = iota((2 * ngx, CX), 1)
    rows = jnp.concatenate(
        [jnp.where(lane32 < M, gathered, 0.0), jnp.where(lane32 < M, pltpu.roll(gathered, M, 1), 0.0)], axis=0
    )
    gram = jnp.dot(rows.T, rows, precision=lax.Precision.HIGHEST, preferred_element_type=F32)
    high, low = gram[0:32], pltpu.roll(gram[32:64], CX - 32, 1)
    across, along = iota((32, CX), 1), iota((32, CX), 0)
    square = jnp.where((across < 32) & (across > along), low, high)
    gram_ref[pl.ds(0, 16), :] = square[0:16] + pltpu.roll(square[16:32], M, 1)
    diagonal = jnp.sum(jnp.where(across == along, low, 0.0), axis=0, keepdims=True)
    gram_ref[pl.ds(16, 8), :] = jnp.where(iota((8, CX), 0) == 0, diagonal, 0.0)

    sent(up_rows, down_rows)
    sent(up_flow, down_flow, side_flow)
    sent(up_corners, down_corners, side_halos)
    wait_all(rf, ngx - 1, gx_send)


def wait_all(buffer, count, sem):
    piece = buffer.at[pl.ds(0, count)]
    pltpu.make_async_copy(piece, piece, sem).wait()


def sum_kernel(ngy, part_ref, gram_ref, rz, rx, z_send, z_recv, x_send, x_recv):
    gy = lax.axis_index("gy")
    gx = lax.axis_index("gx")
    nz = ngy // NX4
    zpos = gy // NX4
    xpos = lax.rem(gy, NX4)
    z_partners = [(lax.rem(gy + NX4 * i, ngy), gx) for i in range(1, nz)]
    x_partners = [(zpos * NX4 + lax.rem(xpos + i, NX4), gx) for i in (2, 1, 3)]
    barrier = pltpu.get_barrier_semaphore()
    for partner in z_partners + x_partners:
        pl.semaphore_signal(barrier, inc=1, device_id=partner, device_id_type=MESH)
    rz[zpos] = part_ref[...]
    pl.semaphore_wait(barrier, nz + NX4 - 2)

    def wait_rows(buffer, count, sem):
        piece = buffer.at[pl.ds(0, count), pl.ds(0, 17)]
        pltpu.make_async_copy(piece, piece, sem).wait()

    def spread(buffer, slot, partners, send, recv):
        for partner in partners:
            pltpu.make_async_remote_copy(
                src_ref=buffer.at[slot, pl.ds(0, 17)], dst_ref=buffer.at[slot, pl.ds(0, 17)], send_sem=send, recv_sem=recv,
                device_id=partner, device_id_type=MESH,
            ).start()

    spread(rz, zpos, z_partners, z_send, z_recv)
    wait_rows(rz, nz - 1, z_recv)
    part = rz[0]
    for i in range(1, nz):
        part = part + rz[i]
    rx[xpos] = part
    spread(rx, xpos, x_partners, x_send, x_recv)
    wait_rows(rx, NX4 - 1, x_recv)
    gram_ref[...] = (rx[0] + rx[1]) + (rx[2] + rx[3])
    wait_rows(rz, nz - 1, z_send)
    wait_rows(rx, NX4 - 1, x_send)


def analysis_kernel(gram_ref, hilo_ref, mean_ref, out_ref):
    lane = iota((8, CX), 1)
    sub = iota((8, CX), 0)
    packed = gram_ref[pl.ds(0, 16), :]
    square = jnp.concatenate([packed, pltpu.roll(packed, M, 1)], axis=0)
    square = jnp.where(iota((32, CX), 1) < M, square, 0.0)
    turned = jnp.concatenate([square, jnp.zeros((CX - 32, CX), F32)], axis=0).T
    across, along = iota((32, CX), 1), iota((32, CX), 0)
    top = jnp.where((across < 32) & (across > along), turned[0:32], square)
    corner = jnp.where(across > along, square, jnp.where(across == along, gram_ref[pl.ds(16, 1), :], turned[0:32]))
    corner = pltpu.roll(jnp.where(across < 32, corner, 0.0), 32, 1)
    bottom = jnp.where(across < 32, turned[32:64], corner)
    blocks = [top[8 * i:8 * i + 8] for i in range(4)] + [bottom[8 * i:8 * i + 8] for i in range(4)]
    blocks = [jnp.where(lane < M - 1, b, 0.0) for b in blocks]
    row_sums = [jnp.sum(b, axis=1, keepdims=True) for b in blocks]
    eyes = [lane == sub + 8 * i for i in range(8)]
    diagonals = [jnp.where(e, b, 0.0) for e, b in zip(eyes, blocks)]
    last = sub == 7
    target_row = blocks[7][7:8] + jnp.where(lane[0:1] == M - 1, -row_sums[7][7:8], 0.0)
    blocks[7] = jnp.where(last, 0.0, blocks[7])
    row_sums[7] = jnp.where(last[:, 0:1], 0.0, row_sums[7])
    col_sum = functools.reduce(jnp.add, blocks)
    col_sum = jnp.sum(col_sum, axis=0, keepdims=True)
    all_sum = jnp.sum(functools.reduce(jnp.add, row_sums), axis=0, keepdims=True)
    blocks = [jnp.where(lane == M - 1, -r, b) for b, r in zip(blocks, row_sums)]
    blocks[7] = jnp.where(last, jnp.where(lane == M - 1, all_sum, -col_sum), blocks[7])
    scale_row = jnp.sum(functools.reduce(jnp.add, diagonals), axis=0, keepdims=True)
    scale_row = lax.rsqrt((M - 1.0) + jnp.where(lane[0:1] == M - 1, all_sum, scale_row))
    scale_col = [jnp.sum(d, axis=1, keepdims=True) for d in diagonals]
    scale_col[7] = jnp.where(last[:, 0:1], all_sum, scale_col[7])
    scale_col = [lax.rsqrt((M - 1.0) + c) for c in scale_col]
    blocks = [jnp.where(e, b + (M - 1.0), b) for e, b in zip(eyes, blocks)]
    a = [
        jnp.where(lane == sub + (M + 8 * i), scale_col[i], jnp.where(lane < M, blocks[i] * scale_col[i] * scale_row, 0.0))
        for i in range(8)
    ]

    lower = [None] * 8
    for p in range(16):
        b, o = p // 2, 4 * (p % 2)
        cols = {
            (t, i): jnp.broadcast_to(a[i][:, 4 * p + t:4 * p + t + 1], (8, CX)) for t in range(4) for i in range(b, 8)
        }
        d = {
            (s, t): jnp.broadcast_to(cols[t, b][o + s:o + s + 1, :], (8, CX)) for s in range(4) for t in range(s + 1)
        }
        r = [jnp.broadcast_to(a[b][o + s:o + s + 1, :], (8, CX)) for s in range(4)]

        det = d[0, 0] * d[1, 1] - d[1, 0] * d[1, 0]
        inv = 1.0 / det
        i00, i10, i11 = d[1, 1] * inv, -d[1, 0] * inv, d[0, 0] * inv
        e00 = i00 * d[2, 0] + i10 * d[2, 1]
        e10 = i10 * d[2, 0] + i11 * d[2, 1]
        e01 = i00 * d[3, 0] + i10 * d[3, 1]
        e11 = i10 * d[3, 0] + i11 * d[3, 1]
        c00 = d[2, 2] - (d[2, 0] * e00 + d[2, 1] * e10)
        c10 = d[3, 2] - (d[3, 0] * e00 + d[3, 1] * e10)
        c11 = d[3, 3] - (d[3, 0] * e01 + d[3, 1] * e11)
        r2 = r[2] - (e00 * r[0] + e10 * r[1])
        r3 = r[3] - (e01 * r[0] + e11 * r[1])
        det2 = c00 * c11 - c10 * c10
        if p < 15:
            u0 = i00 * r[0] + i10 * r[1]
            u1 = i10 * r[0] + i11 * r[1]
            inv2 = 1.0 / det2
            z2 = (c11 * r2 - c10 * r3) * inv2
            z3 = (c00 * r3 - c10 * r2) * inv2
            z0 = u0 - (e00 * z2 + e01 * z3)
            z1 = u1 - (e10 * z2 + e11 * z3)
            z = (z0, z1, z2, z3)
            for i in range(b if o == 0 else b + 1, 8):
                update = (cols[0, i] * z[0] + cols[1, i] * z[1]) + (cols[2, i] * z[2] + cols[3, i] * z[3])
                new = a[i] - update
                a[i] = jnp.where(sub >= 4, new, a[i]) if i == b else new
        n0 = r[0] * lax.rsqrt(d[0, 0])
        n1 = (d[0, 0] * r[1] - d[1, 0] * r[0]) * lax.rsqrt(d[0, 0] * det)
        n2 = r2 * lax.rsqrt(c00)
        n3 = (c00 * r3 - c10 * r2) * lax.rsqrt(c00 * det2)
        rows = jnp.where(sub == o, n0, jnp.where(sub == o + 1, n1, jnp.where(sub == o + 2, n2, n3)))
        lower[b] = rows if o == 0 else jnp.where(sub >= 4, rows, lower[b])
    lower = [pltpu.roll(jnp.where(lane >= M, v, 0.0), M, 1) for v in lower]
    heads = [jnp.sum(v * target_row, axis=1, keepdims=True) for v in lower]
    weight = jnp.sum(functools.reduce(jnp.add, [v * h for v, h in zip(lower, heads)]), axis=0, keepdims=True)
    root = math.sqrt(M - 1.0)
    mix = jnp.concatenate([root * v + weight for v in lower], axis=0)
    high = mix.astype(BF16).astype(F32)
    low = mix - high
    pair = jnp.where(iota((M, CX), 1) < M, high, pltpu.roll(high, M, 1)).astype(BF16)
    low_pair = jnp.where(iota((M, CX), 1) < M, low, pltpu.roll(low, M, 1)).astype(BF16)
    left = jnp.concatenate([pair, low_pair], axis=1)
    for r in range(0, CY, 2):
        cols = pl.ds(r * CX, 2 * CX)
        block = hilo_ref[:, cols]
        right = jnp.concatenate([block, block], axis=0)
        res = jnp.dot(left, right, preferred_element_type=F32)
        out_ref[:, r, :] = res[:, :CX] + mean_ref[r:r + 1, :]
        out_ref[:, r + 1, :] = res[:, CX:] + mean_ref[r + 1:r + 2, :]


def near(array):
    return pltpu.with_memory_space_constraint(array, pltpu.VMEM)


def body(ngy, ngx, ensemble, flow, obs_cell, obs_value, obs_var):
    vmem = pl.BlockSpec(memory_space=pltpu.VMEM)
    hbm = pl.BlockSpec(memory_space=pl.ANY)
    dma = pltpu.SemaphoreType.DMA
    part, hilo, mean = pl.pallas_call(
        functools.partial(forecast_kernel, ngy, ngx),
        out_shape=(
            pltpu.VMEM((24, CX), F32),
            pltpu.VMEM((2 * M, CY * CX), BF16),
            pltpu.VMEM((CY, CX), F32),
        ),
        in_specs=[hbm] * 5,
        out_specs=(vmem,) * 3,
        scratch_shapes=[
            pltpu.VMEM((M, CY, CX), F32),
            pltpu.VMEM((CY + 2, M, CX), F32),
            pltpu.VMEM((CY + 2, M, CX), F32),
            pltpu.VMEM((CY, M, CX), F32),
            pltpu.VMEM((3, CY, CX), F32),
            pltpu.VMEM((5, CY, CX), F32),
            pltpu.SMEM((1, 1, 4), jnp.int32),
            pltpu.SMEM((1, 1, 4), F32),
            pltpu.SMEM((1, 1, 4), F32),
            pltpu.VMEM((16, CX), F32),
            pltpu.VMEM((2, 8, CX), F32),
            pltpu.VMEM((2, M, CX), F32),
            pltpu.VMEM((2, M, CX), F32),
            pltpu.VMEM((16, CX), F32),
            pltpu.VMEM((16, CX), F32),
            pltpu.VMEM((4, 16, CX), F32),
            pltpu.VMEM((4, 8, CX), F32),
            pltpu.VMEM((2, 8, CX), F32),
            pltpu.VMEM((ngx, 2, CX), F32),
            dma((13,)), dma((8,)), dma((8,)), dma((4,)), dma((4,)), dma, dma,
        ],
        compiler_params=pltpu.CompilerParams(collective_id=0, has_side_effects=True),
        name="forecast",
    )(ensemble, flow, obs_cell, obs_value, obs_var)
    gram = pl.pallas_call(
        functools.partial(sum_kernel, ngy),
        out_shape=pltpu.VMEM((24, CX), F32),
        in_specs=[vmem],
        out_specs=vmem,
        scratch_shapes=[
            pltpu.VMEM((ngy // NX4, 24, CX), F32),
            pltpu.VMEM((NX4, 24, CX), F32),
            dma, dma, dma, dma,
        ],
        compiler_params=pltpu.CompilerParams(collective_id=1, has_side_effects=True),
        name="sums",
    )(near(part))
    return pl.pallas_call(
        analysis_kernel,
        out_shape=jax.ShapeDtypeStruct((M, CY, CX), F32),
        in_specs=[vmem] * 3,
        out_specs=vmem,
        name="analysis",
    )(near(gram), near(hilo), near(mean))


def solution(mesh):
    tile = P("gy", "gx", None)
    return jax.shard_map(
        functools.partial(body, mesh.shape["gy"], mesh.shape["gx"]),
        mesh=mesh,
        in_specs=(P(None, "gy", "gx"), P(None, "gy", "gx"), tile, tile, tile),
        out_specs=P(None, "gy", "gx"),
        check_vma=False,
    )
```

```python
import functools
import math

import jax
import jax.numpy as jnp
from jax import lax
from jax.experimental import pallas as pl
from jax.experimental.pallas import tpu as pltpu
from jax.sharding import PartitionSpec as P

MESH = pl.DeviceIdType.MESH
M = 64
CY = 8
CX = 128
F32 = jnp.float32
BF16 = jnp.bfloat16
NX4 = 4


def iota(shape, dim):
    return lax.broadcasted_iota(jnp.int32, shape, dim)


def step(x, n, s, w, e, k, hu, hv):
    return x + k * (n + s + w + e - 4.0 * x) - hu * (e - w) - hv * (s - n)


def forecast_kernel(
    ngy, ngx,
    x_hbm, flow_hbm, cell_hbm, val_hbm, var_hbm,
    gram_ref, hilo_ref, mean_ref,
    xb, xr, yr, zr, fl, cf, cells, vals, varis, qs, fs, hu_rows, hd_rows, hl, hr, kb, fh, zc, rf,
    load_sem, halo_send, halo_recv, flow_send, flow_recv, gx_send, gx_recv,
):
    gy = lax.axis_index("gy")
    gx = lax.axis_index("gx")
    up, down = gy - 1, gy + 1
    has_up, has_down = gy > 0, gy < ngy - 1
    left, right = lax.rem(gx + ngx - 1, ngx), lax.rem(gx + 1, ngx)
    gx_partners = [(gy, lax.rem(gx + i, ngx)) for i in sorted(range(1, ngx), key=lambda i: -min(i, ngx - i))]

    row_loads = [pltpu.make_async_copy(x_hbm.at[:, r, :], xr.at[r + 1], load_sem.at[5 + r]) for r in (0, 1, 6, 7, 2, 3, 4, 5)]
    flow_load = pltpu.make_async_copy(flow_hbm, fl, load_sem.at[1])
    loads = [
        pltpu.make_async_copy(x_hbm, xb, load_sem.at[0]),
        pltpu.make_async_copy(cell_hbm, cells, load_sem.at[2]),
        pltpu.make_async_copy(val_hbm, vals, load_sem.at[3]),
        pltpu.make_async_copy(var_hbm, varis, load_sem.at[4]),
    ]
    flow_load.start()
    for copy in row_loads + loads:
        copy.start()
    barrier = pltpu.get_barrier_semaphore()

    def greet(partners):
        for partner in partners:
            pl.semaphore_signal(barrier, inc=1, device_id=partner, device_id_type=MESH)

    @pl.when(has_up)
    def _():
        greet([(up, gx), (up, left), (up, right)])

    @pl.when(has_down)
    def _():
        greet([(down, gx), (down, left), (down, right)])

    greet(gx_partners)

    lane = iota((8, CX), 1)
    sub = iota((8, CX), 0)
    edge = (lane <= 1) | (lane >= CX - 2)
    s0, s7 = sub == 0, sub == 7
    l0, l127 = lane == 0, lane == CX - 1
    quad = lane & 3
    q0, q1, q3 = quad == 0, quad == 1, quad == 3
    west_side = quad >= 2

    def remote(src, dst, index, target, send=halo_send, recv=halo_recv):
        return pltpu.make_async_remote_copy(
            src_ref=src, dst_ref=dst, send_sem=send.at[index], recv_sem=recv.at[index],
            device_id=target, device_id_type=MESH,
        )

    up_flow = [remote(fs.at[0], fh.at[0], 0, (up, gx), flow_send, flow_recv)]
    down_flow = [remote(fs.at[0], fh.at[1], 1, (down, gx), flow_send, flow_recv)]
    side_flow = [
        remote(fs.at[1], fh.at[2], 2, (gy, left), flow_send, flow_recv),
        remote(fs.at[1], fh.at[3], 3, (gy, right), flow_send, flow_recv),
    ]
    up_rows = [remote(xr.at[pl.ds(1, 2)], hd_rows, 0, (up, gx))]
    down_rows = [remote(xr.at[pl.ds(7, 2)], hu_rows, 1, (down, gx))]
    up_corners = [remote(qs, kb.at[0], 4, (up, left)), remote(qs, kb.at[1], 5, (up, right))]
    down_corners = [remote(qs, kb.at[2], 6, (down, left)), remote(qs, kb.at[3], 7, (down, right))]
    side_halos = [remote(qs, hr, 2, (gy, left)), remote(qs, hl, 3, (gy, right))]

    def start(up_copies, down_copies, side_copies=()):
        @pl.when(has_up)
        def _():
            for copy in up_copies:
                copy.start()

        @pl.when(has_down)
        def _():
            for copy in down_copies:
                copy.start()

        for copy in side_copies:
            copy.start()

    def received(up_copies, down_copies, side_copies=()):
        for copy in side_copies:
            copy.wait_recv()

        @pl.when(has_up)
        def _():
            for copy in down_copies:
                copy.wait_recv()

        @pl.when(has_down)
        def _():
            for copy in up_copies:
                copy.wait_recv()

    def sent(up_copies, down_copies, side_copies=()):
        for copy in side_copies:
            copy.wait_send()

        @pl.when(has_up)
        def _():
            for copy in up_copies:
                copy.wait_send()

        @pl.when(has_down)
        def _():
            for copy in down_copies:
                copy.wait_send()

    flow_load.wait()
    qc = jnp.where(edge, fl[0], 0.0)
    for i in range(1, 3):
        qc = qc + pltpu.roll(jnp.where(edge, fl[i], 0.0), 4 * i, 1)
    fs[1] = qc
    for i in range(3):
        fs[0, pl.ds(i, 1), :] = fl[i, 0:1, :]
        fs[0, pl.ds(3 + i, 1), :] = fl[i, 7:8, :]
    for copy in row_loads[:4]:
        copy.wait()

    @pl.when(has_up & has_down)
    def _():
        pl.semaphore_wait(barrier, ngx + 5)

    @pl.when(jnp.logical_not(has_up & has_down))
    def _():
        pl.semaphore_wait(barrier, ngx + 2)

    start(up_rows, down_rows)
    start(up_flow, down_flow, side_flow)
    for copy in row_loads[4:] + loads:
        copy.wait()

    def pack(half):
        def body(i, q):
            for j in range(8):
                m = i * 8 + j
                q = q + pltpu.roll(jnp.where(edge, xb[half * 32 + m], 0.0), lax.rem(CX - 4 * m, CX), 1)
            return q
        return lax.fori_loop(0, 4, body, jnp.zeros((8, CX), F32))

    qa, qb = pack(0), pack(1)
    qs[pl.ds(0, 8), :] = qa
    qs[pl.ds(8, 8), :] = qb
    start(up_corners, down_corners, side_halos)

    def weights(f0, f1, f2):
        hu, hv = 0.5 * f1, 0.5 * f2
        return 1.0 - 4.0 * f0, f0 + hv, f0 - hv, f0 + hu, f0 - hu

    own = weights(fl[0], fl[1], fl[2])
    a0, an, as_, aw, ae = own
    aw_in, ae_in = jnp.where(l0, 0.0, aw), jnp.where(l127, 0.0, ae)
    for i, v in enumerate((a0, an, as_, aw_in, ae_in)):
        cf[i] = v

    blank = jnp.zeros((M, CX), F32)
    xr[0] = blank
    xr[9] = blank
    yr[0] = blank
    yr[9] = blank

    def inner(source, target, shift):
        def body(r, carry):
            c = [jnp.broadcast_to(cf[i, pl.ds(r, 1), :], (8, CX)) for i in range(5)]
            for b in range(8):
                rows = pl.ds(8 * b, 8)
                x = source[r + 1, rows, :]
                target[r + shift, rows, :] = (
                    (c[0] * x + c[1] * source[r, rows, :]) + (c[2] * source[r + 2, rows, :] + c[3] * pltpu.roll(x, 1, 1))
                    + c[4] * pltpu.roll(x, CX - 1, 1)
                )
            return carry
        lax.fori_loop(0, CY, body, 0)

    inner(xr, yr, 1)
    inner(yr, zr, 0)

    def col(v, l):
        return jnp.broadcast_to(v[:, l:l + 1], (8, CX))

    c_edge = jnp.where(q0, col(aw, 0), jnp.where(q3, col(ae, CX - 1), 0.0))
    a0_edge = jnp.where(q0, col(a0, 0), col(a0, CX - 1))
    an_edge = jnp.where(s0, 0.0, jnp.where(q0, col(an, 0), col(an, CX - 1)))
    as_edge = jnp.where(s7, 0.0, jnp.where(q0, col(as_, 0), col(as_, CX - 1)))
    c_next = jnp.where(q1, col(aw, 1), col(ae, CX - 2))

    has_left, has_right = gx > 0, gx < ngx - 1

    def on(flag):
        return jnp.full((8, CX), jnp.where(flag, 1, 0), jnp.int32) > 0

    hmask = (s7 & on(has_up)) | (s0 & on(has_down))
    cmask = (west_side & on(has_left)) | ((quad <= 1) & on(has_right))

    received(up_flow, down_flow, side_flow)

    def flow_cols(i):
        west, east = col(fh[3], (4 * i - 1) % CX), col(fh[2], 4 * i)
        return jnp.where(cmask, jnp.where(west_side, west, east), 0.0)

    kc, uc, vc = flow_cols(0), 0.5 * flow_cols(1), 0.5 * flow_cols(2)

    def outer_row(tile, offset, flag):
        fields = [jnp.where(on(flag), jnp.broadcast_to(tile[offset + i:offset + i + 1, :], (8, CX)), 0.0) for i in range(3)]
        return weights(*fields)

    def line(v, r):
        return jnp.broadcast_to(v[r:r + 1, :], (8, CX))

    def outside(above):
        if above:
            t0, tn, ts, tw, te = outer_row(fh[1], 3, has_up)
            r, near, far, cross, toward = 0, line(an, 0), tn, ts, line(an, 1)
        else:
            t0, tn, ts, tw, te = outer_row(fh[0], 0, has_down)
            r, near, far, cross, toward = 7, line(as_, 7), ts, tn, line(as_, 6)
        west = near * jnp.where(l0, 0.0, tw) + line(aw_in, r) * pltpu.roll(near, 1, 1)
        east = near * jnp.where(l127, 0.0, te) + line(ae_in, r) * pltpu.roll(near, CX - 1, 1)
        corner = jnp.where(q0, col(near * tw, 0), jnp.where(q3, col(near * te, CX - 1), 0.0))
        return (near * (t0 + line(a0, r)), near * far, near * cross, west, east, toward * near), corner

    above, corner_above = outside(True)
    below, corner_below = outside(False)
    c_corner = jnp.where(s0, corner_above, jnp.where(s7, corner_below, 0.0))

    received(up_corners, down_corners, side_halos)
    west_cell = q3
    for half in range(2):
        q = (qa, qb)[half]
        rows = pl.ds(8 * half, 8)
        ring = jnp.where(cmask, jnp.where(west_side, hl[rows, :], hr[rows, :]), 0.0)
        corner_w = jnp.where(s7, kb[3, rows, :], kb[1, rows, :])
        corner_e = jnp.where(s7, kb[2, rows, :], kb[0, rows, :])
        corner = jnp.where(hmask & cmask, jnp.where(west_side, corner_w, corner_e), 0.0)
        n = pltpu.roll(jnp.where(s7, corner, ring), 1, 0)
        s = pltpu.roll(jnp.where(s0, corner, ring), 7, 0)
        ring_w, ring_e = pltpu.roll(ring, 1, 1), pltpu.roll(ring, CX - 1, 1)
        w = jnp.where(west_cell, ring_w, pltpu.roll(q, 1, 1))
        e = jnp.where(west_cell, pltpu.roll(q, CX - 1, 1), ring_e)
        ring1 = step(ring, n, s, w, e, kc, uc, vc)
        x1 = jnp.where(q0, ring_w, ring_e)
        y1 = jnp.where(q0, pltpu.roll(ring1, 1, 1), pltpu.roll(ring1, CX - 1, 1))
        outer = jnp.where(s0, pltpu.roll(corner, 1, 0), pltpu.roll(corner, 7, 0))
        outer = jnp.where(q0, pltpu.roll(outer, 1, 1), pltpu.roll(outer, CX - 1, 1))
        d = c_edge * x1
        at_edge = a0_edge * d + an_edge * pltpu.roll(d, 1, 0) + as_edge * pltpu.roll(d, 7, 0) + c_edge * y1 + c_corner * outer
        inside = c_next * jnp.where(q1, pltpu.roll(d, 1, 1), pltpu.roll(d, CX - 1, 1))
        zc[half] = jnp.where(q0 | q3, at_edge, inside)

    received(up_rows, down_rows)

    def add_rows(flag, c, near_row, far_row, r, r_in):
        @pl.when(flag)
        def _():
            for b in range(8):
                rows = pl.ds(8 * b, 8)
                p = near_row[rows, :]
                zr[r, rows, :] = zr[r, rows, :] + (
                    (c[0] * p + c[1] * far_row[rows, :]) + (c[2] * xr[r + 1, rows, :] + c[3] * pltpu.roll(p, 1, 1))
                    + c[4] * pltpu.roll(p, CX - 1, 1)
                )
                zr[r_in, rows, :] = zr[r_in, rows, :] + c[5] * p

    add_rows(has_up, above, hu_rows.at[1], hu_rows.at[0], 0, 1)
    add_rows(has_down, below, hd_rows.at[0], hd_rows.at[1], 7, 6)

    def add_columns(r, carry):
        lines = [jnp.broadcast_to(zc[half, pl.ds(r, 1), :], (8, CX)) for half in range(2)]
        for b in range(8):
            rows = pl.ds(8 * b, 8)
            spread = pltpu.roll(lines[b // 4], 32 * (b % 4), 1, stride=4, stride_axis=0)
            zr[r, rows, :] = zr[r, rows, :] + jnp.where(edge, spread, 0.0)
        return carry

    lax.fori_loop(0, CY, add_columns, 0)

    lane64 = iota((M, CX), 1)
    diag64 = lane64 == iota((M, CX), 0)
    ones = jnp.zeros((1, CX), F32)
    picked = []
    for j in range(4):
        cell = cells[0, 0, j]
        row, place = lax.shift_right_logical(cell, 7), cell & (CX - 1)
        column = jnp.sum(jnp.where(lane64 == place, zr[row], 0.0), axis=1, keepdims=True)
        column = jnp.broadcast_to(column, (M, CX))
        average = jnp.sum(column, axis=0, keepdims=True) * (1.0 / M)
        factor = lax.rsqrt(ones + varis[0, 0, j])
        values = jnp.sum(jnp.where(diag64, column, 0.0), axis=0, keepdims=True)
        values = jnp.where(iota((1, CX), 1) < M - 1, values, ones + vals[0, 0, j])
        picked.append(jnp.where(iota((1, CX), 1) < M, (values - average) * factor, 0.0))
    rf[gx] = jnp.concatenate(
        [picked[0] + pltpu.roll(picked[2], M, 1), picked[1] + pltpu.roll(picked[3], M, 1)], axis=0
    )

    gx_copies = [
        pltpu.make_async_remote_copy(
            src_ref=rf.at[gx], dst_ref=rf.at[gx], send_sem=gx_send, recv_sem=gx_recv,
            device_id=partner, device_id_type=MESH,
        )
        for partner in gx_partners
    ]
    for copy in gx_copies:
        copy.start()

    for r in range(CY):
        field = zr[r]
        mean = jnp.sum(field, axis=0, keepdims=True) * (1.0 / M)
        mean_ref[pl.ds(r, 1), :] = mean
        field = field - mean
        high = field.astype(BF16)
        hilo_ref[pl.ds(0, M), pl.ds(r * CX, CX)] = high
        hilo_ref[pl.ds(M, M), pl.ds(r * CX, CX)] = (field - high.astype(F32)).astype(BF16)

    wait_all(rf, ngx - 1, gx_recv)
    gathered = jnp.concatenate([rf[i] for i in range(ngx)], axis=0)
    lane32 = iota((2 * ngx, CX), 1)
    rows = jnp.concatenate(
        [jnp.where(lane32 < M, gathered, 0.0), jnp.where(lane32 < M, pltpu.roll(gathered, M, 1), 0.0)], axis=0
    )
    gram = jnp.dot(rows.T, rows, precision=lax.Precision.HIGHEST, preferred_element_type=F32)
    high, low = gram[0:32], pltpu.roll(gram[32:64], CX - 32, 1)
    across, along = iota((32, CX), 1), iota((32, CX), 0)
    square = jnp.where((across < 32) & (across > along), low, high)
    gram_ref[pl.ds(0, 16), :] = square[0:16] + pltpu.roll(square[16:32], M, 1)
    diagonal = jnp.sum(jnp.where(across == along, low, 0.0), axis=0, keepdims=True)
    gram_ref[pl.ds(16, 8), :] = jnp.where(iota((8, CX), 0) == 0, diagonal, 0.0)

    sent(up_rows, down_rows)
    sent(up_flow, down_flow, side_flow)
    sent(up_corners, down_corners, side_halos)
    wait_all(rf, ngx - 1, gx_send)


def wait_all(buffer, count, sem):
    piece = buffer.at[pl.ds(0, count)]
    pltpu.make_async_copy(piece, piece, sem).wait()


def sum_kernel(ngy, part_ref, gram_ref, rz, rx, z_send, z_recv, x_send, x_recv):
    gy = lax.axis_index("gy")
    gx = lax.axis_index("gx")
    nz = ngy // NX4
    zpos = gy // NX4
    xpos = lax.rem(gy, NX4)
    z_partners = [(lax.rem(gy + NX4 * i, ngy), gx) for i in range(1, nz)]
    x_partners = [(zpos * NX4 + lax.rem(xpos + i, NX4), gx) for i in (2, 1, 3)]
    barrier = pltpu.get_barrier_semaphore()
    for partner in z_partners + x_partners:
        pl.semaphore_signal(barrier, inc=1, device_id=partner, device_id_type=MESH)
    rz[zpos] = part_ref[...]
    pl.semaphore_wait(barrier, nz + NX4 - 2)

    def wait_rows(buffer, count, sem):
        piece = buffer.at[pl.ds(0, count), pl.ds(0, 17)]
        pltpu.make_async_copy(piece, piece, sem).wait()

    def spread(buffer, slot, partners, send, recv):
        for partner in partners:
            pltpu.make_async_remote_copy(
                src_ref=buffer.at[slot, pl.ds(0, 17)], dst_ref=buffer.at[slot, pl.ds(0, 17)], send_sem=send, recv_sem=recv,
                device_id=partner, device_id_type=MESH,
            ).start()

    spread(rz, zpos, z_partners, z_send, z_recv)
    wait_rows(rz, nz - 1, z_recv)
    part = rz[0]
    for i in range(1, nz):
        part = part + rz[i]
    rx[xpos] = part
    spread(rx, xpos, x_partners, x_send, x_recv)
    wait_rows(rx, NX4 - 1, x_recv)
    gram_ref[...] = (rx[0] + rx[1]) + (rx[2] + rx[3])
    wait_rows(rz, nz - 1, z_send)
    wait_rows(rx, NX4 - 1, x_send)


def analysis_kernel(gram_ref, hilo_ref, mean_ref, out_hbm, rows_out, out_sem):
    lane = iota((8, CX), 1)
    sub = iota((8, CX), 0)
    packed = gram_ref[pl.ds(0, 16), :]
    square = jnp.concatenate([packed, pltpu.roll(packed, M, 1)], axis=0)
    square = jnp.where(iota((32, CX), 1) < M, square, 0.0)
    turned = jnp.concatenate([square, jnp.zeros((CX - 32, CX), F32)], axis=0).T
    across, along = iota((32, CX), 1), iota((32, CX), 0)
    top = jnp.where((across < 32) & (across > along), turned[0:32], square)
    corner = jnp.where(across > along, square, jnp.where(across == along, gram_ref[pl.ds(16, 1), :], turned[0:32]))
    corner = pltpu.roll(jnp.where(across < 32, corner, 0.0), 32, 1)
    bottom = jnp.where(across < 32, turned[32:64], corner)
    blocks = [top[8 * i:8 * i + 8] for i in range(4)] + [bottom[8 * i:8 * i + 8] for i in range(4)]
    blocks = [jnp.where(lane < M - 1, b, 0.0) for b in blocks]
    row_sums = [jnp.sum(b, axis=1, keepdims=True) for b in blocks]
    eyes = [lane == sub + 8 * i for i in range(8)]
    diagonals = [jnp.where(e, b, 0.0) for e, b in zip(eyes, blocks)]
    last = sub == 7
    target_row = blocks[7][7:8] + jnp.where(lane[0:1] == M - 1, -row_sums[7][7:8], 0.0)
    blocks[7] = jnp.where(last, 0.0, blocks[7])
    row_sums[7] = jnp.where(last[:, 0:1], 0.0, row_sums[7])
    col_sum = functools.reduce(jnp.add, blocks)
    col_sum = jnp.sum(col_sum, axis=0, keepdims=True)
    all_sum = jnp.sum(functools.reduce(jnp.add, row_sums), axis=0, keepdims=True)
    blocks = [jnp.where(lane == M - 1, -r, b) for b, r in zip(blocks, row_sums)]
    blocks[7] = jnp.where(last, jnp.where(lane == M - 1, all_sum, -col_sum), blocks[7])
    scale_row = jnp.sum(functools.reduce(jnp.add, diagonals), axis=0, keepdims=True)
    scale_row = lax.rsqrt((M - 1.0) + jnp.where(lane[0:1] == M - 1, all_sum, scale_row))
    scale_col = [jnp.sum(d, axis=1, keepdims=True) for d in diagonals]
    scale_col[7] = jnp.where(last[:, 0:1], all_sum, scale_col[7])
    scale_col = [lax.rsqrt((M - 1.0) + c) for c in scale_col]
    blocks = [jnp.where(e, b + (M - 1.0), b) for e, b in zip(eyes, blocks)]
    a = [
        jnp.where(lane == sub + (M + 8 * i), scale_col[i], jnp.where(lane < M, blocks[i] * scale_col[i] * scale_row, 0.0))
        for i in range(8)
    ]

    lower = [None] * 8
    nothing = 0.0 * packed[0:8]
    for p in range(16):
        b, o = p // 2, 4 * (p % 2)
        cols = {
            (t, i): jnp.broadcast_to(a[i][:, 4 * p + t:4 * p + t + 1], (8, CX)) for t in range(4) for i in range(b, 8)
        }
        cols = {key: v + nothing if key[1] == b else v for key, v in cols.items()}
        d = {
            (s, t): jnp.broadcast_to(cols[t, b][o + s:o + s + 1, :], (8, CX)) for s in range(4) for t in range(s + 1)
        }
        r = [jnp.broadcast_to(a[b][o + s:o + s + 1, :], (8, CX)) for s in range(4)]

        det = d[0, 0] * d[1, 1] - d[1, 0] * d[1, 0]
        inv = 1.0 / det
        i00, i10, i11 = d[1, 1] * inv, -d[1, 0] * inv, d[0, 0] * inv
        e00 = i00 * d[2, 0] + i10 * d[2, 1]
        e10 = i10 * d[2, 0] + i11 * d[2, 1]
        e01 = i00 * d[3, 0] + i10 * d[3, 1]
        e11 = i10 * d[3, 0] + i11 * d[3, 1]
        c00 = d[2, 2] - (d[2, 0] * e00 + d[2, 1] * e10)
        c10 = d[3, 2] - (d[3, 0] * e00 + d[3, 1] * e10)
        c11 = d[3, 3] - (d[3, 0] * e01 + d[3, 1] * e11)
        r2 = r[2] - (e00 * r[0] + e10 * r[1])
        r3 = r[3] - (e01 * r[0] + e11 * r[1])
        det2 = c00 * c11 - c10 * c10
        if p < 15:
            u0 = i00 * r[0] + i10 * r[1]
            u1 = i10 * r[0] + i11 * r[1]
            inv2 = 1.0 / det2
            z2 = (c11 * r2 - c10 * r3) * inv2
            z3 = (c00 * r3 - c10 * r2) * inv2
            z0 = u0 - (e00 * z2 + e01 * z3)
            z1 = u1 - (e10 * z2 + e11 * z3)
            z = (z0, z1, z2, z3)
            for i in range(b if o == 0 else b + 1, 8):
                update = (cols[0, i] * z[0] + cols[1, i] * z[1]) + (cols[2, i] * z[2] + cols[3, i] * z[3])
                new = a[i] - update
                a[i] = jnp.where(sub >= 4, new, a[i]) if i == b else new
        n0 = r[0] * lax.rsqrt(d[0, 0])
        n1 = (d[0, 0] * r[1] - d[1, 0] * r[0]) * lax.rsqrt(d[0, 0] * det)
        n2 = r2 * lax.rsqrt(c00)
        n3 = (c00 * r3 - c10 * r2) * lax.rsqrt(c00 * det2)
        rows = jnp.where(sub == o, n0, jnp.where(sub == o + 1, n1, jnp.where(sub == o + 2, n2, n3)))
        lower[b] = rows if o == 0 else jnp.where(sub >= 4, rows, lower[b])
    lower = [pltpu.roll(jnp.where(lane >= M, v, 0.0), M, 1) for v in lower]
    heads = [jnp.sum(v * target_row, axis=1, keepdims=True) for v in lower]
    weight = jnp.sum(functools.reduce(jnp.add, [v * h for v, h in zip(lower, heads)]), axis=0, keepdims=True)
    root = math.sqrt(M - 1.0)
    mix = jnp.concatenate([root * v + weight for v in lower], axis=0)
    high = mix.astype(BF16).astype(F32)
    low = mix - high
    pair = jnp.where(iota((M, CX), 1) < M, high, pltpu.roll(high, M, 1)).astype(BF16)
    low_pair = jnp.where(iota((M, CX), 1) < M, low, pltpu.roll(low, M, 1)).astype(BF16)
    left = jnp.concatenate([pair, low_pair], axis=1)
    for r in range(0, CY, 2):
        cols = pl.ds(r * CX, 2 * CX)
        block = hilo_ref[:, cols]
        right = jnp.concatenate([block, block], axis=0)
        res = jnp.dot(left, right, preferred_element_type=F32)
        for half in range(2):
            rows_out[r + half] = res[:, half * CX:(half + 1) * CX] + mean_ref[r + half:r + half + 1, :]
            pltpu.make_async_copy(rows_out.at[r + half], out_hbm.at[:, r + half, :], out_sem.at[r + half]).start()
    for r in range(CY):
        pltpu.make_async_copy(rows_out.at[r], out_hbm.at[:, r, :], out_sem.at[r]).wait()


def near(array):
    return pltpu.with_memory_space_constraint(array, pltpu.VMEM)


def body(ngy, ngx, ensemble, flow, obs_cell, obs_value, obs_var):
    vmem = pl.BlockSpec(memory_space=pltpu.VMEM)
    hbm = pl.BlockSpec(memory_space=pl.ANY)
    dma = pltpu.SemaphoreType.DMA
    part, hilo, mean = pl.pallas_call(
        functools.partial(forecast_kernel, ngy, ngx),
        out_shape=(
            pltpu.VMEM((24, CX), F32),
            pltpu.VMEM((2 * M, CY * CX), BF16),
            pltpu.VMEM((CY, CX), F32),
        ),
        in_specs=[hbm] * 5,
        out_specs=(vmem,) * 3,
        scratch_shapes=[
            pltpu.VMEM((M, CY, CX), F32),
            pltpu.VMEM((CY + 2, M, CX), F32),
            pltpu.VMEM((CY + 2, M, CX), F32),
            pltpu.VMEM((CY, M, CX), F32),
            pltpu.VMEM((3, CY, CX), F32),
            pltpu.VMEM((5, CY, CX), F32),
            pltpu.SMEM((1, 1, 4), jnp.int32),
            pltpu.SMEM((1, 1, 4), F32),
            pltpu.SMEM((1, 1, 4), F32),
            pltpu.VMEM((16, CX), F32),
            pltpu.VMEM((2, 8, CX), F32),
            pltpu.VMEM((2, M, CX), F32),
            pltpu.VMEM((2, M, CX), F32),
            pltpu.VMEM((16, CX), F32),
            pltpu.VMEM((16, CX), F32),
            pltpu.VMEM((4, 16, CX), F32),
            pltpu.VMEM((4, 8, CX), F32),
            pltpu.VMEM((2, 8, CX), F32),
            pltpu.VMEM((ngx, 2, CX), F32),
            dma((13,)), dma((8,)), dma((8,)), dma((4,)), dma((4,)), dma, dma,
        ],
        compiler_params=pltpu.CompilerParams(collective_id=0, has_side_effects=True),
        name="forecast",
    )(ensemble, flow, obs_cell, obs_value, obs_var)
    gram = pl.pallas_call(
        functools.partial(sum_kernel, ngy),
        out_shape=pltpu.VMEM((24, CX), F32),
        in_specs=[vmem],
        out_specs=vmem,
        scratch_shapes=[
            pltpu.VMEM((ngy // NX4, 24, CX), F32),
            pltpu.VMEM((NX4, 24, CX), F32),
            dma, dma, dma, dma,
        ],
        compiler_params=pltpu.CompilerParams(collective_id=1, has_side_effects=True),
        name="sums",
    )(near(part))
    return pl.pallas_call(
        analysis_kernel,
        out_shape=jax.ShapeDtypeStruct((M, CY, CX), F32),
        in_specs=[vmem] * 3,
        out_specs=hbm,
        scratch_shapes=[pltpu.VMEM((CY, M, CX), F32), dma((CY,))],
        name="analysis",
    )(near(gram), near(hilo), near(mean))


def solution(mesh):
    tile = P("gy", "gx", None)
    return jax.shard_map(
        functools.partial(body, mesh.shape["gy"], mesh.shape["gx"]),
        mesh=mesh,
        in_specs=(P(None, "gy", "gx"), P(None, "gy", "gx"), tile, tile, tile),
        out_specs=P(None, "gy", "gx"),
        check_vma=False,
    )
```

```python
import functools
import math

import jax
import jax.numpy as jnp
from jax import lax
from jax.experimental import pallas as pl
from jax.experimental.pallas import tpu as pltpu
from jax.sharding import PartitionSpec as P

MESH = pl.DeviceIdType.MESH
M = 64
CY = 8
CX = 128
F32 = jnp.float32
BF16 = jnp.bfloat16
NX4 = 4


def iota(shape, dim):
    return lax.broadcasted_iota(jnp.int32, shape, dim)


def step(x, n, s, w, e, k, hu, hv):
    return x + k * (n + s + w + e - 4.0 * x) - hu * (e - w) - hv * (s - n)


def forecast_kernel(
    ngy, ngx,
    x_hbm, flow_hbm, cell_hbm, val_hbm, var_hbm,
    gram_ref, hilo_ref, mean_ref,
    xb, xr, yr, zr, fl, cf, cells, obs, qs, fs, ct, h_rows, h_sides, h_corners, fh, zc, rf,
    load_sem, halo_send, halo_recv, gx_send, gx_recv,
):
    gy = lax.axis_index("gy")
    gx = lax.axis_index("gx")
    up, down = gy - 1, gy + 1
    has_up, has_down = gy > 0, gy < ngy - 1
    left, right = lax.rem(gx + ngx - 1, ngx), lax.rem(gx + 1, ngx)
    gx_partners = [(gy, lax.rem(gx + i, ngx)) for i in sorted(range(1, ngx), key=lambda i: -min(i, ngx - i))]

    def load(src, dst, index):
        pltpu.make_async_copy(src, dst, load_sem.at[index]).start()

    def loaded(piece, index):
        pltpu.make_async_copy(piece, piece, load_sem.at[index]).wait()

    load(flow_hbm, fl, 0)
    for r in (0, 7, 1, 6):
        load(x_hbm.at[:, r, :], xr.at[r + 1], 1)
    load(x_hbm, xb, 2)
    for r in (2, 3, 4, 5):
        load(x_hbm.at[:, r, :], xr.at[r + 1], 3)
    load(cell_hbm, cells, 4)
    load(val_hbm, obs.at[0], 5)
    load(var_hbm, obs.at[1], 5)
    barrier = pltpu.get_barrier_semaphore()

    def greet(partners):
        for partner in partners:
            pl.semaphore_signal(barrier, inc=1, device_id=partner, device_id_type=MESH)

    @pl.when(has_up)
    def _():
        greet([(up, gx), (up, left), (up, right)])

    @pl.when(has_down)
    def _():
        greet([(down, gx), (down, left), (down, right)])

    greet(gx_partners)

    lane = iota((8, CX), 1)
    sub = iota((8, CX), 0)
    edge = (lane <= 1) | (lane >= CX - 2)
    s0, s7 = sub == 0, sub == 7
    l0, l127 = lane == 0, lane == CX - 1
    quad = lane & 3
    q0, q1, q3 = quad == 0, quad == 1, quad == 3
    west_side = quad >= 2

    def remote(src, dst, index, target):
        return pltpu.make_async_remote_copy(
            src_ref=src, dst_ref=dst, send_sem=halo_send.at[index], recv_sem=halo_recv.at[index],
            device_id=target, device_id_type=MESH,
        )

    def start(index, to_up, to_down, to_left=None, to_right=None):
        @pl.when(has_up)
        def _():
            for src, dst, target in to_up:
                remote(src, dst, index, (up, target)).start()

        @pl.when(has_down)
        def _():
            for src, dst, target in to_down:
                remote(src, dst, index, (down, target)).start()

        if to_left:
            remote(*to_left, index, (gy, left)).start()
            remote(*to_right, index, (gy, right)).start()

    both = has_up & has_down

    def settle(sem, buffer, most, least):
        def wait(count):
            piece = buffer.at[pl.ds(0, count)]
            pltpu.make_async_copy(piece, piece, sem).wait()

        if most == least:
            wait(most)
        else:
            pl.when(both)(lambda: wait(most))
            pl.when(jnp.logical_not(both))(lambda: wait(least))

    groups = [(fh, 4, 3), (h_sides, 2, 2), (h_rows, 4, 2), (h_corners, 4, 2)]

    def received(index):
        settle(halo_recv.at[index], *groups[index])

    loaded(fl, 0)
    qc = jnp.where(edge, fl[0], 0.0)
    for i in range(1, 3):
        qc = qc + pltpu.roll(jnp.where(edge, fl[i], 0.0), 4 * i, 1)
    fs[1] = qc
    for i in range(3):
        fs[0, pl.ds(i, 1), :] = fl[i, 0:1, :]
        fs[0, pl.ds(3 + i, 1), :] = fl[i, 7:8, :]
    loaded(xr.at[pl.ds(0, 4)], 1)

    @pl.when(both)
    def _():
        pl.semaphore_wait(barrier, ngx + 5)

    @pl.when(jnp.logical_not(both))
    def _():
        pl.semaphore_wait(barrier, ngx + 2)

    start(2, [(xr.at[pl.ds(1, 2)], h_rows.at[pl.ds(2, 2)], gx)], [(xr.at[pl.ds(7, 2)], h_rows.at[pl.ds(0, 2)], gx)])
    start(0, [(fs.at[0], fh.at[1], gx)], [(fs.at[0], fh.at[0], gx)], (fs.at[1], fh.at[2]), (fs.at[1], fh.at[3]))
    ends = l0 | l127
    tile = jnp.zeros((8, CX), F32)
    for b in range(8):
        rows = pl.ds(8 * b, 8)
        tile = tile + pltpu.roll(jnp.where(ends, xr[1, rows, :], 0.0), 4 * b, 1)
        tile = tile + pltpu.roll(jnp.where(ends, xr[8, rows, :], 0.0), 4 * b + 2, 1)
    ct[...] = tile
    start(
        3,
        [(ct, h_corners.at[3], left), (ct, h_corners.at[2], right)],
        [(ct, h_corners.at[1], left), (ct, h_corners.at[0], right)],
    )
    loaded(xb, 2)

    def pack(half):
        def body(i, q):
            for j in range(8):
                m = i * 8 + j
                q = q + pltpu.roll(jnp.where(edge, xb[half * 32 + m], 0.0), lax.rem(CX - 4 * m, CX), 1)
            return q
        return lax.fori_loop(0, 4, body, jnp.zeros((8, CX), F32))

    qa, qb = pack(0), pack(1)
    qs[pl.ds(0, 8), :] = qa
    qs[pl.ds(8, 8), :] = qb
    start(1, [], [], (qs, h_sides.at[0]), (qs, h_sides.at[1]))
    loaded(xr.at[pl.ds(0, 4)], 3)
    loaded(cells, 4)
    loaded(obs, 5)

    def weights(f0, f1, f2):
        hu, hv = 0.5 * f1, 0.5 * f2
        return 1.0 - 4.0 * f0, f0 + hv, f0 - hv, f0 + hu, f0 - hu

    own = weights(fl[0], fl[1], fl[2])
    a0, an, as_, aw, ae = own
    aw_in, ae_in = jnp.where(l0, 0.0, aw), jnp.where(l127, 0.0, ae)
    for i, v in enumerate((a0, an, as_, aw_in, ae_in)):
        cf[i] = v

    blank = jnp.zeros((M, CX), F32)
    xr[0] = blank
    xr[9] = blank
    yr[0] = blank
    yr[9] = blank

    def inner(source, target, shift):
        def body(r, carry):
            c = [jnp.broadcast_to(cf[i, pl.ds(r, 1), :], (8, CX)) for i in range(5)]
            for b in range(8):
                rows = pl.ds(8 * b, 8)
                x = source[r + 1, rows, :]
                target[r + shift, rows, :] = (
                    (c[0] * x + c[1] * source[r, rows, :]) + (c[2] * source[r + 2, rows, :] + c[3] * pltpu.roll(x, 1, 1))
                    + c[4] * pltpu.roll(x, CX - 1, 1)
                )
            return carry
        lax.fori_loop(0, CY, body, 0)

    inner(xr, yr, 1)
    inner(yr, zr, 0)

    def col(v, l):
        return jnp.broadcast_to(v[:, l:l + 1], (8, CX))

    c_edge = jnp.where(q0, col(aw, 0), jnp.where(q3, col(ae, CX - 1), 0.0))
    a0_edge = jnp.where(q0, col(a0, 0), col(a0, CX - 1))
    an_edge = jnp.where(s0, 0.0, jnp.where(q0, col(an, 0), col(an, CX - 1)))
    as_edge = jnp.where(s7, 0.0, jnp.where(q0, col(as_, 0), col(as_, CX - 1)))
    c_next = jnp.where(q1, col(aw, 1), col(ae, CX - 2))

    has_left, has_right = gx > 0, gx < ngx - 1

    def on(flag):
        return jnp.full((8, CX), jnp.where(flag, 1, 0), jnp.int32) > 0

    cmask = (west_side & on(has_left)) | ((quad <= 1) & on(has_right))

    received(0)

    def flow_cols(i):
        west, east = col(fh[3], (4 * i - 1) % CX), col(fh[2], 4 * i)
        return jnp.where(cmask, jnp.where(west_side, west, east), 0.0)

    kc, uc, vc = flow_cols(0), 0.5 * flow_cols(1), 0.5 * flow_cols(2)

    def outer_row(tile, offset, flag):
        fields = [jnp.where(on(flag), jnp.broadcast_to(tile[offset + i:offset + i + 1, :], (8, CX)), 0.0) for i in range(3)]
        return weights(*fields)

    def line(v, r):
        return jnp.broadcast_to(v[r:r + 1, :], (8, CX))

    ends_in = (l0 & on(has_left)) | (l127 & on(has_right))

    def beside(i):
        return jnp.where(l0, pltpu.roll(fh[3], (1 - 4 * i) % CX, 1), pltpu.roll(fh[2], CX - 1 - 4 * i, 1))

    k_side, v_side = beside(0), 0.5 * beside(2)

    def outside(above):
        if above:
            t0, tn, ts, tw, te = outer_row(fh[0], 3, has_up)
            r, near, far, cross, toward = 0, line(an, 0), tn, ts, line(an, 1)
            side = line(k_side + v_side, 0)
        else:
            t0, tn, ts, tw, te = outer_row(fh[1], 0, has_down)
            r, near, far, cross, toward = 7, line(as_, 7), ts, tn, line(as_, 6)
            side = line(k_side - v_side, 7)
        west = near * jnp.where(l0, 0.0, tw) + line(aw_in, r) * pltpu.roll(near, 1, 1)
        east = near * jnp.where(l127, 0.0, te) + line(ae_in, r) * pltpu.roll(near, CX - 1, 1)
        corner = jnp.where(l0, near * tw + line(aw, r) * side, near * te + line(ae, r) * side)
        corner = jnp.where(ends_in, corner, 0.0)
        return near * (t0 + line(a0, r)), near * far, near * cross, west, east, toward * near, corner

    above = outside(True)
    below = outside(False)

    received(1)
    west_cell = q3
    for half in range(2):
        q = (qa, qb)[half]
        rows = pl.ds(8 * half, 8)
        ring = jnp.where(cmask, jnp.where(west_side, h_sides[1, rows, :], h_sides[0, rows, :]), 0.0)
        n = pltpu.roll(jnp.where(s7, 0.0, ring), 1, 0)
        s = pltpu.roll(jnp.where(s0, 0.0, ring), 7, 0)
        ring_w, ring_e = pltpu.roll(ring, 1, 1), pltpu.roll(ring, CX - 1, 1)
        w = jnp.where(west_cell, ring_w, pltpu.roll(q, 1, 1))
        e = jnp.where(west_cell, pltpu.roll(q, CX - 1, 1), ring_e)
        ring1 = step(ring, n, s, w, e, kc, uc, vc)
        x1 = jnp.where(q0, ring_w, ring_e)
        y1 = jnp.where(q0, pltpu.roll(ring1, 1, 1), pltpu.roll(ring1, CX - 1, 1))
        d = c_edge * x1
        at_edge = a0_edge * d + an_edge * pltpu.roll(d, 1, 0) + as_edge * pltpu.roll(d, 7, 0) + c_edge * y1
        inside = c_next * jnp.where(q1, pltpu.roll(d, 1, 1), pltpu.roll(d, CX - 1, 1))
        zc[half] = jnp.where(q0 | q3, at_edge, inside)

    received(2)
    received(3)

    def add_rows(flag, c, near_row, far_row, r, r_in, corners, first):
        @pl.when(flag)
        def _():
            merged = corners()
            for b in range(8):
                rows = pl.ds(8 * b, 8)
                p = h_rows[near_row, rows, :]
                zr[r, rows, :] = zr[r, rows, :] + (
                    (c[0] * p + c[1] * h_rows[far_row, rows, :]) + (c[2] * xr[r + 1, rows, :] + c[3] * pltpu.roll(p, 1, 1))
                    + (c[4] * pltpu.roll(p, CX - 1, 1) + c[6] * pltpu.roll(merged, (first - 4 * b) % CX, 1))
                )
                zr[r_in, rows, :] = zr[r_in, rows, :] + c[5] * p

    add_rows(has_up, above, 1, 0, 0, 1, lambda: jnp.where(q1, h_corners[0], pltpu.roll(h_corners[1], CX - 2, 1)), CX - 1)
    add_rows(has_down, below, 2, 3, 7, 6, lambda: jnp.where(q3, h_corners[2], pltpu.roll(h_corners[3], CX - 2, 1)), 1)

    def add_columns(r, carry):
        lines = [jnp.broadcast_to(zc[half, pl.ds(r, 1), :], (8, CX)) for half in range(2)]
        for b in range(8):
            rows = pl.ds(8 * b, 8)
            spread = pltpu.roll(lines[b // 4], 32 * (b % 4), 1, stride=4, stride_axis=0)
            zr[r, rows, :] = zr[r, rows, :] + jnp.where(edge, spread, 0.0)
        return carry

    lax.fori_loop(0, CY, add_columns, 0)

    lane64 = iota((M, CX), 1)
    diag64 = lane64 == iota((M, CX), 0)
    ones = jnp.zeros((1, CX), F32)
    picked = []
    for j in range(4):
        cell = cells[0, 0, j]
        row, place = lax.shift_right_logical(cell, 7), cell & (CX - 1)
        column = jnp.sum(jnp.where(lane64 == place, zr[row], 0.0), axis=1, keepdims=True)
        column = jnp.broadcast_to(column, (M, CX))
        average = jnp.sum(column, axis=0, keepdims=True) * (1.0 / M)
        factor = lax.rsqrt(ones + obs[1, 0, 0, j])
        values = jnp.sum(jnp.where(diag64, column, 0.0), axis=0, keepdims=True)
        values = jnp.where(iota((1, CX), 1) < M - 1, values, ones + obs[0, 0, 0, j])
        picked.append(jnp.where(iota((1, CX), 1) < M, (values - average) * factor, 0.0))
    rf[gx] = jnp.concatenate(
        [picked[0] + pltpu.roll(picked[2], M, 1), picked[1] + pltpu.roll(picked[3], M, 1)], axis=0
    )

    gx_copies = [
        pltpu.make_async_remote_copy(
            src_ref=rf.at[gx], dst_ref=rf.at[gx], send_sem=gx_send, recv_sem=gx_recv,
            device_id=partner, device_id_type=MESH,
        )
        for partner in gx_partners
    ]
    for copy in gx_copies:
        copy.start()

    for r in range(CY):
        field = zr[r]
        mean = jnp.sum(field, axis=0, keepdims=True) * (1.0 / M)
        mean_ref[pl.ds(r, 1), :] = mean
        field = field - mean
        high = field.astype(BF16)
        hilo_ref[pl.ds(0, M), pl.ds(r * CX, CX)] = high
        hilo_ref[pl.ds(M, M), pl.ds(r * CX, CX)] = (field - high.astype(F32)).astype(BF16)

    wait_all(rf, ngx - 1, gx_recv)
    gathered = jnp.concatenate([rf[i] for i in range(ngx)], axis=0)
    lane32 = iota((2 * ngx, CX), 1)
    rows = jnp.concatenate(
        [jnp.where(lane32 < M, gathered, 0.0), jnp.where(lane32 < M, pltpu.roll(gathered, M, 1), 0.0)], axis=0
    )
    gram = jnp.dot(rows.T, rows, precision=lax.Precision.HIGHEST, preferred_element_type=F32)
    high, low = gram[0:32], pltpu.roll(gram[32:64], CX - 32, 1)
    across, along = iota((32, CX), 1), iota((32, CX), 0)
    square = jnp.where((across < 32) & (across > along), low, high)
    gram_ref[pl.ds(0, 16), :] = square[0:16] + pltpu.roll(square[16:32], M, 1)
    diagonal = jnp.sum(jnp.where(across == along, low, 0.0), axis=0, keepdims=True)
    gram_ref[pl.ds(16, 8), :] = jnp.where(iota((8, CX), 0) == 0, diagonal, 0.0)

    for index, group in enumerate(groups):
        settle(halo_send.at[index], *group)
    wait_all(rf, ngx - 1, gx_send)


def wait_all(buffer, count, sem):
    piece = buffer.at[pl.ds(0, count)]
    pltpu.make_async_copy(piece, piece, sem).wait()


def sum_kernel(ngy, part_ref, gram_ref, rz, rx, z_send, z_recv, x_send, x_recv):
    gy = lax.axis_index("gy")
    gx = lax.axis_index("gx")
    nz = ngy // NX4
    zpos = gy // NX4
    xpos = lax.rem(gy, NX4)
    z_partners = [(lax.rem(gy + NX4 * i, ngy), gx) for i in range(1, nz)]
    x_partners = [(zpos * NX4 + lax.rem(xpos + i, NX4), gx) for i in (2, 1, 3)]
    barrier = pltpu.get_barrier_semaphore()
    for partner in z_partners + x_partners:
        pl.semaphore_signal(barrier, inc=1, device_id=partner, device_id_type=MESH)
    rz[zpos] = part_ref[...]
    pl.semaphore_wait(barrier, nz + NX4 - 2)

    def wait_rows(buffer, count, sem):
        piece = buffer.at[pl.ds(0, count), pl.ds(0, 17)]
        pltpu.make_async_copy(piece, piece, sem).wait()

    def spread(buffer, slot, partners, send, recv):
        for partner in partners:
            pltpu.make_async_remote_copy(
                src_ref=buffer.at[slot, pl.ds(0, 17)], dst_ref=buffer.at[slot, pl.ds(0, 17)], send_sem=send, recv_sem=recv,
                device_id=partner, device_id_type=MESH,
            ).start()

    spread(rz, zpos, z_partners, z_send, z_recv)
    wait_rows(rz, nz - 1, z_recv)
    part = rz[0]
    for i in range(1, nz):
        part = part + rz[i]
    rx[xpos] = part
    spread(rx, xpos, x_partners, x_send, x_recv)
    wait_rows(rx, NX4 - 1, x_recv)
    gram_ref[...] = (rx[0] + rx[1]) + (rx[2] + rx[3])
    wait_rows(rz, nz - 1, z_send)
    wait_rows(rx, NX4 - 1, x_send)


def analysis_kernel(gram_ref, hilo_ref, mean_ref, out_hbm, rows_out, out_sem):
    lane = iota((8, CX), 1)
    sub = iota((8, CX), 0)
    packed = gram_ref[pl.ds(0, 16), :]
    square = jnp.concatenate([packed, pltpu.roll(packed, M, 1)], axis=0)
    square = jnp.where(iota((32, CX), 1) < M, square, 0.0)
    turned = jnp.concatenate([square, jnp.zeros((CX - 32, CX), F32)], axis=0).T
    across, along = iota((32, CX), 1), iota((32, CX), 0)
    top = jnp.where((across < 32) & (across > along), turned[0:32], square)
    corner = jnp.where(across > along, square, jnp.where(across == along, gram_ref[pl.ds(16, 1), :], turned[0:32]))
    corner = pltpu.roll(jnp.where(across < 32, corner, 0.0), 32, 1)
    bottom = jnp.where(across < 32, turned[32:64], corner)
    blocks = [top[8 * i:8 * i + 8] for i in range(4)] + [bottom[8 * i:8 * i + 8] for i in range(4)]
    blocks = [jnp.where(lane < M - 1, b, 0.0) for b in blocks]
    row_sums = [jnp.sum(b, axis=1, keepdims=True) for b in blocks]
    eyes = [lane == sub + 8 * i for i in range(8)]
    diagonals = [jnp.where(e, b, 0.0) for e, b in zip(eyes, blocks)]
    last = sub == 7
    target_row = blocks[7][7:8] + jnp.where(lane[0:1] == M - 1, -row_sums[7][7:8], 0.0)
    blocks[7] = jnp.where(last, 0.0, blocks[7])
    row_sums[7] = jnp.where(last[:, 0:1], 0.0, row_sums[7])
    col_sum = functools.reduce(jnp.add, blocks)
    col_sum = jnp.sum(col_sum, axis=0, keepdims=True)
    all_sum = jnp.sum(functools.reduce(jnp.add, row_sums), axis=0, keepdims=True)
    blocks = [jnp.where(lane == M - 1, -r, b) for b, r in zip(blocks, row_sums)]
    blocks[7] = jnp.where(last, jnp.where(lane == M - 1, all_sum, -col_sum), blocks[7])
    scale_row = jnp.sum(functools.reduce(jnp.add, diagonals), axis=0, keepdims=True)
    scale_row = lax.rsqrt((M - 1.0) + jnp.where(lane[0:1] == M - 1, all_sum, scale_row))
    scale_col = [jnp.sum(d, axis=1, keepdims=True) for d in diagonals]
    scale_col[7] = jnp.where(last[:, 0:1], all_sum, scale_col[7])
    scale_col = [lax.rsqrt((M - 1.0) + c) for c in scale_col]
    blocks = [jnp.where(e, b + (M - 1.0), b) for e, b in zip(eyes, blocks)]
    a = [
        jnp.where(lane == sub + (M + 8 * i), scale_col[i], jnp.where(lane < M, blocks[i] * scale_col[i] * scale_row, 0.0))
        for i in range(8)
    ]

    lower = [None] * 8
    nothing = 0.0 * packed[0:8]
    for p in range(16):
        b, o = p // 2, 4 * (p % 2)
        cols = {
            (t, i): jnp.broadcast_to(a[i][:, 4 * p + t:4 * p + t + 1], (8, CX)) for t in range(4) for i in range(b, 8)
        }
        cols = {key: v + nothing if key[1] == b else v for key, v in cols.items()}
        d = {
            (s, t): jnp.broadcast_to(cols[t, b][o + s:o + s + 1, :], (8, CX)) for s in range(4) for t in range(s + 1)
        }
        r = [jnp.broadcast_to(a[b][o + s:o + s + 1, :], (8, CX)) for s in range(4)]

        det = d[0, 0] * d[1, 1] - d[1, 0] * d[1, 0]
        inv = 1.0 / det
        i00, i10, i11 = d[1, 1] * inv, -d[1, 0] * inv, d[0, 0] * inv
        e00 = i00 * d[2, 0] + i10 * d[2, 1]
        e10 = i10 * d[2, 0] + i11 * d[2, 1]
        e01 = i00 * d[3, 0] + i10 * d[3, 1]
        e11 = i10 * d[3, 0] + i11 * d[3, 1]
        c00 = d[2, 2] - (d[2, 0] * e00 + d[2, 1] * e10)
        c10 = d[3, 2] - (d[3, 0] * e00 + d[3, 1] * e10)
        c11 = d[3, 3] - (d[3, 0] * e01 + d[3, 1] * e11)
        r2 = r[2] - (e00 * r[0] + e10 * r[1])
        r3 = r[3] - (e01 * r[0] + e11 * r[1])
        det2 = c00 * c11 - c10 * c10
        if p < 15:
            u0 = i00 * r[0] + i10 * r[1]
            u1 = i10 * r[0] + i11 * r[1]
            inv2 = 1.0 / det2
            z2 = (c11 * r2 - c10 * r3) * inv2
            z3 = (c00 * r3 - c10 * r2) * inv2
            z0 = u0 - (e00 * z2 + e01 * z3)
            z1 = u1 - (e10 * z2 + e11 * z3)
            z = (z0, z1, z2, z3)
            for i in range(b if o == 0 else b + 1, 8):
                update = (cols[0, i] * z[0] + cols[1, i] * z[1]) + (cols[2, i] * z[2] + cols[3, i] * z[3])
                new = a[i] - update
                a[i] = jnp.where(sub >= 4, new, a[i]) if i == b else new
        n0 = r[0] * lax.rsqrt(d[0, 0])
        n1 = (d[0, 0] * r[1] - d[1, 0] * r[0]) * lax.rsqrt(d[0, 0] * det)
        n2 = r2 * lax.rsqrt(c00)
        n3 = (c00 * r3 - c10 * r2) * lax.rsqrt(c00 * det2)
        rows = jnp.where(sub == o, n0, jnp.where(sub == o + 1, n1, jnp.where(sub == o + 2, n2, n3)))
        lower[b] = rows if o == 0 else jnp.where(sub >= 4, rows, lower[b])
    lower = [pltpu.roll(jnp.where(lane >= M, v, 0.0), M, 1) for v in lower]
    heads = [jnp.sum(v * target_row, axis=1, keepdims=True) for v in lower]
    weight = jnp.sum(functools.reduce(jnp.add, [v * h for v, h in zip(lower, heads)]), axis=0, keepdims=True)
    root = math.sqrt(M - 1.0)
    mix = jnp.concatenate([root * v + weight for v in lower], axis=0)
    high = mix.astype(BF16).astype(F32)
    low = mix - high
    pair = jnp.where(iota((M, CX), 1) < M, high, pltpu.roll(high, M, 1)).astype(BF16)
    low_pair = jnp.where(iota((M, CX), 1) < M, low, pltpu.roll(low, M, 1)).astype(BF16)
    left = jnp.concatenate([pair, low_pair], axis=1)
    for r in range(0, CY, 2):
        cols = pl.ds(r * CX, 2 * CX)
        block = hilo_ref[:, cols]
        right = jnp.concatenate([block, block], axis=0)
        res = jnp.dot(left, right, preferred_element_type=F32)
        for half in range(2):
            rows_out[r + half] = res[:, half * CX:(half + 1) * CX] + mean_ref[r + half:r + half + 1, :]
            pltpu.make_async_copy(rows_out.at[r + half], out_hbm.at[:, r + half, :], out_sem).start()
    pltpu.make_async_copy(rows_out, rows_out, out_sem).wait()


def near(array):
    return pltpu.with_memory_space_constraint(array, pltpu.VMEM)


def body(ngy, ngx, ensemble, flow, obs_cell, obs_value, obs_var):
    vmem = pl.BlockSpec(memory_space=pltpu.VMEM)
    hbm = pl.BlockSpec(memory_space=pl.ANY)
    dma = pltpu.SemaphoreType.DMA
    part, hilo, mean = pl.pallas_call(
        functools.partial(forecast_kernel, ngy, ngx),
        out_shape=(
            pltpu.VMEM((24, CX), F32),
            pltpu.VMEM((2 * M, CY * CX), BF16),
            pltpu.VMEM((CY, CX), F32),
        ),
        in_specs=[hbm] * 5,
        out_specs=(vmem,) * 3,
        scratch_shapes=[
            pltpu.VMEM((M, CY, CX), F32),
            pltpu.VMEM((CY + 2, M, CX), F32),
            pltpu.VMEM((CY + 2, M, CX), F32),
            pltpu.VMEM((CY, M, CX), F32),
            pltpu.VMEM((3, CY, CX), F32),
            pltpu.VMEM((5, CY, CX), F32),
            pltpu.SMEM((1, 1, 4), jnp.int32),
            pltpu.SMEM((2, 1, 1, 4), F32),
            pltpu.VMEM((16, CX), F32),
            pltpu.VMEM((2, 8, CX), F32),
            pltpu.VMEM((8, CX), F32),
            pltpu.VMEM((4, M, CX), F32),
            pltpu.VMEM((2, 16, CX), F32),
            pltpu.VMEM((4, 8, CX), F32),
            pltpu.VMEM((4, 8, CX), F32),
            pltpu.VMEM((2, 8, CX), F32),
            pltpu.VMEM((ngx, 2, CX), F32),
            dma((6,)), dma((4,)), dma((4,)), dma, dma,
        ],
        compiler_params=pltpu.CompilerParams(collective_id=0, has_side_effects=True),
        name="forecast",
    )(ensemble, flow, obs_cell, obs_value, obs_var)
    gram = pl.pallas_call(
        functools.partial(sum_kernel, ngy),
        out_shape=pltpu.VMEM((24, CX), F32),
        in_specs=[vmem],
        out_specs=vmem,
        scratch_shapes=[
            pltpu.VMEM((ngy // NX4, 24, CX), F32),
            pltpu.VMEM((NX4, 24, CX), F32),
            dma, dma, dma, dma,
        ],
        compiler_params=pltpu.CompilerParams(collective_id=1, has_side_effects=True),
        name="sums",
    )(near(part))
    return pl.pallas_call(
        analysis_kernel,
        out_shape=jax.ShapeDtypeStruct((M, CY, CX), F32),
        in_specs=[vmem] * 3,
        out_specs=hbm,
        scratch_shapes=[pltpu.VMEM((CY, M, CX), F32), dma],
        name="analysis",
    )(near(gram), near(hilo), near(mean))


def solution(mesh):
    tile = P("gy", "gx", None)
    return jax.shard_map(
        functools.partial(body, mesh.shape["gy"], mesh.shape["gx"]),
        mesh=mesh,
        in_specs=(P(None, "gy", "gx"), P(None, "gy", "gx"), tile, tile, tile),
        out_specs=P(None, "gy", "gx"),
        check_vma=False,
    )
```

```python
import functools
import math

import jax
import jax.numpy as jnp
from jax import lax
from jax.experimental import pallas as pl
from jax.experimental.pallas import tpu as pltpu
from jax.sharding import PartitionSpec as P

MESH = pl.DeviceIdType.MESH
M = 64
CY = 8
CX = 128
F32 = jnp.float32
BF16 = jnp.bfloat16
NX4 = 4


def iota(shape, dim):
    return lax.broadcasted_iota(jnp.int32, shape, dim)


def step(x, n, s, w, e, k, hu, hv):
    return x + k * (n + s + w + e - 4.0 * x) - hu * (e - w) - hv * (s - n)


def forecast_kernel(
    ngy, ngx,
    x_hbm, flow_hbm, cell_hbm, val_hbm, var_hbm,
    gram_ref, hilo_ref, mean_ref,
    xb, xr, yr, zr, fl, cf, cells, obs, qs, fs, ct, h_rows, h_sides, h_corners, fh, zc, rf,
    load_sem, halo_send, halo_recv, gx_send, gx_recv,
):
    gy = lax.axis_index("gy")
    gx = lax.axis_index("gx")
    up, down = gy - 1, gy + 1
    has_up, has_down = gy > 0, gy < ngy - 1
    left, right = lax.rem(gx + ngx - 1, ngx), lax.rem(gx + 1, ngx)
    gx_partners = [(gy, lax.rem(gx + i, ngx)) for i in sorted(range(1, ngx), key=lambda i: -min(i, ngx - i))]

    def load(src, dst, index):
        pltpu.make_async_copy(src, dst, load_sem.at[index]).start()

    def loaded(piece, index):
        pltpu.make_async_copy(piece, piece, load_sem.at[index]).wait()

    load(flow_hbm, fl, 0)
    for r in (0, 7, 1, 6):
        load(x_hbm.at[:, r, :], xr.at[r + 1], 1)
    load(x_hbm, xb, 2)
    for r in (2, 3, 4, 5):
        load(x_hbm.at[:, r, :], xr.at[r + 1], 3)
    load(cell_hbm, cells, 4)
    load(val_hbm, obs.at[0], 5)
    load(var_hbm, obs.at[1], 5)
    barrier = pltpu.get_barrier_semaphore()

    def greet(partners):
        for partner in partners:
            pl.semaphore_signal(barrier, inc=1, device_id=partner, device_id_type=MESH)

    @pl.when(has_up)
    def _():
        greet([(up, gx), (up, left), (up, right)])

    @pl.when(has_down)
    def _():
        greet([(down, gx), (down, left), (down, right)])

    greet(gx_partners)

    lane = iota((8, CX), 1)
    sub = iota((8, CX), 0)
    edge = (lane <= 1) | (lane >= CX - 2)
    s0, s7 = sub == 0, sub == 7
    l0, l127 = lane == 0, lane == CX - 1
    quad = lane & 3
    q0, q1, q3 = quad == 0, quad == 1, quad == 3
    west_side = quad >= 2

    def remote(src, dst, index, target):
        return pltpu.make_async_remote_copy(
            src_ref=src, dst_ref=dst, send_sem=halo_send.at[index], recv_sem=halo_recv.at[index],
            device_id=target, device_id_type=MESH,
        )

    def start(index, to_up, to_down, to_left=None, to_right=None):
        @pl.when(has_up)
        def _():
            for src, dst, target in to_up:
                remote(src, dst, index, (up, target)).start()

        @pl.when(has_down)
        def _():
            for src, dst, target in to_down:
                remote(src, dst, index, (down, target)).start()

        if to_left:
            remote(*to_left, index, (gy, left)).start()
            remote(*to_right, index, (gy, right)).start()

    both = has_up & has_down

    def settle(sem, buffer, most, least):
        def wait(count):
            piece = buffer.at[pl.ds(0, count)]
            pltpu.make_async_copy(piece, piece, sem).wait()

        if most == least:
            wait(most)
        else:
            pl.when(both)(lambda: wait(most))
            pl.when(jnp.logical_not(both))(lambda: wait(least))

    groups = [(fh, 4, 3), (h_sides, 2, 2), (h_rows, 4, 2), (h_corners, 4, 2)]

    def received(index):
        settle(halo_recv.at[index], *groups[index])

    loaded(fl, 0)
    qc = jnp.where(edge, fl[0], 0.0)
    for i in range(1, 3):
        qc = qc + pltpu.roll(jnp.where(edge, fl[i], 0.0), 4 * i, 1)
    fs[1] = qc
    for i in range(3):
        fs[0, pl.ds(i, 1), :] = fl[i, 0:1, :]
        fs[0, pl.ds(3 + i, 1), :] = fl[i, 7:8, :]
    loaded(xr.at[pl.ds(0, 4)], 1)

    @pl.when(both)
    def _():
        pl.semaphore_wait(barrier, ngx + 5)

    @pl.when(jnp.logical_not(both))
    def _():
        pl.semaphore_wait(barrier, ngx + 2)

    start(2, [(xr.at[pl.ds(1, 2)], h_rows.at[pl.ds(2, 2)], gx)], [(xr.at[pl.ds(7, 2)], h_rows.at[pl.ds(0, 2)], gx)])
    start(0, [(fs.at[0], fh.at[1], gx)], [(fs.at[0], fh.at[0], gx)], (fs.at[1], fh.at[2]), (fs.at[1], fh.at[3]))
    ends = l0 | l127
    tile = jnp.zeros((8, CX), F32)
    for b in range(8):
        rows = pl.ds(8 * b, 8)
        tile = tile + pltpu.roll(jnp.where(ends, xr[1, rows, :], 0.0), 4 * b, 1)
        tile = tile + pltpu.roll(jnp.where(ends, xr[8, rows, :], 0.0), 4 * b + 2, 1)
    ct[...] = tile
    start(
        3,
        [(ct, h_corners.at[3], left), (ct, h_corners.at[2], right)],
        [(ct, h_corners.at[1], left), (ct, h_corners.at[0], right)],
    )
    loaded(xb, 2)

    def pack(half):
        def body(i, q):
            for j in range(8):
                m = i * 8 + j
                q = q + pltpu.roll(jnp.where(edge, xb[half * 32 + m], 0.0), lax.rem(CX - 4 * m, CX), 1)
            return q
        return lax.fori_loop(0, 4, body, jnp.zeros((8, CX), F32))

    qa, qb = pack(0), pack(1)
    qs[pl.ds(0, 8), :] = qa
    qs[pl.ds(8, 8), :] = qb
    start(1, [], [], (qs, h_sides.at[0]), (qs, h_sides.at[1]))
    loaded(xr.at[pl.ds(0, 4)], 3)
    loaded(cells, 4)
    loaded(obs, 5)

    def weights(f0, f1, f2):
        hu, hv = 0.5 * f1, 0.5 * f2
        return 1.0 - 4.0 * f0, f0 + hv, f0 - hv, f0 + hu, f0 - hu

    own = weights(fl[0], fl[1], fl[2])
    a0, an, as_, aw, ae = own
    aw_in, ae_in = jnp.where(l0, 0.0, aw), jnp.where(l127, 0.0, ae)
    for i, v in enumerate((a0, an, as_, aw_in, ae_in)):
        cf[i] = v

    blank = jnp.zeros((M, CX), F32)
    xr[0] = blank
    xr[9] = blank
    yr[0] = blank
    yr[9] = blank

    def inner(source, target, shift):
        def body(r, carry):
            c = [jnp.broadcast_to(cf[i, pl.ds(r, 1), :], (8, CX)) for i in range(5)]
            for b in range(8):
                rows = pl.ds(8 * b, 8)
                x = source[r + 1, rows, :]
                target[r + shift, rows, :] = (
                    (c[0] * x + c[1] * source[r, rows, :]) + (c[2] * source[r + 2, rows, :] + c[3] * pltpu.roll(x, 1, 1))
                    + c[4] * pltpu.roll(x, CX - 1, 1)
                )
            return carry
        lax.fori_loop(0, CY, body, 0)

    inner(xr, yr, 1)
    inner(yr, zr, 0)

    def col(v, l):
        return jnp.broadcast_to(v[:, l:l + 1], (8, CX))

    c_edge = jnp.where(q0, col(aw, 0), jnp.where(q3, col(ae, CX - 1), 0.0))
    a0_edge = jnp.where(q0, col(a0, 0), col(a0, CX - 1))
    an_edge = jnp.where(s0, 0.0, jnp.where(q0, col(an, 0), col(an, CX - 1)))
    as_edge = jnp.where(s7, 0.0, jnp.where(q0, col(as_, 0), col(as_, CX - 1)))
    c_next = jnp.where(q1, col(aw, 1), col(ae, CX - 2))

    has_left, has_right = gx > 0, gx < ngx - 1

    def on(flag):
        return jnp.full((8, CX), jnp.where(flag, 1, 0), jnp.int32) > 0

    cmask = (west_side & on(has_left)) | ((quad <= 1) & on(has_right))

    received(0)

    def flow_cols(i):
        west, east = col(fh[3], (4 * i - 1) % CX), col(fh[2], 4 * i)
        return jnp.where(cmask, jnp.where(west_side, west, east), 0.0)

    kc, uc, vc = flow_cols(0), 0.5 * flow_cols(1), 0.5 * flow_cols(2)

    def outer_row(tile, offset, flag):
        fields = [jnp.where(on(flag), jnp.broadcast_to(tile[offset + i:offset + i + 1, :], (8, CX)), 0.0) for i in range(3)]
        return weights(*fields)

    def line(v, r):
        return jnp.broadcast_to(v[r:r + 1, :], (8, CX))

    ends_in = (l0 & on(has_left)) | (l127 & on(has_right))

    def beside(i):
        return jnp.where(l0, pltpu.roll(fh[3], (1 - 4 * i) % CX, 1), pltpu.roll(fh[2], CX - 1 - 4 * i, 1))

    k_side, v_side = beside(0), 0.5 * beside(2)

    def outside(above):
        if above:
            t0, tn, ts, tw, te = outer_row(fh[0], 3, has_up)
            r, near, far, cross, toward = 0, line(an, 0), tn, ts, line(an, 1)
            side = line(k_side + v_side, 0)
        else:
            t0, tn, ts, tw, te = outer_row(fh[1], 0, has_down)
            r, near, far, cross, toward = 7, line(as_, 7), ts, tn, line(as_, 6)
            side = line(k_side - v_side, 7)
        west = near * jnp.where(l0, 0.0, tw) + line(aw_in, r) * pltpu.roll(near, 1, 1)
        east = near * jnp.where(l127, 0.0, te) + line(ae_in, r) * pltpu.roll(near, CX - 1, 1)
        corner = jnp.where(l0, near * tw + line(aw, r) * side, near * te + line(ae, r) * side)
        corner = jnp.where(ends_in, corner, 0.0)
        return near * (t0 + line(a0, r)), near * far, near * cross, west, east, toward * near, corner

    above = outside(True)
    below = outside(False)

    received(1)
    west_cell = q3
    for half in range(2):
        q = (qa, qb)[half]
        rows = pl.ds(8 * half, 8)
        ring = jnp.where(cmask, jnp.where(west_side, h_sides[1, rows, :], h_sides[0, rows, :]), 0.0)
        n = pltpu.roll(jnp.where(s7, 0.0, ring), 1, 0)
        s = pltpu.roll(jnp.where(s0, 0.0, ring), 7, 0)
        ring_w, ring_e = pltpu.roll(ring, 1, 1), pltpu.roll(ring, CX - 1, 1)
        w = jnp.where(west_cell, ring_w, pltpu.roll(q, 1, 1))
        e = jnp.where(west_cell, pltpu.roll(q, CX - 1, 1), ring_e)
        ring1 = step(ring, n, s, w, e, kc, uc, vc)
        x1 = jnp.where(q0, ring_w, ring_e)
        y1 = jnp.where(q0, pltpu.roll(ring1, 1, 1), pltpu.roll(ring1, CX - 1, 1))
        d = c_edge * x1
        at_edge = a0_edge * d + an_edge * pltpu.roll(d, 1, 0) + as_edge * pltpu.roll(d, 7, 0) + c_edge * y1
        inside = c_next * jnp.where(q1, pltpu.roll(d, 1, 1), pltpu.roll(d, CX - 1, 1))
        zc[half] = jnp.where(q0 | q3, at_edge, inside)

    received(2)
    received(3)

    def add_rows(flag, c, near_row, far_row, r, r_in, corners, first):
        @pl.when(flag)
        def _():
            merged = corners()
            for b in range(8):
                rows = pl.ds(8 * b, 8)
                p = h_rows[near_row, rows, :]
                zr[r, rows, :] = zr[r, rows, :] + (
                    (c[0] * p + c[1] * h_rows[far_row, rows, :]) + (c[2] * xr[r + 1, rows, :] + c[3] * pltpu.roll(p, 1, 1))
                    + (c[4] * pltpu.roll(p, CX - 1, 1) + c[6] * pltpu.roll(merged, (first - 4 * b) % CX, 1))
                )
                zr[r_in, rows, :] = zr[r_in, rows, :] + c[5] * p

    add_rows(has_up, above, 1, 0, 0, 1, lambda: jnp.where(q1, h_corners[0], pltpu.roll(h_corners[1], CX - 2, 1)), CX - 1)
    add_rows(has_down, below, 2, 3, 7, 6, lambda: jnp.where(q3, h_corners[2], pltpu.roll(h_corners[3], CX - 2, 1)), 1)

    def with_columns(r, b, lines):
        spread = pltpu.roll(lines[b // 4], 32 * (b % 4), 1, stride=4, stride_axis=0)
        return zr[r, 8 * b:8 * b + 8, :] + jnp.where(edge, spread, 0.0)

    def column_lines(r):
        return [jnp.broadcast_to(zc[half, pl.ds(r, 1), :], (8, CX)) for half in range(2)]

    lane64 = iota((M, CX), 1)
    diag64 = lane64 == iota((M, CX), 0)
    ones = jnp.zeros((1, CX), F32)
    picked = []
    for j in range(4):
        cell = cells[0, 0, j]
        row, place = lax.shift_right_logical(cell, 7), cell & (CX - 1)
        lines = column_lines(row)
        field = jnp.concatenate([with_columns(row, b, lines) for b in range(8)], axis=0)
        column = jnp.sum(jnp.where(lane64 == place, field, 0.0), axis=1, keepdims=True)
        column = jnp.broadcast_to(column, (M, CX))
        average = jnp.sum(column, axis=0, keepdims=True) * (1.0 / M)
        factor = lax.rsqrt(ones + obs[1, 0, 0, j])
        values = jnp.sum(jnp.where(diag64, column, 0.0), axis=0, keepdims=True)
        values = jnp.where(iota((1, CX), 1) < M - 1, values, ones + obs[0, 0, 0, j])
        picked.append(jnp.where(iota((1, CX), 1) < M, (values - average) * factor, 0.0))
    rf[gx] = jnp.concatenate(
        [picked[0] + pltpu.roll(picked[2], M, 1), picked[1] + pltpu.roll(picked[3], M, 1)], axis=0
    )

    gx_copies = [
        pltpu.make_async_remote_copy(
            src_ref=rf.at[gx], dst_ref=rf.at[gx], send_sem=gx_send, recv_sem=gx_recv,
            device_id=partner, device_id_type=MESH,
        )
        for partner in gx_partners
    ]
    for copy in gx_copies:
        copy.start()

    for r in range(CY):
        lines = column_lines(r)
        field = jnp.concatenate([with_columns(r, b, lines) for b in range(8)], axis=0)
        mean = jnp.sum(field, axis=0, keepdims=True) * (1.0 / M)
        mean_ref[pl.ds(r, 1), :] = mean
        field = field - mean
        high = field.astype(BF16)
        hilo_ref[pl.ds(0, M), pl.ds(r * CX, CX)] = high
        hilo_ref[pl.ds(M, M), pl.ds(r * CX, CX)] = (field - high.astype(F32)).astype(BF16)

    wait_all(rf, ngx - 1, gx_recv)
    gathered = jnp.concatenate([rf[i] for i in range(ngx)], axis=0)
    lane32 = iota((2 * ngx, CX), 1)
    rows = jnp.concatenate(
        [jnp.where(lane32 < M, gathered, 0.0), jnp.where(lane32 < M, pltpu.roll(gathered, M, 1), 0.0)], axis=0
    )
    gram = jnp.dot(rows.T, rows, precision=lax.Precision.HIGHEST, preferred_element_type=F32)
    high, low = gram[0:32], pltpu.roll(gram[32:64], CX - 32, 1)
    across, along = iota((32, CX), 1), iota((32, CX), 0)
    square = jnp.where((across < 32) & (across > along), low, high)
    gram_ref[pl.ds(0, 16), :] = square[0:16] + pltpu.roll(square[16:32], M, 1)
    diagonal = jnp.sum(jnp.where(across == along, low, 0.0), axis=0, keepdims=True)
    gram_ref[pl.ds(16, 8), :] = jnp.where(iota((8, CX), 0) == 0, diagonal, 0.0)

    for index, group in enumerate(groups):
        settle(halo_send.at[index], *group)
    wait_all(rf, ngx - 1, gx_send)


def wait_all(buffer, count, sem):
    piece = buffer.at[pl.ds(0, count)]
    pltpu.make_async_copy(piece, piece, sem).wait()


def sum_kernel(ngy, part_ref, gram_ref, rz, rx, z_send, z_recv, x_send, x_recv):
    gy = lax.axis_index("gy")
    gx = lax.axis_index("gx")
    nz = ngy // NX4
    zpos = gy // NX4
    xpos = lax.rem(gy, NX4)
    z_partners = [(lax.rem(gy + NX4 * i, ngy), gx) for i in range(1, nz)]
    x_partners = [(zpos * NX4 + lax.rem(xpos + i, NX4), gx) for i in (2, 1, 3)]
    barrier = pltpu.get_barrier_semaphore()
    for partner in z_partners + x_partners:
        pl.semaphore_signal(barrier, inc=1, device_id=partner, device_id_type=MESH)
    rz[zpos] = part_ref[...]
    pl.semaphore_wait(barrier, nz + NX4 - 2)

    def wait_rows(buffer, count, sem):
        piece = buffer.at[pl.ds(0, count), pl.ds(0, 17)]
        pltpu.make_async_copy(piece, piece, sem).wait()

    def spread(buffer, slot, partners, send, recv):
        for partner in partners:
            pltpu.make_async_remote_copy(
                src_ref=buffer.at[slot, pl.ds(0, 17)], dst_ref=buffer.at[slot, pl.ds(0, 17)], send_sem=send, recv_sem=recv,
                device_id=partner, device_id_type=MESH,
            ).start()

    spread(rz, zpos, z_partners, z_send, z_recv)
    wait_rows(rz, nz - 1, z_recv)
    part = rz[0]
    for i in range(1, nz):
        part = part + rz[i]
    rx[xpos] = part
    spread(rx, xpos, x_partners, x_send, x_recv)
    wait_rows(rx, NX4 - 1, x_recv)
    gram_ref[...] = (rx[0] + rx[1]) + (rx[2] + rx[3])
    wait_rows(rz, nz - 1, z_send)
    wait_rows(rx, NX4 - 1, x_send)


def analysis_kernel(gram_ref, hilo_ref, mean_ref, out_hbm, rows_out, out_sem):
    lane = iota((8, CX), 1)
    sub = iota((8, CX), 0)
    packed = gram_ref[pl.ds(0, 16), :]
    square = jnp.concatenate([packed, pltpu.roll(packed, M, 1)], axis=0)
    square = jnp.where(iota((32, CX), 1) < M, square, 0.0)
    turned = jnp.concatenate([square, jnp.zeros((CX - 32, CX), F32)], axis=0).T
    across, along = iota((32, CX), 1), iota((32, CX), 0)
    top = jnp.where((across < 32) & (across > along), turned[0:32], square)
    corner = jnp.where(across > along, square, jnp.where(across == along, gram_ref[pl.ds(16, 1), :], turned[0:32]))
    corner = pltpu.roll(jnp.where(across < 32, corner, 0.0), 32, 1)
    bottom = jnp.where(across < 32, turned[32:64], corner)
    blocks = [top[8 * i:8 * i + 8] for i in range(4)] + [bottom[8 * i:8 * i + 8] for i in range(4)]
    blocks = [jnp.where(lane < M - 1, b, 0.0) for b in blocks]
    row_sums = [jnp.sum(b, axis=1, keepdims=True) for b in blocks]
    eyes = [lane == sub + 8 * i for i in range(8)]
    diagonals = [jnp.where(e, b, 0.0) for e, b in zip(eyes, blocks)]
    last = sub == 7
    target_row = blocks[7][7:8] + jnp.where(lane[0:1] == M - 1, -row_sums[7][7:8], 0.0)
    blocks[7] = jnp.where(last, 0.0, blocks[7])
    row_sums[7] = jnp.where(last[:, 0:1], 0.0, row_sums[7])
    col_sum = functools.reduce(jnp.add, blocks)
    col_sum = jnp.sum(col_sum, axis=0, keepdims=True)
    all_sum = jnp.sum(functools.reduce(jnp.add, row_sums), axis=0, keepdims=True)
    blocks = [jnp.where(lane == M - 1, -r, b) for b, r in zip(blocks, row_sums)]
    blocks[7] = jnp.where(last, jnp.where(lane == M - 1, all_sum, -col_sum), blocks[7])
    scale_row = jnp.sum(functools.reduce(jnp.add, diagonals), axis=0, keepdims=True)
    scale_row = lax.rsqrt((M - 1.0) + jnp.where(lane[0:1] == M - 1, all_sum, scale_row))
    scale_col = [jnp.sum(d, axis=1, keepdims=True) for d in diagonals]
    scale_col[7] = jnp.where(last[:, 0:1], all_sum, scale_col[7])
    scale_col = [lax.rsqrt((M - 1.0) + c) for c in scale_col]
    blocks = [jnp.where(e, b + (M - 1.0), b) for e, b in zip(eyes, blocks)]
    a = [
        jnp.where(lane == sub + (M + 8 * i), scale_col[i], jnp.where(lane < M, blocks[i] * scale_col[i] * scale_row, 0.0))
        for i in range(8)
    ]

    lower = [None] * 8
    nothing = 0.0 * packed[0:8]
    for p in range(16):
        b, o = p // 2, 4 * (p % 2)
        cols = {
            (t, i): jnp.broadcast_to(a[i][:, 4 * p + t:4 * p + t + 1], (8, CX)) for t in range(4) for i in range(b, 8)
        }
        cols = {key: v + nothing if key[1] == b else v for key, v in cols.items()}
        d = {
            (s, t): jnp.broadcast_to(cols[t, b][o + s:o + s + 1, :], (8, CX)) for s in range(4) for t in range(s + 1)
        }
        r = [jnp.broadcast_to(a[b][o + s:o + s + 1, :], (8, CX)) for s in range(4)]

        det = d[0, 0] * d[1, 1] - d[1, 0] * d[1, 0]
        inv = 1.0 / det
        i00, i10, i11 = d[1, 1] * inv, -d[1, 0] * inv, d[0, 0] * inv
        e00 = i00 * d[2, 0] + i10 * d[2, 1]
        e10 = i10 * d[2, 0] + i11 * d[2, 1]
        e01 = i00 * d[3, 0] + i10 * d[3, 1]
        e11 = i10 * d[3, 0] + i11 * d[3, 1]
        c00 = d[2, 2] - (d[2, 0] * e00 + d[2, 1] * e10)
        c10 = d[3, 2] - (d[3, 0] * e00 + d[3, 1] * e10)
        c11 = d[3, 3] - (d[3, 0] * e01 + d[3, 1] * e11)
        r2 = r[2] - (e00 * r[0] + e10 * r[1])
        r3 = r[3] - (e01 * r[0] + e11 * r[1])
        det2 = c00 * c11 - c10 * c10
        if p < 15:
            u0 = i00 * r[0] + i10 * r[1]
            u1 = i10 * r[0] + i11 * r[1]
            inv2 = 1.0 / det2
            z2 = (c11 * r2 - c10 * r3) * inv2
            z3 = (c00 * r3 - c10 * r2) * inv2
            z0 = u0 - (e00 * z2 + e01 * z3)
            z1 = u1 - (e10 * z2 + e11 * z3)
            z = (z0, z1, z2, z3)
            for i in range(b if o == 0 else b + 1, 8):
                update = (cols[0, i] * z[0] + cols[1, i] * z[1]) + (cols[2, i] * z[2] + cols[3, i] * z[3])
                new = a[i] - update
                a[i] = jnp.where(sub >= 4, new, a[i]) if i == b else new
        n0 = r[0] * lax.rsqrt(d[0, 0])
        n1 = (d[0, 0] * r[1] - d[1, 0] * r[0]) * lax.rsqrt(d[0, 0] * det)
        n2 = r2 * lax.rsqrt(c00)
        n3 = (c00 * r3 - c10 * r2) * lax.rsqrt(c00 * det2)
        rows = jnp.where(sub == o, n0, jnp.where(sub == o + 1, n1, jnp.where(sub == o + 2, n2, n3)))
        lower[b] = rows if o == 0 else jnp.where(sub >= 4, rows, lower[b])
    lower = [pltpu.roll(jnp.where(lane >= M, v, 0.0), M, 1) for v in lower]
    heads = [jnp.sum(v * target_row, axis=1, keepdims=True) for v in lower]
    weight = jnp.sum(functools.reduce(jnp.add, [v * h for v, h in zip(lower, heads)]), axis=0, keepdims=True)
    root = math.sqrt(M - 1.0)
    mix = jnp.concatenate([root * v + weight for v in lower], axis=0)
    high = mix.astype(BF16).astype(F32)
    low = mix - high
    pair = jnp.where(iota((M, CX), 1) < M, high, pltpu.roll(high, M, 1)).astype(BF16)
    low_pair = jnp.where(iota((M, CX), 1) < M, low, pltpu.roll(low, M, 1)).astype(BF16)
    left = jnp.concatenate([pair, low_pair], axis=1)
    for r in range(0, CY, 2):
        cols = pl.ds(r * CX, 2 * CX)
        block = hilo_ref[:, cols]
        right = jnp.concatenate([block, block], axis=0)
        res = jnp.dot(left, right, preferred_element_type=F32)
        for half in range(2):
            rows_out[r + half] = res[:, half * CX:(half + 1) * CX] + mean_ref[r + half:r + half + 1, :]
            pltpu.make_async_copy(rows_out.at[r + half], out_hbm.at[:, r + half, :], out_sem).start()
    pltpu.make_async_copy(rows_out, rows_out, out_sem).wait()


def near(array):
    return pltpu.with_memory_space_constraint(array, pltpu.VMEM)


def body(ngy, ngx, ensemble, flow, obs_cell, obs_value, obs_var):
    vmem = pl.BlockSpec(memory_space=pltpu.VMEM)
    hbm = pl.BlockSpec(memory_space=pl.ANY)
    dma = pltpu.SemaphoreType.DMA
    part, hilo, mean = pl.pallas_call(
        functools.partial(forecast_kernel, ngy, ngx),
        out_shape=(
            pltpu.VMEM((24, CX), F32),
            pltpu.VMEM((2 * M, CY * CX), BF16),
            pltpu.VMEM((CY, CX), F32),
        ),
        in_specs=[hbm] * 5,
        out_specs=(vmem,) * 3,
        scratch_shapes=[
            pltpu.VMEM((M, CY, CX), F32),
            pltpu.VMEM((CY + 2, M, CX), F32),
            pltpu.VMEM((CY + 2, M, CX), F32),
            pltpu.VMEM((CY, M, CX), F32),
            pltpu.VMEM((3, CY, CX), F32),
            pltpu.VMEM((5, CY, CX), F32),
            pltpu.SMEM((1, 1, 4), jnp.int32),
            pltpu.SMEM((2, 1, 1, 4), F32),
            pltpu.VMEM((16, CX), F32),
            pltpu.VMEM((2, 8, CX), F32),
            pltpu.VMEM((8, CX), F32),
            pltpu.VMEM((4, M, CX), F32),
            pltpu.VMEM((2, 16, CX), F32),
            pltpu.VMEM((4, 8, CX), F32),
            pltpu.VMEM((4, 8, CX), F32),
            pltpu.VMEM((2, 8, CX), F32),
            pltpu.VMEM((ngx, 2, CX), F32),
            dma((6,)), dma((4,)), dma((4,)), dma, dma,
        ],
        compiler_params=pltpu.CompilerParams(collective_id=0, has_side_effects=True),
        name="forecast",
    )(ensemble, flow, obs_cell, obs_value, obs_var)
    gram = pl.pallas_call(
        functools.partial(sum_kernel, ngy),
        out_shape=pltpu.VMEM((24, CX), F32),
        in_specs=[vmem],
        out_specs=vmem,
        scratch_shapes=[
            pltpu.VMEM((ngy // NX4, 24, CX), F32),
            pltpu.VMEM((NX4, 24, CX), F32),
            dma, dma, dma, dma,
        ],
        compiler_params=pltpu.CompilerParams(collective_id=1, has_side_effects=True),
        name="sums",
    )(near(part))
    return pl.pallas_call(
        analysis_kernel,
        out_shape=jax.ShapeDtypeStruct((M, CY, CX), F32),
        in_specs=[vmem] * 3,
        out_specs=hbm,
        scratch_shapes=[pltpu.VMEM((CY, M, CX), F32), dma],
        name="analysis",
    )(near(gram), near(hilo), near(mean))


def solution(mesh):
    tile = P("gy", "gx", None)
    return jax.shard_map(
        functools.partial(body, mesh.shape["gy"], mesh.shape["gx"]),
        mesh=mesh,
        in_specs=(P(None, "gy", "gx"), P(None, "gy", "gx"), tile, tile, tile),
        out_specs=P(None, "gy", "gx"),
        check_vma=False,
    )
```

```python
import functools
import math

import jax
import jax.numpy as jnp
from jax import lax
from jax.experimental import pallas as pl
from jax.experimental.pallas import tpu as pltpu
from jax.sharding import PartitionSpec as P

MESH = pl.DeviceIdType.MESH
M = 64
CY = 8
CX = 128
F32 = jnp.float32
BF16 = jnp.bfloat16
NX4 = 4


def iota(shape, dim):
    return lax.broadcasted_iota(jnp.int32, shape, dim)


def step(x, n, s, w, e, k, hu, hv):
    return x + k * (n + s + w + e - 4.0 * x) - hu * (e - w) - hv * (s - n)


def forecast_kernel(
    ngy, ngx,
    x_hbm, flow_hbm, cell_hbm, val_hbm, var_hbm,
    gram_ref, hilo_ref, mean_ref,
    xb, xr, yr, zr, fl, cf, cells, obs, qs, fs, ct, h_rows, h_sides, h_corners, fh, zc, rf,
    load_sem, corner_send, halo_recv, gx_recv,
):
    gy = lax.axis_index("gy")
    gx = lax.axis_index("gx")
    up, down = gy - 1, gy + 1
    has_up, has_down = gy > 0, gy < ngy - 1
    left, right = lax.rem(gx + ngx - 1, ngx), lax.rem(gx + 1, ngx)
    gx_partners = [(gy, lax.rem(gx + i, ngx)) for i in sorted(range(1, ngx), key=lambda i: -min(i, ngx - i))]

    def load(src, dst, index):
        pltpu.make_async_copy(src, dst, load_sem.at[index]).start()

    def loaded(piece, index):
        pltpu.make_async_copy(piece, piece, load_sem.at[index]).wait()

    load(flow_hbm, fl, 0)
    for r in (0, 7, 1, 6):
        load(x_hbm.at[:, r, :], xr.at[r + 1], 1)
    load(x_hbm, xb, 2)
    for r in (2, 3, 4, 5):
        load(x_hbm.at[:, r, :], xr.at[r + 1], 3)
    load(cell_hbm, cells, 4)
    load(val_hbm, obs.at[0], 5)
    load(var_hbm, obs.at[1], 5)
    barrier = pltpu.get_barrier_semaphore()

    def greet(partners):
        for partner in partners:
            pl.semaphore_signal(barrier, inc=1, device_id=partner, device_id_type=MESH)

    @pl.when(has_up)
    def _():
        greet([(up, gx), (up, left), (up, right)])

    @pl.when(has_down)
    def _():
        greet([(down, gx), (down, left), (down, right)])

    greet(gx_partners)

    lane = iota((8, CX), 1)
    sub = iota((8, CX), 0)
    edge = (lane <= 1) | (lane >= CX - 2)
    s0, s7 = sub == 0, sub == 7
    l0, l127 = lane == 0, lane == CX - 1
    quad = lane & 3
    q0, q1, q3 = quad == 0, quad == 1, quad == 3
    west_side = quad >= 2

    sends = [load_sem.at[0], load_sem.at[2], load_sem.at[1], corner_send]
    gx_send = load_sem.at[3]

    def remote(src, dst, index, target):
        return pltpu.make_async_remote_copy(
            src_ref=src, dst_ref=dst, send_sem=sends[index], recv_sem=halo_recv.at[index],
            device_id=target, device_id_type=MESH,
        )

    def start(index, to_up, to_down, to_left=None, to_right=None):
        @pl.when(has_up)
        def _():
            for src, dst, target in to_up:
                remote(src, dst, index, (up, target)).start()

        @pl.when(has_down)
        def _():
            for src, dst, target in to_down:
                remote(src, dst, index, (down, target)).start()

        if to_left:
            remote(*to_left, index, (gy, left)).start()
            remote(*to_right, index, (gy, right)).start()

    both = has_up & has_down

    def settle(sem, buffer, most, least):
        def wait(count):
            piece = buffer.at[pl.ds(0, count)]
            pltpu.make_async_copy(piece, piece, sem).wait()

        if most == least:
            wait(most)
        else:
            pl.when(both)(lambda: wait(most))
            pl.when(jnp.logical_not(both))(lambda: wait(least))

    groups = [(fh, 4, 3), (h_sides, 2, 2), (h_rows, 4, 2), (h_corners, 4, 2)]

    def received(index):
        settle(halo_recv.at[index], *groups[index])

    loaded(fl, 0)
    qc = jnp.where(edge, fl[0], 0.0)
    for i in range(1, 3):
        qc = qc + pltpu.roll(jnp.where(edge, fl[i], 0.0), 4 * i, 1)
    fs[1] = qc
    for i in range(3):
        fs[0, pl.ds(i, 1), :] = fl[i, 0:1, :]
        fs[0, pl.ds(3 + i, 1), :] = fl[i, 7:8, :]
    loaded(xr.at[pl.ds(0, 4)], 1)

    ends = l0 | l127
    tile = jnp.zeros((8, CX), F32)
    for b in range(8):
        rows = pl.ds(8 * b, 8)
        tile = tile + pltpu.roll(jnp.where(ends, xr[1, rows, :], 0.0), 4 * b, 1)
        tile = tile + pltpu.roll(jnp.where(ends, xr[8, rows, :], 0.0), 4 * b + 2, 1)
    ct[...] = tile

    @pl.when(both)
    def _():
        pl.semaphore_wait(barrier, ngx + 5)

    @pl.when(jnp.logical_not(both))
    def _():
        pl.semaphore_wait(barrier, ngx + 2)

    start(
        3,
        [(ct, h_corners.at[3], left), (ct, h_corners.at[2], right)],
        [(ct, h_corners.at[1], left), (ct, h_corners.at[0], right)],
    )
    start(0, [(fs.at[0], fh.at[1], gx)], [(fs.at[0], fh.at[0], gx)], (fs.at[1], fh.at[2]), (fs.at[1], fh.at[3]))
    start(2, [(xr.at[pl.ds(1, 2)], h_rows.at[pl.ds(2, 2)], gx)], [(xr.at[pl.ds(7, 2)], h_rows.at[pl.ds(0, 2)], gx)])
    loaded(xb, 2)

    def pack(half):
        sums = [None] * 4
        for m in range(32):
            piece = pltpu.roll(jnp.where(edge, xb[half * 32 + m], 0.0), (CX - 4 * m) % CX, 1)
            sums[m % 4] = piece if m < 4 else sums[m % 4] + piece
        return (sums[0] + sums[1]) + (sums[2] + sums[3])

    qa, qb = pack(0), pack(1)
    qs[pl.ds(0, 8), :] = qa
    qs[pl.ds(8, 8), :] = qb
    start(1, [], [], (qs, h_sides.at[0]), (qs, h_sides.at[1]))
    loaded(xr.at[pl.ds(0, 4)], 3)
    loaded(cells, 4)
    loaded(obs, 5)

    def weights(f0, f1, f2):
        hu, hv = 0.5 * f1, 0.5 * f2
        return 1.0 - 4.0 * f0, f0 + hv, f0 - hv, f0 + hu, f0 - hu

    own = weights(fl[0], fl[1], fl[2])
    a0, an, as_, aw, ae = own
    aw_in, ae_in = jnp.where(l0, 0.0, aw), jnp.where(l127, 0.0, ae)
    for i, v in enumerate((a0, an, as_, aw_in, ae_in)):
        cf[i] = v

    blank = jnp.zeros((M, CX), F32)
    xr[0] = blank
    xr[9] = blank
    yr[0] = blank
    yr[9] = blank

    def inner(source, target, shift):
        def body(r, carry):
            c = [jnp.broadcast_to(cf[i, pl.ds(r, 1), :], (8, CX)) for i in range(5)]
            for b in range(8):
                rows = pl.ds(8 * b, 8)
                x = source[r + 1, rows, :]
                target[r + shift, rows, :] = (
                    (c[0] * x + c[1] * source[r, rows, :]) + (c[2] * source[r + 2, rows, :] + c[3] * pltpu.roll(x, 1, 1))
                    + c[4] * pltpu.roll(x, CX - 1, 1)
                )
            return carry
        lax.fori_loop(0, CY, body, 0)

    inner(xr, yr, 1)
    inner(yr, zr, 0)

    def col(v, l):
        return jnp.broadcast_to(v[:, l:l + 1], (8, CX))

    c_edge = jnp.where(q0, col(aw, 0), jnp.where(q3, col(ae, CX - 1), 0.0))
    a0_edge = jnp.where(q0, col(a0, 0), col(a0, CX - 1))
    an_edge = jnp.where(s0, 0.0, jnp.where(q0, col(an, 0), col(an, CX - 1)))
    as_edge = jnp.where(s7, 0.0, jnp.where(q0, col(as_, 0), col(as_, CX - 1)))
    c_next = jnp.where(q1, col(aw, 1), col(ae, CX - 2))

    has_left, has_right = gx > 0, gx < ngx - 1

    def on(flag):
        return jnp.full((8, CX), jnp.where(flag, 1, 0), jnp.int32) > 0

    cmask = (west_side & on(has_left)) | ((quad <= 1) & on(has_right))

    received(0)

    def flow_cols(i):
        west, east = col(fh[3], (4 * i - 1) % CX), col(fh[2], 4 * i)
        return jnp.where(cmask, jnp.where(west_side, west, east), 0.0)

    kc, uc, vc = flow_cols(0), 0.5 * flow_cols(1), 0.5 * flow_cols(2)

    def outer_row(tile, offset, flag):
        fields = [jnp.where(on(flag), jnp.broadcast_to(tile[offset + i:offset + i + 1, :], (8, CX)), 0.0) for i in range(3)]
        return weights(*fields)

    def line(v, r):
        return jnp.broadcast_to(v[r:r + 1, :], (8, CX))

    ends_in = (l0 & on(has_left)) | (l127 & on(has_right))

    def beside(i):
        return jnp.where(l0, pltpu.roll(fh[3], (1 - 4 * i) % CX, 1), pltpu.roll(fh[2], CX - 1 - 4 * i, 1))

    k_side, v_side = beside(0), 0.5 * beside(2)

    def outside(above):
        if above:
            t0, tn, ts, tw, te = outer_row(fh[0], 3, has_up)
            r, near, far, cross, toward = 0, line(an, 0), tn, ts, line(an, 1)
            side = line(k_side + v_side, 0)
        else:
            t0, tn, ts, tw, te = outer_row(fh[1], 0, has_down)
            r, near, far, cross, toward = 7, line(as_, 7), ts, tn, line(as_, 6)
            side = line(k_side - v_side, 7)
        west = near * jnp.where(l0, 0.0, tw) + line(aw_in, r) * pltpu.roll(near, 1, 1)
        east = near * jnp.where(l127, 0.0, te) + line(ae_in, r) * pltpu.roll(near, CX - 1, 1)
        corner = jnp.where(l0, near * tw + line(aw, r) * side, near * te + line(ae, r) * side)
        corner = jnp.where(ends_in, corner, 0.0)
        return near * (t0 + line(a0, r)), near * far, near * cross, west, east, toward * near, corner

    above = outside(True)
    below = outside(False)

    received(1)
    west_cell = q3
    for half in range(2):
        q = (qa, qb)[half]
        rows = pl.ds(8 * half, 8)
        ring = jnp.where(cmask, jnp.where(west_side, h_sides[1, rows, :], h_sides[0, rows, :]), 0.0)
        n = pltpu.roll(jnp.where(s7, 0.0, ring), 1, 0)
        s = pltpu.roll(jnp.where(s0, 0.0, ring), 7, 0)
        ring_w, ring_e = pltpu.roll(ring, 1, 1), pltpu.roll(ring, CX - 1, 1)
        w = jnp.where(west_cell, ring_w, pltpu.roll(q, 1, 1))
        e = jnp.where(west_cell, pltpu.roll(q, CX - 1, 1), ring_e)
        ring1 = step(ring, n, s, w, e, kc, uc, vc)
        x1 = jnp.where(q0, ring_w, ring_e)
        y1 = jnp.where(q0, pltpu.roll(ring1, 1, 1), pltpu.roll(ring1, CX - 1, 1))
        d = c_edge * x1
        at_edge = a0_edge * d + an_edge * pltpu.roll(d, 1, 0) + as_edge * pltpu.roll(d, 7, 0) + c_edge * y1
        inside = c_next * jnp.where(q1, pltpu.roll(d, 1, 1), pltpu.roll(d, CX - 1, 1))
        zc[half] = jnp.where(q0 | q3, at_edge, inside)

    received(2)
    received(3)

    def add_rows(flag, c, near_row, far_row, r, r_in, corners, first):
        @pl.when(flag)
        def _():
            merged = corners()
            for b in range(8):
                rows = pl.ds(8 * b, 8)
                p = h_rows[near_row, rows, :]
                zr[r, rows, :] = zr[r, rows, :] + (
                    (c[0] * p + c[1] * h_rows[far_row, rows, :]) + (c[2] * xr[r + 1, rows, :] + c[3] * pltpu.roll(p, 1, 1))
                    + (c[4] * pltpu.roll(p, CX - 1, 1) + c[6] * pltpu.roll(merged, (first - 4 * b) % CX, 1))
                )
                zr[r_in, rows, :] = zr[r_in, rows, :] + c[5] * p

    add_rows(has_up, above, 1, 0, 0, 1, lambda: jnp.where(q1, h_corners[0], pltpu.roll(h_corners[1], CX - 2, 1)), CX - 1)
    add_rows(has_down, below, 2, 3, 7, 6, lambda: jnp.where(q3, h_corners[2], pltpu.roll(h_corners[3], CX - 2, 1)), 1)

    def with_columns(r, b, lines):
        spread = pltpu.roll(lines[b // 4], 32 * (b % 4), 1, stride=4, stride_axis=0)
        return zr[r, 8 * b:8 * b + 8, :] + jnp.where(edge, spread, 0.0)

    def column_lines(r):
        return [jnp.broadcast_to(zc[half, pl.ds(r, 1), :], (8, CX)) for half in range(2)]

    lane64 = iota((M, CX), 1)
    diag64 = lane64 == iota((M, CX), 0)
    ones = jnp.zeros((1, CX), F32)
    picked = []
    for j in range(4):
        cell = cells[0, 0, j]
        row, place = lax.shift_right_logical(cell, 7), cell & (CX - 1)
        lines = column_lines(row)
        field = jnp.concatenate([with_columns(row, b, lines) for b in range(8)], axis=0)
        column = jnp.sum(jnp.where(lane64 == place, field, 0.0), axis=1, keepdims=True)
        column = jnp.broadcast_to(column, (M, CX))
        average = jnp.sum(column, axis=0, keepdims=True) * (1.0 / M)
        factor = lax.rsqrt(ones + obs[1, 0, 0, j])
        values = jnp.sum(jnp.where(diag64, column, 0.0), axis=0, keepdims=True)
        values = jnp.where(iota((1, CX), 1) < M - 1, values, ones + obs[0, 0, 0, j])
        picked.append(jnp.where(iota((1, CX), 1) < M, (values - average) * factor, 0.0))
    rf[gx] = jnp.concatenate(
        [picked[0] + pltpu.roll(picked[2], M, 1), picked[1] + pltpu.roll(picked[3], M, 1)], axis=0
    )

    gx_copies = [
        pltpu.make_async_remote_copy(
            src_ref=rf.at[gx], dst_ref=rf.at[gx], send_sem=gx_send, recv_sem=gx_recv,
            device_id=partner, device_id_type=MESH,
        )
        for partner in gx_partners
    ]
    for copy in gx_copies:
        copy.start()

    for r in range(CY):
        lines = column_lines(r)
        field = jnp.concatenate([with_columns(r, b, lines) for b in range(8)], axis=0)
        mean = jnp.sum(field, axis=0, keepdims=True) * (1.0 / M)
        mean_ref[pl.ds(r, 1), :] = mean
        field = field - mean
        high = field.astype(BF16)
        hilo_ref[pl.ds(0, M), pl.ds(r * CX, CX)] = high
        hilo_ref[pl.ds(M, M), pl.ds(r * CX, CX)] = (field - high.astype(F32)).astype(BF16)

    for index, group in enumerate(groups):
        settle(sends[index], *group)

    wait_all(rf, ngx - 1, gx_recv)
    gathered = jnp.concatenate([rf[i] for i in range(ngx)], axis=0)
    lane32 = iota((2 * ngx, CX), 1)
    rows = jnp.concatenate(
        [jnp.where(lane32 < M, gathered, 0.0), jnp.where(lane32 < M, pltpu.roll(gathered, M, 1), 0.0)], axis=0
    )
    gram = jnp.dot(rows.T[0:M], rows, precision=lax.Precision.HIGHEST, preferred_element_type=F32)
    high, low = gram[0:32], pltpu.roll(gram[32:64], CX - 32, 1)
    across, along = iota((32, CX), 1), iota((32, CX), 0)
    square = jnp.where((across < 32) & (across > along), low, high)
    gram_ref[pl.ds(0, 16), :] = square[0:16] + pltpu.roll(square[16:32], M, 1)
    diagonal = jnp.sum(jnp.where(across == along, low, 0.0), axis=0, keepdims=True)
    gram_ref[pl.ds(16, 8), :] = jnp.where(iota((8, CX), 0) == 0, diagonal, 0.0)

    wait_all(rf, ngx - 1, gx_send)


def wait_all(buffer, count, sem):
    piece = buffer.at[pl.ds(0, count)]
    pltpu.make_async_copy(piece, piece, sem).wait()


def sum_kernel(ngy, part_ref, gram_ref, rz, rx, z_send, z_recv, x_send, x_recv):
    gy = lax.axis_index("gy")
    gx = lax.axis_index("gx")
    nz = ngy // NX4
    zpos = gy // NX4
    xpos = lax.rem(gy, NX4)
    z_partners = [(lax.rem(gy + NX4 * i, ngy), gx) for i in range(1, nz)]
    x_partners = [(zpos * NX4 + lax.rem(xpos + i, NX4), gx) for i in (2, 1, 3)]
    barrier = pltpu.get_barrier_semaphore()
    for partner in z_partners + x_partners:
        pl.semaphore_signal(barrier, inc=1, device_id=partner, device_id_type=MESH)
    rz[zpos] = part_ref[...]
    pl.semaphore_wait(barrier, nz + NX4 - 2)

    def wait_rows(buffer, count, sem):
        piece = buffer.at[pl.ds(0, count), pl.ds(0, 17)]
        pltpu.make_async_copy(piece, piece, sem).wait()

    def spread(buffer, slot, partners, send, recv):
        for partner in partners:
            pltpu.make_async_remote_copy(
                src_ref=buffer.at[slot, pl.ds(0, 17)], dst_ref=buffer.at[slot, pl.ds(0, 17)], send_sem=send, recv_sem=recv,
                device_id=partner, device_id_type=MESH,
            ).start()

    spread(rz, zpos, z_partners, z_send, z_recv)
    wait_rows(rz, nz - 1, z_recv)
    part = rz[0]
    for i in range(1, nz):
        part = part + rz[i]
    rx[xpos] = part
    spread(rx, xpos, x_partners, x_send, x_recv)
    wait_rows(rx, NX4 - 1, x_recv)
    gram_ref[...] = (rx[0] + rx[1]) + (rx[2] + rx[3])
    wait_rows(rz, nz - 1, z_send)
    wait_rows(rx, NX4 - 1, x_send)


def analysis_kernel(gram_ref, hilo_ref, mean_ref, out_hbm, rows_out, out_sem):
    lane = iota((8, CX), 1)
    sub = iota((8, CX), 0)
    packed = gram_ref[pl.ds(0, 16), :]
    square = jnp.concatenate([packed, pltpu.roll(packed, M, 1)], axis=0)
    square = jnp.where(iota((32, CX), 1) < M, square, 0.0)
    turned = jnp.concatenate([square, jnp.zeros((CX - 32, CX), F32)], axis=0).T
    across, along = iota((32, CX), 1), iota((32, CX), 0)
    top = jnp.where((across < 32) & (across > along), turned[0:32], square)
    corner = jnp.where(across > along, square, jnp.where(across == along, gram_ref[pl.ds(16, 1), :], turned[0:32]))
    corner = pltpu.roll(jnp.where(across < 32, corner, 0.0), 32, 1)
    bottom = jnp.where(across < 32, turned[32:64], corner)
    blocks = [top[8 * i:8 * i + 8] for i in range(4)] + [bottom[8 * i:8 * i + 8] for i in range(4)]
    blocks = [jnp.where(lane < M - 1, b, 0.0) for b in blocks]
    row_sums = [jnp.sum(b, axis=1, keepdims=True) for b in blocks]
    eyes = [lane == sub + 8 * i for i in range(8)]
    diagonals = [jnp.where(e, b, 0.0) for e, b in zip(eyes, blocks)]
    last = sub == 7
    target_row = blocks[7][7:8] + jnp.where(lane[0:1] == M - 1, -row_sums[7][7:8], 0.0)
    blocks[7] = jnp.where(last, 0.0, blocks[7])
    row_sums[7] = jnp.where(last[:, 0:1], 0.0, row_sums[7])
    col_sum = functools.reduce(jnp.add, blocks)
    col_sum = jnp.sum(col_sum, axis=0, keepdims=True)
    all_sum = jnp.sum(functools.reduce(jnp.add, row_sums), axis=0, keepdims=True)
    blocks = [jnp.where(lane == M - 1, -r, b) for b, r in zip(blocks, row_sums)]
    blocks[7] = jnp.where(last, jnp.where(lane == M - 1, all_sum, -col_sum), blocks[7])
    scale_row = jnp.sum(functools.reduce(jnp.add, diagonals), axis=0, keepdims=True)
    scale_row = lax.rsqrt((M - 1.0) + jnp.where(lane[0:1] == M - 1, all_sum, scale_row))
    scale_col = [jnp.sum(d, axis=1, keepdims=True) for d in diagonals]
    scale_col[7] = jnp.where(last[:, 0:1], all_sum, scale_col[7])
    scale_col = [lax.rsqrt((M - 1.0) + c) for c in scale_col]
    blocks = [jnp.where(e, b + (M - 1.0), b) for e, b in zip(eyes, blocks)]
    a = [
        jnp.where(lane == sub + (M + 8 * i), scale_col[i], jnp.where(lane < M, blocks[i] * scale_col[i] * scale_row, 0.0))
        for i in range(8)
    ]

    lower = [None] * 8
    nothing = 0.0 * packed[0:8]
    for p in range(16):
        b, o = p // 2, 4 * (p % 2)
        cols = {
            (t, i): jnp.broadcast_to(a[i][:, 4 * p + t:4 * p + t + 1], (8, CX)) for t in range(4) for i in range(b, 8)
        }
        cols = {key: v + nothing if key[1] == b else v for key, v in cols.items()}
        d = {
            (s, t): jnp.broadcast_to(cols[t, b][o + s:o + s + 1, :], (8, CX)) for s in range(4) for t in range(s + 1)
        }
        r = [jnp.broadcast_to(a[b][o + s:o + s + 1, :], (8, CX)) for s in range(4)]

        det = d[0, 0] * d[1, 1] - d[1, 0] * d[1, 0]
        inv = 1.0 / det
        i00, i10, i11 = d[1, 1] * inv, -d[1, 0] * inv, d[0, 0] * inv
        e00 = i00 * d[2, 0] + i10 * d[2, 1]
        e10 = i10 * d[2, 0] + i11 * d[2, 1]
        e01 = i00 * d[3, 0] + i10 * d[3, 1]
        e11 = i10 * d[3, 0] + i11 * d[3, 1]
        c00 = d[2, 2] - (d[2, 0] * e00 + d[2, 1] * e10)
        c10 = d[3, 2] - (d[3, 0] * e00 + d[3, 1] * e10)
        c11 = d[3, 3] - (d[3, 0] * e01 + d[3, 1] * e11)
        r2 = r[2] - (e00 * r[0] + e10 * r[1])
        r3 = r[3] - (e01 * r[0] + e11 * r[1])
        det2 = c00 * c11 - c10 * c10
        if p < 15:
            u0 = i00 * r[0] + i10 * r[1]
            u1 = i10 * r[0] + i11 * r[1]
            inv2 = 1.0 / det2
            z2 = (c11 * r2 - c10 * r3) * inv2
            z3 = (c00 * r3 - c10 * r2) * inv2
            z0 = u0 - (e00 * z2 + e01 * z3)
            z1 = u1 - (e10 * z2 + e11 * z3)
            z = (z0, z1, z2, z3)
            for i in range(b if o == 0 else b + 1, 8):
                update = (cols[0, i] * z[0] + cols[1, i] * z[1]) + (cols[2, i] * z[2] + cols[3, i] * z[3])
                new = a[i] - update
                a[i] = jnp.where(sub >= 4, new, a[i]) if i == b else new
        n0 = r[0] * lax.rsqrt(d[0, 0])
        n1 = (d[0, 0] * r[1] - d[1, 0] * r[0]) * lax.rsqrt(d[0, 0] * det)
        n2 = r2 * lax.rsqrt(c00)
        n3 = (c00 * r3 - c10 * r2) * lax.rsqrt(c00 * det2)
        rows = jnp.where(sub == o, n0, jnp.where(sub == o + 1, n1, jnp.where(sub == o + 2, n2, n3)))
        lower[b] = rows if o == 0 else jnp.where(sub >= 4, rows, lower[b])
    lower = [pltpu.roll(jnp.where(lane >= M, v, 0.0), M, 1) for v in lower]
    heads = [jnp.sum(v * target_row, axis=1, keepdims=True) for v in lower]
    weight = jnp.sum(functools.reduce(jnp.add, [v * h for v, h in zip(lower, heads)]), axis=0, keepdims=True)
    root = math.sqrt(M - 1.0)
    mix = jnp.concatenate([root * v + weight for v in lower], axis=0)
    high = mix.astype(BF16).astype(F32)
    low = mix - high
    pair = jnp.where(iota((M, CX), 1) < M, high, pltpu.roll(high, M, 1)).astype(BF16)
    low_pair = jnp.where(iota((M, CX), 1) < M, low, pltpu.roll(low, M, 1)).astype(BF16)
    left = jnp.concatenate([pair, low_pair], axis=1)
    for r in range(0, CY, 2):
        cols = pl.ds(r * CX, 2 * CX)
        block = hilo_ref[:, cols]
        right = jnp.concatenate([block, block], axis=0)
        res = jnp.dot(left, right, preferred_element_type=F32)
        for half in range(2):
            rows_out[r + half] = res[:, half * CX:(half + 1) * CX] + mean_ref[r + half:r + half + 1, :]
            pltpu.make_async_copy(rows_out.at[r + half], out_hbm.at[:, r + half, :], out_sem).start()
    pltpu.make_async_copy(rows_out, rows_out, out_sem).wait()


def near(array):
    return pltpu.with_memory_space_constraint(array, pltpu.VMEM)


def body(ngy, ngx, ensemble, flow, obs_cell, obs_value, obs_var):
    vmem = pl.BlockSpec(memory_space=pltpu.VMEM)
    hbm = pl.BlockSpec(memory_space=pl.ANY)
    dma = pltpu.SemaphoreType.DMA
    part, hilo, mean = pl.pallas_call(
        functools.partial(forecast_kernel, ngy, ngx),
        out_shape=(
            pltpu.VMEM((24, CX), F32),
            pltpu.VMEM((2 * M, CY * CX), BF16),
            pltpu.VMEM((CY, CX), F32),
        ),
        in_specs=[hbm] * 5,
        out_specs=(vmem,) * 3,
        scratch_shapes=[
            pltpu.VMEM((M, CY, CX), F32),
            pltpu.VMEM((CY + 2, M, CX), F32),
            pltpu.VMEM((CY + 2, M, CX), F32),
            pltpu.VMEM((CY, M, CX), F32),
            pltpu.VMEM((3, CY, CX), F32),
            pltpu.VMEM((5, CY, CX), F32),
            pltpu.SMEM((1, 1, 4), jnp.int32),
            pltpu.SMEM((2, 1, 1, 4), F32),
            pltpu.VMEM((16, CX), F32),
            pltpu.VMEM((2, 8, CX), F32),
            pltpu.VMEM((8, CX), F32),
            pltpu.VMEM((4, M, CX), F32),
            pltpu.VMEM((2, 16, CX), F32),
            pltpu.VMEM((4, 8, CX), F32),
            pltpu.VMEM((4, 8, CX), F32),
            pltpu.VMEM((2, 8, CX), F32),
            pltpu.VMEM((ngx, 2, CX), F32),
            dma((6,)), dma, dma((4,)), dma,
        ],
        compiler_params=pltpu.CompilerParams(collective_id=0, has_side_effects=True),
        name="forecast",
    )(ensemble, flow, obs_cell, obs_value, obs_var)
    gram = pl.pallas_call(
        functools.partial(sum_kernel, ngy),
        out_shape=pltpu.VMEM((24, CX), F32),
        in_specs=[vmem],
        out_specs=vmem,
        scratch_shapes=[
            pltpu.VMEM((ngy // NX4, 24, CX), F32),
            pltpu.VMEM((NX4, 24, CX), F32),
            dma, dma, dma, dma,
        ],
        compiler_params=pltpu.CompilerParams(collective_id=1, has_side_effects=True),
        name="sums",
    )(near(part))
    return pl.pallas_call(
        analysis_kernel,
        out_shape=jax.ShapeDtypeStruct((M, CY, CX), F32),
        in_specs=[vmem] * 3,
        out_specs=hbm,
        scratch_shapes=[pltpu.VMEM((CY, M, CX), F32), dma],
        name="analysis",
    )(near(gram), near(hilo), near(mean))


def solution(mesh):
    tile = P("gy", "gx", None)
    return jax.shard_map(
        functools.partial(body, mesh.shape["gy"], mesh.shape["gx"]),
        mesh=mesh,
        in_specs=(P(None, "gy", "gx"), P(None, "gy", "gx"), tile, tile, tile),
        out_specs=P(None, "gy", "gx"),
        check_vma=False,
    )
```

```python
import functools
import math

import jax
import jax.numpy as jnp
from jax import lax
from jax.experimental import pallas as pl
from jax.experimental.pallas import tpu as pltpu
from jax.sharding import PartitionSpec as P

MESH = pl.DeviceIdType.MESH
M = 64
CY = 8
CX = 128
F32 = jnp.float32
BF16 = jnp.bfloat16
NX4 = 4


def iota(shape, dim):
    return lax.broadcasted_iota(jnp.int32, shape, dim)


def step(x, n, s, w, e, k, hu, hv):
    return x + k * (n + s + w + e - 4.0 * x) - hu * (e - w) - hv * (s - n)


def forecast_kernel(
    ngy, ngx,
    x_hbm, flow_hbm, cell_hbm, val_hbm, var_hbm,
    gram_ref, hilo_ref, mean_ref,
    xb, xr, yr, zr, fl, cf, cells, obs, qs, fs, ct, h_rows, h_sides, h_corners, fh, zc, rf,
    load_sem, corner_send, halo_recv, gx_recv,
):
    gy = lax.axis_index("gy")
    gx = lax.axis_index("gx")
    up, down = gy - 1, gy + 1
    has_up, has_down = gy > 0, gy < ngy - 1
    left, right = lax.rem(gx + ngx - 1, ngx), lax.rem(gx + 1, ngx)
    gx_partners = [(gy, lax.rem(gx + i, ngx)) for i in sorted(range(1, ngx), key=lambda i: -min(i, ngx - i))]

    def load(src, dst, index):
        pltpu.make_async_copy(src, dst, load_sem.at[index]).start()

    def loaded(piece, index):
        pltpu.make_async_copy(piece, piece, load_sem.at[index]).wait()

    load(flow_hbm, fl, 0)
    for r in (0, 7, 1, 6):
        load(x_hbm.at[:, r, :], xr.at[r + 1], 1)
    load(x_hbm, xb, 2)
    for r in (2, 3, 4, 5):
        load(x_hbm.at[:, r, :], xr.at[r + 1], 3)
    load(cell_hbm, cells, 4)
    load(val_hbm, obs.at[0], 5)
    load(var_hbm, obs.at[1], 5)
    barrier = pltpu.get_barrier_semaphore()

    def greet(partners):
        for partner in partners:
            pl.semaphore_signal(barrier, inc=1, device_id=partner, device_id_type=MESH)

    @pl.when(has_up)
    def _():
        greet([(up, gx), (up, left), (up, right)])

    @pl.when(has_down)
    def _():
        greet([(down, gx), (down, left), (down, right)])

    greet(gx_partners)

    lane = iota((8, CX), 1)
    sub = iota((8, CX), 0)
    edge = (lane <= 1) | (lane >= CX - 2)
    s0, s7 = sub == 0, sub == 7
    l0, l127 = lane == 0, lane == CX - 1
    quad = lane & 3
    q0, q1, q3 = quad == 0, quad == 1, quad == 3
    west_side = quad >= 2

    sends = [load_sem.at[0], load_sem.at[2], load_sem.at[1], corner_send]
    gx_send = load_sem.at[3]

    def remote(src, dst, index, target):
        return pltpu.make_async_remote_copy(
            src_ref=src, dst_ref=dst, send_sem=sends[index], recv_sem=halo_recv.at[index],
            device_id=target, device_id_type=MESH,
        )

    def start(index, to_up, to_down, to_left=None, to_right=None):
        @pl.when(has_up)
        def _():
            for src, dst, target in to_up:
                remote(src, dst, index, (up, target)).start()

        @pl.when(has_down)
        def _():
            for src, dst, target in to_down:
                remote(src, dst, index, (down, target)).start()

        if to_left:
            remote(*to_left, index, (gy, left)).start()
            remote(*to_right, index, (gy, right)).start()

    both = has_up & has_down

    def settle(sem, buffer, most, least):
        def wait(count):
            piece = buffer.at[pl.ds(0, count)]
            pltpu.make_async_copy(piece, piece, sem).wait()

        if most == least:
            wait(most)
        else:
            pl.when(both)(lambda: wait(most))
            pl.when(jnp.logical_not(both))(lambda: wait(least))

    groups = [(fh, 4, 3), (h_sides, 2, 2), (h_rows, 4, 2), (h_corners, 4, 2)]

    def received(index):
        settle(halo_recv.at[index], *groups[index])

    loaded(fl, 0)
    qc = jnp.where(edge, fl[0], 0.0)
    for i in range(1, 3):
        qc = qc + pltpu.roll(jnp.where(edge, fl[i], 0.0), 4 * i, 1)
    fs[1] = qc
    for i in range(3):
        fs[0, pl.ds(i, 1), :] = fl[i, 0:1, :]
        fs[0, pl.ds(3 + i, 1), :] = fl[i, 7:8, :]
    loaded(xr.at[pl.ds(0, 4)], 1)

    ends = l0 | l127
    tile = jnp.zeros((8, CX), F32)
    for b in range(8):
        rows = pl.ds(8 * b, 8)
        tile = tile + pltpu.roll(jnp.where(ends, xr[1, rows, :], 0.0), 4 * b, 1)
        tile = tile + pltpu.roll(jnp.where(ends, xr[8, rows, :], 0.0), 4 * b + 2, 1)
    ct[...] = tile

    @pl.when(both)
    def _():
        pl.semaphore_wait(barrier, ngx + 5)

    @pl.when(jnp.logical_not(both))
    def _():
        pl.semaphore_wait(barrier, ngx + 2)

    start(
        3,
        [(ct, h_corners.at[3], left), (ct, h_corners.at[2], right)],
        [(ct, h_corners.at[1], left), (ct, h_corners.at[0], right)],
    )
    start(0, [(fs.at[0], fh.at[1], gx)], [(fs.at[0], fh.at[0], gx)], (fs.at[1], fh.at[2]), (fs.at[1], fh.at[3]))
    start(2, [(xr.at[pl.ds(1, 2)], h_rows.at[pl.ds(2, 2)], gx)], [(xr.at[pl.ds(7, 2)], h_rows.at[pl.ds(0, 2)], gx)])
    loaded(xb, 2)

    def pack(half):
        sums = [None] * 4
        for m in range(32):
            piece = pltpu.roll(jnp.where(edge, xb[half * 32 + m], 0.0), (CX - 4 * m) % CX, 1)
            sums[m % 4] = piece if m < 4 else sums[m % 4] + piece
        return (sums[0] + sums[1]) + (sums[2] + sums[3])

    qa, qb = pack(0), pack(1)
    qs[pl.ds(0, 8), :] = qa
    qs[pl.ds(8, 8), :] = qb
    start(1, [], [], (qs, h_sides.at[0]), (qs, h_sides.at[1]))
    loaded(xr.at[pl.ds(0, 4)], 3)
    loaded(cells, 4)
    loaded(obs, 5)

    def weights(f0, f1, f2):
        hu, hv = 0.5 * f1, 0.5 * f2
        return 1.0 - 4.0 * f0, f0 + hv, f0 - hv, f0 + hu, f0 - hu

    own = weights(fl[0], fl[1], fl[2])
    a0, an, as_, aw, ae = own
    aw_in, ae_in = jnp.where(l0, 0.0, aw), jnp.where(l127, 0.0, ae)
    for i, v in enumerate((a0, an, as_, aw_in, ae_in)):
        cf[i] = v

    blank = jnp.zeros((M, CX), F32)
    xr[0] = blank
    xr[9] = blank
    yr[0] = blank
    yr[9] = blank

    def inner(source, target, shift):
        def body(r, carry):
            c = [jnp.broadcast_to(cf[i, pl.ds(r, 1), :], (8, CX)) for i in range(5)]
            for b in range(8):
                rows = pl.ds(8 * b, 8)
                x = source[r + 1, rows, :]
                target[r + shift, rows, :] = (
                    (c[0] * x + c[1] * source[r, rows, :]) + (c[2] * source[r + 2, rows, :] + c[3] * pltpu.roll(x, 1, 1))
                    + c[4] * pltpu.roll(x, CX - 1, 1)
                )
            return carry
        lax.fori_loop(0, CY, body, 0)

    inner(xr, yr, 1)
    inner(yr, zr, 0)

    def col(v, l):
        return jnp.broadcast_to(v[:, l:l + 1], (8, CX))

    c_edge = jnp.where(q0, col(aw, 0), jnp.where(q3, col(ae, CX - 1), 0.0))
    a0_edge = jnp.where(q0, col(a0, 0), col(a0, CX - 1))
    an_edge = jnp.where(s0, 0.0, jnp.where(q0, col(an, 0), col(an, CX - 1)))
    as_edge = jnp.where(s7, 0.0, jnp.where(q0, col(as_, 0), col(as_, CX - 1)))
    c_next = jnp.where(q1, col(aw, 1), col(ae, CX - 2))

    has_left, has_right = gx > 0, gx < ngx - 1

    def on(flag):
        return jnp.full((8, CX), jnp.where(flag, 1, 0), jnp.int32) > 0

    cmask = (west_side & on(has_left)) | ((quad <= 1) & on(has_right))

    received(0)

    def flow_cols(i):
        west, east = col(fh[3], (4 * i - 1) % CX), col(fh[2], 4 * i)
        return jnp.where(cmask, jnp.where(west_side, west, east), 0.0)

    kc, uc, vc = flow_cols(0), 0.5 * flow_cols(1), 0.5 * flow_cols(2)

    def outer_row(tile, offset, flag):
        fields = [jnp.where(on(flag), jnp.broadcast_to(tile[offset + i:offset + i + 1, :], (8, CX)), 0.0) for i in range(3)]
        return weights(*fields)

    def line(v, r):
        return jnp.broadcast_to(v[r:r + 1, :], (8, CX))

    ends_in = (l0 & on(has_left)) | (l127 & on(has_right))

    def beside(i):
        return jnp.where(l0, pltpu.roll(fh[3], (1 - 4 * i) % CX, 1), pltpu.roll(fh[2], CX - 1 - 4 * i, 1))

    k_side, v_side = beside(0), 0.5 * beside(2)

    def outside(above):
        if above:
            t0, tn, ts, tw, te = outer_row(fh[0], 3, has_up)
            r, near, far, cross, toward = 0, line(an, 0), tn, ts, line(an, 1)
            side = line(k_side + v_side, 0)
        else:
            t0, tn, ts, tw, te = outer_row(fh[1], 0, has_down)
            r, near, far, cross, toward = 7, line(as_, 7), ts, tn, line(as_, 6)
            side = line(k_side - v_side, 7)
        west = near * jnp.where(l0, 0.0, tw) + line(aw_in, r) * pltpu.roll(near, 1, 1)
        east = near * jnp.where(l127, 0.0, te) + line(ae_in, r) * pltpu.roll(near, CX - 1, 1)
        corner = jnp.where(l0, near * tw + line(aw, r) * side, near * te + line(ae, r) * side)
        corner = jnp.where(ends_in, corner, 0.0)
        return near * (t0 + line(a0, r)), near * far, near * cross, west, east, toward * near, corner

    above = outside(True)
    below = outside(False)

    received(1)
    west_cell = q3
    for half in range(2):
        q = (qa, qb)[half]
        rows = pl.ds(8 * half, 8)
        ring = jnp.where(cmask, jnp.where(west_side, h_sides[1, rows, :], h_sides[0, rows, :]), 0.0)
        n = pltpu.roll(jnp.where(s7, 0.0, ring), 1, 0)
        s = pltpu.roll(jnp.where(s0, 0.0, ring), 7, 0)
        ring_w, ring_e = pltpu.roll(ring, 1, 1), pltpu.roll(ring, CX - 1, 1)
        w = jnp.where(west_cell, ring_w, pltpu.roll(q, 1, 1))
        e = jnp.where(west_cell, pltpu.roll(q, CX - 1, 1), ring_e)
        ring1 = step(ring, n, s, w, e, kc, uc, vc)
        x1 = jnp.where(q0, ring_w, ring_e)
        y1 = jnp.where(q0, pltpu.roll(ring1, 1, 1), pltpu.roll(ring1, CX - 1, 1))
        d = c_edge * x1
        at_edge = a0_edge * d + an_edge * pltpu.roll(d, 1, 0) + as_edge * pltpu.roll(d, 7, 0) + c_edge * y1
        inside = c_next * jnp.where(q1, pltpu.roll(d, 1, 1), pltpu.roll(d, CX - 1, 1))
        zc[half] = jnp.where(q0 | q3, at_edge, inside)

    received(2)
    received(3)

    def add_rows(flag, c, near_row, far_row, r, r_in, corners, first):
        @pl.when(flag)
        def _():
            merged = corners()
            for b in range(8):
                rows = pl.ds(8 * b, 8)
                p = h_rows[near_row, rows, :]
                zr[r, rows, :] = zr[r, rows, :] + (
                    (c[0] * p + c[1] * h_rows[far_row, rows, :]) + (c[2] * xr[r + 1, rows, :] + c[3] * pltpu.roll(p, 1, 1))
                    + (c[4] * pltpu.roll(p, CX - 1, 1) + c[6] * pltpu.roll(merged, (first - 4 * b) % CX, 1))
                )
                zr[r_in, rows, :] = zr[r_in, rows, :] + c[5] * p

    add_rows(has_up, above, 1, 0, 0, 1, lambda: jnp.where(q1, h_corners[0], pltpu.roll(h_corners[1], CX - 2, 1)), CX - 1)
    add_rows(has_down, below, 2, 3, 7, 6, lambda: jnp.where(q3, h_corners[2], pltpu.roll(h_corners[3], CX - 2, 1)), 1)

    def with_columns(r, b, lines):
        spread = pltpu.roll(lines[b // 4], 32 * (b % 4), 1, stride=4, stride_axis=0)
        return zr[r, 8 * b:8 * b + 8, :] + jnp.where(edge, spread, 0.0)

    def column_lines(r):
        return [jnp.broadcast_to(zc[half, pl.ds(r, 1), :], (8, CX)) for half in range(2)]

    lane64 = iota((M, CX), 1)
    diag64 = lane64 == iota((M, CX), 0)
    ones = jnp.zeros((1, CX), F32)
    picked = []
    for j in range(4):
        cell = cells[0, 0, j]
        row, place = lax.shift_right_logical(cell, 7), cell & (CX - 1)
        lines = column_lines(row)
        field = jnp.concatenate([with_columns(row, b, lines) for b in range(8)], axis=0)
        column = jnp.sum(jnp.where(lane64 == place, field, 0.0), axis=1, keepdims=True)
        column = jnp.broadcast_to(column, (M, CX))
        average = jnp.sum(column, axis=0, keepdims=True) * (1.0 / M)
        factor = lax.rsqrt(ones + obs[1, 0, 0, j])
        values = jnp.sum(jnp.where(diag64, column, 0.0), axis=0, keepdims=True)
        values = jnp.where(iota((1, CX), 1) < M - 1, values, ones + obs[0, 0, 0, j])
        picked.append(jnp.where(iota((1, CX), 1) < M, (values - average) * factor, 0.0))
    rf[gx] = jnp.concatenate(
        [picked[0] + pltpu.roll(picked[2], M, 1), picked[1] + pltpu.roll(picked[3], M, 1)], axis=0
    )

    gx_copies = [
        pltpu.make_async_remote_copy(
            src_ref=rf.at[gx], dst_ref=rf.at[gx], send_sem=gx_send, recv_sem=gx_recv,
            device_id=partner, device_id_type=MESH,
        )
        for partner in gx_partners
    ]
    for copy in gx_copies:
        copy.start()

    for r in range(CY):
        lines = column_lines(r)
        field = jnp.concatenate([with_columns(r, b, lines) for b in range(8)], axis=0)
        mean = jnp.sum(field, axis=0, keepdims=True) * (1.0 / M)
        mean_ref[pl.ds(r, 1), :] = mean
        field = field - mean
        high = field.astype(BF16)
        hilo_ref[pl.ds(0, M), pl.ds(r * CX, CX)] = high
        hilo_ref[pl.ds(M, M), pl.ds(r * CX, CX)] = (field - high.astype(F32)).astype(BF16)

    for index, group in enumerate(groups):
        settle(sends[index], *group)

    wait_all(rf, ngx - 1, gx_recv)
    gathered = jnp.concatenate([rf[i] for i in range(ngx)], axis=0)
    lane32 = iota((2 * ngx, CX), 1)
    rows = jnp.concatenate(
        [jnp.where(lane32 < M, gathered, 0.0), jnp.where(lane32 < M, pltpu.roll(gathered, M, 1), 0.0)], axis=0
    )
    gram = jnp.dot(rows.T[0:M], rows, precision=lax.Precision.HIGHEST, preferred_element_type=F32)
    high, low = gram[0:32], pltpu.roll(gram[32:64], CX - 32, 1)
    across, along = iota((32, CX), 1), iota((32, CX), 0)
    square = jnp.where((across < 32) & (across > along), low, high)
    gram_ref[pl.ds(0, 16), :] = square[0:16] + pltpu.roll(square[16:32], M, 1)
    diagonal = jnp.sum(jnp.where(across == along, low, 0.0), axis=0, keepdims=True)
    gram_ref[pl.ds(16, 8), :] = jnp.where(iota((8, CX), 0) == 0, diagonal, 0.0)

    wait_all(rf, ngx - 1, gx_send)


def wait_all(buffer, count, sem):
    piece = buffer.at[pl.ds(0, count)]
    pltpu.make_async_copy(piece, piece, sem).wait()


def sum_kernel(ngy, part_ref, gram_ref, rz, rx, z_send, z_recv, x_send, x_recv):
    gy = lax.axis_index("gy")
    gx = lax.axis_index("gx")
    nz = ngy // NX4
    zpos = gy // NX4
    xpos = lax.rem(gy, NX4)
    z_partners = [(lax.rem(gy + NX4 * i, ngy), gx) for i in range(1, nz)]
    x_partners = [(zpos * NX4 + lax.rem(xpos + i, NX4), gx) for i in (2, 1, 3)]
    barrier = pltpu.get_barrier_semaphore()
    for partner in z_partners + x_partners:
        pl.semaphore_signal(barrier, inc=1, device_id=partner, device_id_type=MESH)
    rz[zpos] = part_ref[...]
    pl.semaphore_wait(barrier, nz + NX4 - 2)

    def wait_rows(buffer, count, sem):
        piece = buffer.at[pl.ds(0, count), pl.ds(0, 17)]
        pltpu.make_async_copy(piece, piece, sem).wait()

    def spread(buffer, slot, partners, send, recv):
        for partner in partners:
            pltpu.make_async_remote_copy(
                src_ref=buffer.at[slot, pl.ds(0, 17)], dst_ref=buffer.at[slot, pl.ds(0, 17)], send_sem=send, recv_sem=recv,
                device_id=partner, device_id_type=MESH,
            ).start()

    spread(rz, zpos, z_partners, z_send, z_recv)
    wait_rows(rz, nz - 1, z_recv)
    part = rz[0]
    for i in range(1, nz):
        part = part + rz[i]
    rx[xpos] = part
    spread(rx, xpos, x_partners, x_send, x_recv)
    wait_rows(rx, NX4 - 1, x_recv)
    gram_ref[...] = (rx[0] + rx[1]) + (rx[2] + rx[3])
    wait_rows(rz, nz - 1, z_send)
    wait_rows(rx, NX4 - 1, x_send)


def analysis_kernel(gram_ref, hilo_ref, mean_ref, out_hbm, rows_out, out_sem):
    lane = iota((8, CX), 1)
    sub = iota((8, CX), 0)
    packed = gram_ref[pl.ds(0, 16), :]
    square = jnp.concatenate([packed, pltpu.roll(packed, M, 1)], axis=0)
    square = jnp.where(iota((32, CX), 1) < M, square, 0.0)
    turned = jnp.concatenate([square, jnp.zeros((CX - 32, CX), F32)], axis=0).T
    across, along = iota((32, CX), 1), iota((32, CX), 0)
    top = jnp.where((across < 32) & (across > along), turned[0:32], square)
    corner = jnp.where(across > along, square, jnp.where(across == along, gram_ref[pl.ds(16, 1), :], turned[0:32]))
    corner = pltpu.roll(jnp.where(across < 32, corner, 0.0), 32, 1)
    bottom = jnp.where(across < 32, turned[32:64], corner)
    blocks = [top[8 * i:8 * i + 8] for i in range(4)] + [bottom[8 * i:8 * i + 8] for i in range(4)]
    blocks = [jnp.where(lane < M - 1, b, 0.0) for b in blocks]
    row_sums = [jnp.sum(b, axis=1, keepdims=True) for b in blocks]
    eyes = [lane == sub + 8 * i for i in range(8)]
    diagonals = [jnp.where(e, b, 0.0) for e, b in zip(eyes, blocks)]
    last = sub == 7
    target_row = blocks[7][7:8] + jnp.where(lane[0:1] == M - 1, -row_sums[7][7:8], 0.0)
    blocks[7] = jnp.where(last, 0.0, blocks[7])
    row_sums[7] = jnp.where(last[:, 0:1], 0.0, row_sums[7])
    col_sum = functools.reduce(jnp.add, blocks)
    col_sum = jnp.sum(col_sum, axis=0, keepdims=True)
    all_sum = jnp.sum(functools.reduce(jnp.add, row_sums), axis=0, keepdims=True)
    blocks = [jnp.where(lane == M - 1, -r, b) for b, r in zip(blocks, row_sums)]
    blocks[7] = jnp.where(last, jnp.where(lane == M - 1, all_sum, -col_sum), blocks[7])
    scale_row = jnp.sum(functools.reduce(jnp.add, diagonals), axis=0, keepdims=True)
    scale_row = lax.rsqrt((M - 1.0) + jnp.where(lane[0:1] == M - 1, all_sum, scale_row))
    scale_col = [jnp.sum(d, axis=1, keepdims=True) for d in diagonals]
    scale_col[7] = jnp.where(last[:, 0:1], all_sum, scale_col[7])
    scale_col = [lax.rsqrt((M - 1.0) + c) for c in scale_col]
    blocks = [jnp.where(e, b + (M - 1.0), b) for e, b in zip(eyes, blocks)]
    a = [
        jnp.where(lane == sub + (M + 8 * i), scale_col[i], jnp.where(lane < M, blocks[i] * scale_col[i] * scale_row, 0.0))
        for i in range(8)
    ]

    lower = [None] * 8
    heads = []
    target_high = pltpu.roll(jnp.broadcast_to(target_row, (8, CX)), M, 1)
    nothing = 0.0 * packed[0:8]
    for p in range(16):
        b, o = p // 2, 4 * (p % 2)
        cols = {
            (t, i): jnp.broadcast_to(a[i][:, 4 * p + t:4 * p + t + 1], (8, CX)) for t in range(4) for i in range(b, 8)
        }
        cols = {key: v + nothing if key[1] == b else v for key, v in cols.items()}
        d = {
            (s, t): jnp.broadcast_to(cols[t, b][o + s:o + s + 1, :], (8, CX)) for s in range(4) for t in range(s + 1)
        }
        r = [jnp.broadcast_to(a[b][o + s:o + s + 1, :], (8, CX)) for s in range(4)]

        det = d[0, 0] * d[1, 1] - d[1, 0] * d[1, 0]
        inv = 1.0 / det
        f00 = d[1, 1] * d[2, 0] - d[1, 0] * d[2, 1]
        f10 = d[0, 0] * d[2, 1] - d[1, 0] * d[2, 0]
        f01 = d[1, 1] * d[3, 0] - d[1, 0] * d[3, 1]
        f11 = d[0, 0] * d[3, 1] - d[1, 0] * d[3, 0]
        g00 = det * d[2, 2] - (d[2, 0] * f00 + d[2, 1] * f10)
        g10 = det * d[3, 2] - (d[3, 0] * f00 + d[3, 1] * f10)
        g11 = det * d[3, 3] - (d[3, 0] * f01 + d[3, 1] * f11)
        det2 = g00 * g11 - g10 * g10
        i00, i10, i11 = d[1, 1] * inv, -d[1, 0] * inv, d[0, 0] * inv
        e00, e10, e01, e11 = f00 * inv, f10 * inv, f01 * inv, f11 * inv
        r2 = r[2] - (e00 * r[0] + e10 * r[1])
        r3 = r[3] - (e01 * r[0] + e11 * r[1])
        if p < 15:
            u0 = i00 * r[0] + i10 * r[1]
            u1 = i10 * r[0] + i11 * r[1]
            inv2 = det * (1.0 / det2)
            z2 = (g11 * r2 - g10 * r3) * inv2
            z3 = (g00 * r3 - g10 * r2) * inv2
            z0 = u0 - (e00 * z2 + e01 * z3)
            z1 = u1 - (e10 * z2 + e11 * z3)
            z = (z0, z1, z2, z3)
            for i in range(b if o == 0 else b + 1, 8):
                update = (cols[0, i] * z[0] + cols[1, i] * z[1]) + (cols[2, i] * z[2] + cols[3, i] * z[3])
                new = a[i] - update
                a[i] = jnp.where(sub >= 4, new, a[i]) if i == b else new
        n0 = r[0] * lax.rsqrt(d[0, 0])
        n1 = (d[0, 0] * r[1] - d[1, 0] * r[0]) * lax.rsqrt(d[0, 0] * det)
        c00, c10 = g00 * inv, g10 * inv
        n2 = r2 * lax.rsqrt(c00)
        n3 = (c00 * r3 - c10 * r2) * lax.rsqrt(c00 * (det2 * inv * inv))
        rows = jnp.where(sub == o, n0, jnp.where(sub == o + 1, n1, jnp.where(sub == o + 2, n2, n3)))
        lower[b] = rows if o == 0 else jnp.where(sub >= 4, rows, lower[b])
        if o:
            lower[b] = jnp.where(lane >= M, lower[b], 0.0)
            heads.append(jnp.sum(lower[b] * target_high, axis=1, keepdims=True))
    weight = jnp.sum(functools.reduce(jnp.add, [v * h for v, h in zip(lower, heads)]), axis=0, keepdims=True)
    root = math.sqrt(M - 1.0)
    mix = jnp.concatenate([root * v + weight for v in lower], axis=0)
    mix = jnp.where(iota((M, CX), 1) < M, pltpu.roll(mix, M, 1), mix)
    high = mix.astype(BF16)
    pair, low_pair = high, (mix - high.astype(F32)).astype(BF16)
    left = jnp.concatenate([pair, low_pair], axis=1)
    for r in range(0, CY, 2):
        cols = pl.ds(r * CX, 2 * CX)
        block = hilo_ref[:, cols]
        right = jnp.concatenate([block, block], axis=0)
        res = jnp.dot(left, right, preferred_element_type=F32)
        for half in range(2):
            rows_out[r + half] = res[:, half * CX:(half + 1) * CX] + mean_ref[r + half:r + half + 1, :]
            pltpu.make_async_copy(rows_out.at[r + half], out_hbm.at[:, r + half, :], out_sem).start()
    pltpu.make_async_copy(rows_out, rows_out, out_sem).wait()


def near(array):
    return pltpu.with_memory_space_constraint(array, pltpu.VMEM)


def body(ngy, ngx, ensemble, flow, obs_cell, obs_value, obs_var):
    vmem = pl.BlockSpec(memory_space=pltpu.VMEM)
    hbm = pl.BlockSpec(memory_space=pl.ANY)
    dma = pltpu.SemaphoreType.DMA
    part, hilo, mean = pl.pallas_call(
        functools.partial(forecast_kernel, ngy, ngx),
        out_shape=(
            pltpu.VMEM((24, CX), F32),
            pltpu.VMEM((2 * M, CY * CX), BF16),
            pltpu.VMEM((CY, CX), F32),
        ),
        in_specs=[hbm] * 5,
        out_specs=(vmem,) * 3,
        scratch_shapes=[
            pltpu.VMEM((M, CY, CX), F32),
            pltpu.VMEM((CY + 2, M, CX), F32),
            pltpu.VMEM((CY + 2, M, CX), F32),
            pltpu.VMEM((CY, M, CX), F32),
            pltpu.VMEM((3, CY, CX), F32),
            pltpu.VMEM((5, CY, CX), F32),
            pltpu.SMEM((1, 1, 4), jnp.int32),
            pltpu.SMEM((2, 1, 1, 4), F32),
            pltpu.VMEM((16, CX), F32),
            pltpu.VMEM((2, 8, CX), F32),
            pltpu.VMEM((8, CX), F32),
            pltpu.VMEM((4, M, CX), F32),
            pltpu.VMEM((2, 16, CX), F32),
            pltpu.VMEM((4, 8, CX), F32),
            pltpu.VMEM((4, 8, CX), F32),
            pltpu.VMEM((2, 8, CX), F32),
            pltpu.VMEM((ngx, 2, CX), F32),
            dma((6,)), dma, dma((4,)), dma,
        ],
        compiler_params=pltpu.CompilerParams(collective_id=0, has_side_effects=True),
        name="forecast",
    )(ensemble, flow, obs_cell, obs_value, obs_var)
    gram = pl.pallas_call(
        functools.partial(sum_kernel, ngy),
        out_shape=pltpu.VMEM((24, CX), F32),
        in_specs=[vmem],
        out_specs=vmem,
        scratch_shapes=[
            pltpu.VMEM((ngy // NX4, 24, CX), F32),
            pltpu.VMEM((NX4, 24, CX), F32),
            dma, dma, dma, dma,
        ],
        compiler_params=pltpu.CompilerParams(collective_id=1, has_side_effects=True),
        name="sums",
    )(near(part))
    return pl.pallas_call(
        analysis_kernel,
        out_shape=jax.ShapeDtypeStruct((M, CY, CX), F32),
        in_specs=[vmem] * 3,
        out_specs=hbm,
        scratch_shapes=[pltpu.VMEM((CY, M, CX), F32), dma],
        name="analysis",
    )(near(gram), near(hilo), near(mean))


def solution(mesh):
    tile = P("gy", "gx", None)
    return jax.shard_map(
        functools.partial(body, mesh.shape["gy"], mesh.shape["gx"]),
        mesh=mesh,
        in_specs=(P(None, "gy", "gx"), P(None, "gy", "gx"), tile, tile, tile),
        out_specs=P(None, "gy", "gx"),
        check_vma=False,
    )
```

```python
import functools
import math

import jax
import jax.numpy as jnp
from jax import lax
from jax.experimental import pallas as pl
from jax.experimental.pallas import tpu as pltpu
from jax.sharding import PartitionSpec as P

MESH = pl.DeviceIdType.MESH
M = 64
CY = 8
CX = 128
F32 = jnp.float32
BF16 = jnp.bfloat16
NX4 = 4


def iota(shape, dim):
    return lax.broadcasted_iota(jnp.int32, shape, dim)


def step(x, n, s, w, e, k, hu, hv):
    return x + k * (n + s + w + e - 4.0 * x) - hu * (e - w) - hv * (s - n)


def forecast_kernel(
    ngy, ngx,
    x_hbm, flow_hbm, cell_hbm, val_hbm, var_hbm,
    gram_ref, hilo_ref, mean_ref,
    xb, xr, yr, zr, fl, cf, cells, obs, qs, fs, ct, h_rows, h_sides, h_corners, fh, zc, rf,
    load_sem, corner_send, halo_recv, gx_recv,
):
    gy = lax.axis_index("gy")
    gx = lax.axis_index("gx")
    up, down = gy - 1, gy + 1
    has_up, has_down = gy > 0, gy < ngy - 1
    left, right = lax.rem(gx + ngx - 1, ngx), lax.rem(gx + 1, ngx)
    gx_partners = [(gy, lax.rem(gx + i, ngx)) for i in sorted(range(1, ngx), key=lambda i: -min(i, ngx - i))]

    def load(src, dst, index):
        pltpu.make_async_copy(src, dst, load_sem.at[index]).start()

    def loaded(piece, index):
        pltpu.make_async_copy(piece, piece, load_sem.at[index]).wait()

    load(flow_hbm, fl, 0)
    for r in (0, 7, 1, 6):
        load(x_hbm.at[:, r, :], xr.at[r + 1], 1)
    load(x_hbm, xb, 2)
    for r in (2, 3, 4, 5):
        load(x_hbm.at[:, r, :], xr.at[r + 1], 3)
    load(cell_hbm, cells, 4)
    load(val_hbm, obs.at[0], 5)
    load(var_hbm, obs.at[1], 5)
    barrier = pltpu.get_barrier_semaphore()

    def greet(partners):
        for partner in partners:
            pl.semaphore_signal(barrier, inc=1, device_id=partner, device_id_type=MESH)

    @pl.when(has_up)
    def _():
        greet([(up, gx), (up, left), (up, right)])

    @pl.when(has_down)
    def _():
        greet([(down, gx), (down, left), (down, right)])

    greet(gx_partners)

    lane = iota((8, CX), 1)
    sub = iota((8, CX), 0)
    edge = (lane <= 1) | (lane >= CX - 2)
    s0, s7 = sub == 0, sub == 7
    l0, l127 = lane == 0, lane == CX - 1
    quad = lane & 3
    q0, q1, q3 = quad == 0, quad == 1, quad == 3
    west_side = quad >= 2

    sends = [load_sem.at[0], load_sem.at[2], load_sem.at[1], corner_send]
    gx_send = load_sem.at[3]

    def remote(src, dst, index, target):
        return pltpu.make_async_remote_copy(
            src_ref=src, dst_ref=dst, send_sem=sends[index], recv_sem=halo_recv.at[index],
            device_id=target, device_id_type=MESH,
        )

    def start(index, to_up, to_down, to_left=None, to_right=None):
        @pl.when(has_up)
        def _():
            for src, dst, target in to_up:
                remote(src, dst, index, (up, target)).start()

        @pl.when(has_down)
        def _():
            for src, dst, target in to_down:
                remote(src, dst, index, (down, target)).start()

        if to_left:
            remote(*to_left, index, (gy, left)).start()
            remote(*to_right, index, (gy, right)).start()

    both = has_up & has_down

    def settle(sem, buffer, most, least):
        def wait(count):
            piece = buffer.at[pl.ds(0, count)]
            pltpu.make_async_copy(piece, piece, sem).wait()

        if most == least:
            wait(most)
        else:
            pl.when(both)(lambda: wait(most))
            pl.when(jnp.logical_not(both))(lambda: wait(least))

    groups = [(fh, 4, 3), (h_sides, 2, 2), (h_rows, 4, 2), (h_corners, 4, 2)]

    def received(index):
        settle(halo_recv.at[index], *groups[index])

    loaded(fl, 0)
    qc = jnp.where(edge, fl[0], 0.0)
    for i in range(1, 3):
        qc = qc + pltpu.roll(jnp.where(edge, fl[i], 0.0), 4 * i, 1)
    fs[1] = qc
    for i in range(3):
        fs[0, pl.ds(i, 1), :] = fl[i, 0:1, :]
        fs[0, pl.ds(3 + i, 1), :] = fl[i, 7:8, :]
    loaded(xr.at[pl.ds(0, 4)], 1)

    ends = l0 | l127
    tile = jnp.zeros((8, CX), F32)
    for b in range(8):
        rows = pl.ds(8 * b, 8)
        tile = tile + pltpu.roll(jnp.where(ends, xr[1, rows, :], 0.0), 4 * b, 1)
        tile = tile + pltpu.roll(jnp.where(ends, xr[8, rows, :], 0.0), 4 * b + 2, 1)
    ct[...] = tile

    @pl.when(both)
    def _():
        pl.semaphore_wait(barrier, ngx + 5)

    @pl.when(jnp.logical_not(both))
    def _():
        pl.semaphore_wait(barrier, ngx + 2)

    start(
        3,
        [(ct, h_corners.at[3], left), (ct, h_corners.at[2], right)],
        [(ct, h_corners.at[1], left), (ct, h_corners.at[0], right)],
    )
    start(0, [(fs.at[0], fh.at[1], gx)], [(fs.at[0], fh.at[0], gx)], (fs.at[1], fh.at[2]), (fs.at[1], fh.at[3]))
    start(2, [(xr.at[pl.ds(1, 2)], h_rows.at[pl.ds(2, 2)], gx)], [(xr.at[pl.ds(7, 2)], h_rows.at[pl.ds(0, 2)], gx)])
    loaded(xb, 2)

    def pack(half):
        sums = [None] * 4
        for m in range(32):
            piece = pltpu.roll(jnp.where(edge, xb[half * 32 + m], 0.0), (CX - 4 * m) % CX, 1)
            sums[m % 4] = piece if m < 4 else sums[m % 4] + piece
        return (sums[0] + sums[1]) + (sums[2] + sums[3])

    qa, qb = pack(0), pack(1)
    qs[pl.ds(0, 8), :] = qa
    qs[pl.ds(8, 8), :] = qb
    start(1, [], [], (qs, h_sides.at[0]), (qs, h_sides.at[1]))
    loaded(xr.at[pl.ds(0, 4)], 3)
    loaded(cells, 4)
    loaded(obs, 5)

    def weights(f0, f1, f2):
        hu, hv = 0.5 * f1, 0.5 * f2
        return 1.0 - 4.0 * f0, f0 + hv, f0 - hv, f0 + hu, f0 - hu

    own = weights(fl[0], fl[1], fl[2])
    a0, an, as_, aw, ae = own
    aw_in, ae_in = jnp.where(l0, 0.0, aw), jnp.where(l127, 0.0, ae)
    for i, v in enumerate((a0, an, as_, aw_in, ae_in)):
        cf[i] = v

    blank = jnp.zeros((M, CX), F32)
    xr[0] = blank
    xr[9] = blank
    yr[0] = blank
    yr[9] = blank

    def inner(source, target, shift):
        def body(r, carry):
            c = [jnp.broadcast_to(cf[i, pl.ds(r, 1), :], (8, CX)) for i in range(5)]
            for b in range(8):
                rows = pl.ds(8 * b, 8)
                x = source[r + 1, rows, :]
                target[r + shift, rows, :] = (
                    (c[0] * x + c[1] * source[r, rows, :]) + (c[2] * source[r + 2, rows, :] + c[3] * pltpu.roll(x, 1, 1))
                    + c[4] * pltpu.roll(x, CX - 1, 1)
                )
            return carry
        lax.fori_loop(0, CY, body, 0)

    inner(xr, yr, 1)
    inner(yr, zr, 0)

    def col(v, l):
        return jnp.broadcast_to(v[:, l:l + 1], (8, CX))

    c_edge = jnp.where(q0, col(aw, 0), jnp.where(q3, col(ae, CX - 1), 0.0))
    a0_edge = jnp.where(q0, col(a0, 0), col(a0, CX - 1))
    an_edge = jnp.where(s0, 0.0, jnp.where(q0, col(an, 0), col(an, CX - 1)))
    as_edge = jnp.where(s7, 0.0, jnp.where(q0, col(as_, 0), col(as_, CX - 1)))
    c_next = jnp.where(q1, col(aw, 1), col(ae, CX - 2))

    has_left, has_right = gx > 0, gx < ngx - 1

    def on(flag):
        return jnp.full((8, CX), jnp.where(flag, 1, 0), jnp.int32) > 0

    cmask = (west_side & on(has_left)) | ((quad <= 1) & on(has_right))

    received(0)

    def flow_cols(i):
        west, east = col(fh[3], (4 * i - 1) % CX), col(fh[2], 4 * i)
        return jnp.where(cmask, jnp.where(west_side, west, east), 0.0)

    kc, uc, vc = flow_cols(0), 0.5 * flow_cols(1), 0.5 * flow_cols(2)

    def outer_row(tile, offset, flag):
        fields = [jnp.where(on(flag), jnp.broadcast_to(tile[offset + i:offset + i + 1, :], (8, CX)), 0.0) for i in range(3)]
        return weights(*fields)

    def line(v, r):
        return jnp.broadcast_to(v[r:r + 1, :], (8, CX))

    ends_in = (l0 & on(has_left)) | (l127 & on(has_right))

    def beside(i):
        return jnp.where(l0, pltpu.roll(fh[3], (1 - 4 * i) % CX, 1), pltpu.roll(fh[2], CX - 1 - 4 * i, 1))

    k_side, v_side = beside(0), 0.5 * beside(2)

    def outside(above):
        if above:
            t0, tn, ts, tw, te = outer_row(fh[0], 3, has_up)
            r, near, far, cross, toward = 0, line(an, 0), tn, ts, line(an, 1)
            side = line(k_side + v_side, 0)
        else:
            t0, tn, ts, tw, te = outer_row(fh[1], 0, has_down)
            r, near, far, cross, toward = 7, line(as_, 7), ts, tn, line(as_, 6)
            side = line(k_side - v_side, 7)
        west = near * jnp.where(l0, 0.0, tw) + line(aw_in, r) * pltpu.roll(near, 1, 1)
        east = near * jnp.where(l127, 0.0, te) + line(ae_in, r) * pltpu.roll(near, CX - 1, 1)
        corner = jnp.where(l0, near * tw + line(aw, r) * side, near * te + line(ae, r) * side)
        corner = jnp.where(ends_in, corner, 0.0)
        return near * (t0 + line(a0, r)), near * far, near * cross, west, east, toward * near, corner

    above = outside(True)
    below = outside(False)

    received(1)
    west_cell = q3
    for half in range(2):
        q = (qa, qb)[half]
        rows = pl.ds(8 * half, 8)
        ring = jnp.where(cmask, jnp.where(west_side, h_sides[1, rows, :], h_sides[0, rows, :]), 0.0)
        n = pltpu.roll(jnp.where(s7, 0.0, ring), 1, 0)
        s = pltpu.roll(jnp.where(s0, 0.0, ring), 7, 0)
        ring_w, ring_e = pltpu.roll(ring, 1, 1), pltpu.roll(ring, CX - 1, 1)
        w = jnp.where(west_cell, ring_w, pltpu.roll(q, 1, 1))
        e = jnp.where(west_cell, pltpu.roll(q, CX - 1, 1), ring_e)
        ring1 = step(ring, n, s, w, e, kc, uc, vc)
        x1 = jnp.where(q0, ring_w, ring_e)
        y1 = jnp.where(q0, pltpu.roll(ring1, 1, 1), pltpu.roll(ring1, CX - 1, 1))
        d = c_edge * x1
        at_edge = a0_edge * d + an_edge * pltpu.roll(d, 1, 0) + as_edge * pltpu.roll(d, 7, 0) + c_edge * y1
        inside = c_next * jnp.where(q1, pltpu.roll(d, 1, 1), pltpu.roll(d, CX - 1, 1))
        zc[half] = jnp.where(q0 | q3, at_edge, inside)

    received(2)
    received(3)

    def add_rows(flag, c, near_row, far_row, r, r_in, corners, first):
        @pl.when(flag)
        def _():
            merged = corners()
            for b in range(8):
                rows = pl.ds(8 * b, 8)
                p = h_rows[near_row, rows, :]
                zr[r, rows, :] = zr[r, rows, :] + (
                    (c[0] * p + c[1] * h_rows[far_row, rows, :]) + (c[2] * xr[r + 1, rows, :] + c[3] * pltpu.roll(p, 1, 1))
                    + (c[4] * pltpu.roll(p, CX - 1, 1) + c[6] * pltpu.roll(merged, (first - 4 * b) % CX, 1))
                )
                zr[r_in, rows, :] = zr[r_in, rows, :] + c[5] * p

    add_rows(has_up, above, 1, 0, 0, 1, lambda: jnp.where(q1, h_corners[0], pltpu.roll(h_corners[1], CX - 2, 1)), CX - 1)
    add_rows(has_down, below, 2, 3, 7, 6, lambda: jnp.where(q3, h_corners[2], pltpu.roll(h_corners[3], CX - 2, 1)), 1)

    def with_columns(r, b, lines):
        spread = pltpu.roll(lines[b // 4], 32 * (b % 4), 1, stride=4, stride_axis=0)
        return zr[r, 8 * b:8 * b + 8, :] + jnp.where(edge, spread, 0.0)

    def column_lines(r):
        return [jnp.broadcast_to(zc[half, pl.ds(r, 1), :], (8, CX)) for half in range(2)]

    lane64 = iota((M, CX), 1)
    diag64 = lane64 == iota((M, CX), 0)
    ones = jnp.zeros((1, CX), F32)
    picked = []
    for j in range(4):
        cell = cells[0, 0, j]
        row, place = lax.shift_right_logical(cell, 7), cell & (CX - 1)
        lines = column_lines(row)
        field = jnp.concatenate([with_columns(row, b, lines) for b in range(8)], axis=0)
        column = jnp.sum(jnp.where(lane64 == place, field, 0.0), axis=1, keepdims=True)
        column = jnp.broadcast_to(column, (M, CX))
        average = jnp.sum(column, axis=0, keepdims=True) * (1.0 / M)
        factor = lax.rsqrt(ones + obs[1, 0, 0, j])
        values = jnp.sum(jnp.where(diag64, column, 0.0), axis=0, keepdims=True)
        values = jnp.where(iota((1, CX), 1) < M - 1, values, ones + obs[0, 0, 0, j])
        picked.append(jnp.where(iota((1, CX), 1) < M, (values - average) * factor, 0.0))
    rf[gx] = jnp.concatenate(
        [picked[0] + pltpu.roll(picked[2], M, 1), picked[1] + pltpu.roll(picked[3], M, 1)], axis=0
    )

    gx_copies = [
        pltpu.make_async_remote_copy(
            src_ref=rf.at[gx], dst_ref=rf.at[gx], send_sem=gx_send, recv_sem=gx_recv,
            device_id=partner, device_id_type=MESH,
        )
        for partner in gx_partners
    ]
    for copy in gx_copies:
        copy.start()

    for r in range(CY):
        lines = column_lines(r)
        field = jnp.concatenate([with_columns(r, b, lines) for b in range(8)], axis=0)
        mean = jnp.sum(field, axis=0, keepdims=True) * (1.0 / M)
        mean_ref[pl.ds(r, 1), :] = mean
        field = field - mean
        high = field.astype(BF16)
        hilo_ref[pl.ds(0, M), pl.ds(r * CX, CX)] = high
        hilo_ref[pl.ds(M, M), pl.ds(r * CX, CX)] = (field - high.astype(F32)).astype(BF16)

    for index, group in enumerate(groups):
        settle(sends[index], *group)

    wait_all(rf, ngx - 1, gx_recv)
    gathered = jnp.concatenate([rf[i] for i in range(ngx)], axis=0)
    lane32 = iota((2 * ngx, CX), 1)
    rows = jnp.concatenate(
        [jnp.where(lane32 < M, gathered, 0.0), jnp.where(lane32 < M, pltpu.roll(gathered, M, 1), 0.0)], axis=0
    )
    gram = jnp.dot(rows.T[0:M], rows, precision=lax.Precision.HIGHEST, preferred_element_type=F32)
    high, low = gram[0:32], pltpu.roll(gram[32:64], CX - 32, 1)
    across, along = iota((32, CX), 1), iota((32, CX), 0)
    square = jnp.where((across < 32) & (across > along), low, high)
    gram_ref[pl.ds(0, 16), :] = square[0:16] + pltpu.roll(square[16:32], M, 1)
    diagonal = jnp.sum(jnp.where(across == along, low, 0.0), axis=0, keepdims=True)
    gram_ref[pl.ds(16, 8), :] = jnp.where(iota((8, CX), 0) == 0, diagonal, 0.0)

    wait_all(rf, ngx - 1, gx_send)


def wait_all(buffer, count, sem):
    piece = buffer.at[pl.ds(0, count)]
    pltpu.make_async_copy(piece, piece, sem).wait()


def sum_kernel(ngy, part_ref, gram_ref, rz, rx, z_send, z_recv, x_send, x_recv):
    gy = lax.axis_index("gy")
    gx = lax.axis_index("gx")
    nz = ngy // NX4
    zpos = gy // NX4
    xpos = lax.rem(gy, NX4)
    z_partners = [(lax.rem(gy + NX4 * i, ngy), gx) for i in sorted(range(1, nz), key=lambda i: -min(i, nz - i))]
    x_partners = [(zpos * NX4 + lax.rem(xpos + i, NX4), gx) for i in (2, 1, 3)]
    barrier = pltpu.get_barrier_semaphore()
    for partner in z_partners + x_partners:
        pl.semaphore_signal(barrier, inc=1, device_id=partner, device_id_type=MESH)
    rz[zpos] = part_ref[...]
    pl.semaphore_wait(barrier, nz + NX4 - 2)

    def wait_rows(buffer, count, sem):
        piece = buffer.at[pl.ds(0, count), pl.ds(0, 17)]
        pltpu.make_async_copy(piece, piece, sem).wait()

    def spread(buffer, slot, partners, send, recv):
        for partner in partners:
            pltpu.make_async_remote_copy(
                src_ref=buffer.at[slot, pl.ds(0, 17)], dst_ref=buffer.at[slot, pl.ds(0, 17)], send_sem=send, recv_sem=recv,
                device_id=partner, device_id_type=MESH,
            ).start()

    spread(rz, zpos, z_partners, z_send, z_recv)
    wait_rows(rz, nz - 1, z_recv)
    part = rz[0]
    for i in range(1, nz):
        part = part + rz[i]
    rx[xpos] = part
    spread(rx, xpos, x_partners, x_send, x_recv)
    wait_rows(rx, NX4 - 1, x_recv)
    gram_ref[...] = (rx[0] + rx[1]) + (rx[2] + rx[3])
    wait_rows(rz, nz - 1, z_send)
    wait_rows(rx, NX4 - 1, x_send)


def analysis_kernel(gram_ref, hilo_ref, mean_ref, out_hbm, rows_out, out_sem):
    lane = iota((8, CX), 1)
    sub = iota((8, CX), 0)
    packed = gram_ref[pl.ds(0, 16), :]
    square = jnp.concatenate([packed, pltpu.roll(packed, M, 1)], axis=0)
    square = jnp.where(iota((32, CX), 1) < M, square, 0.0)
    turned = jnp.concatenate([square, jnp.zeros((CX - 32, CX), F32)], axis=0).T
    across, along = iota((32, CX), 1), iota((32, CX), 0)
    top = jnp.where((across < 32) & (across > along), turned[0:32], square)
    corner = jnp.where(across > along, square, jnp.where(across == along, gram_ref[pl.ds(16, 1), :], turned[0:32]))
    corner = pltpu.roll(jnp.where(across < 32, corner, 0.0), 32, 1)
    bottom = jnp.where(across < 32, turned[32:64], corner)
    blocks = [top[8 * i:8 * i + 8] for i in range(4)] + [bottom[8 * i:8 * i + 8] for i in range(4)]
    blocks = [jnp.where(lane < M - 1, b, 0.0) for b in blocks]
    row_sums = [jnp.sum(b, axis=1, keepdims=True) for b in blocks]
    eyes = [lane == sub + 8 * i for i in range(8)]
    diagonals = [jnp.where(e, b, 0.0) for e, b in zip(eyes, blocks)]
    last = sub == 7
    target_row = blocks[7][7:8] + jnp.where(lane[0:1] == M - 1, -row_sums[7][7:8], 0.0)
    blocks[7] = jnp.where(last, 0.0, blocks[7])
    row_sums[7] = jnp.where(last[:, 0:1], 0.0, row_sums[7])
    col_sum = functools.reduce(jnp.add, blocks)
    col_sum = jnp.sum(col_sum, axis=0, keepdims=True)
    all_sum = jnp.sum(functools.reduce(jnp.add, row_sums), axis=0, keepdims=True)
    blocks = [jnp.where(lane == M - 1, -r, b) for b, r in zip(blocks, row_sums)]
    blocks[7] = jnp.where(last, jnp.where(lane == M - 1, all_sum, -col_sum), blocks[7])
    scale_row = jnp.sum(functools.reduce(jnp.add, diagonals), axis=0, keepdims=True)
    scale_row = lax.rsqrt((M - 1.0) + jnp.where(lane[0:1] == M - 1, all_sum, scale_row))
    scale_col = [jnp.sum(d, axis=1, keepdims=True) for d in diagonals]
    scale_col[7] = jnp.where(last[:, 0:1], all_sum, scale_col[7])
    scale_col = [lax.rsqrt((M - 1.0) + c) for c in scale_col]
    blocks = [jnp.where(e, b + (M - 1.0), b) for e, b in zip(eyes, blocks)]
    a = [
        jnp.where(lane == sub + (M + 8 * i), scale_col[i], jnp.where(lane < M, blocks[i] * scale_col[i] * scale_row, 0.0))
        for i in range(8)
    ]

    lower = [None] * 8
    heads = []
    target_high = pltpu.roll(jnp.broadcast_to(target_row, (8, CX)), M, 1)
    nothing = 0.0 * packed[0:8]
    for p in range(16):
        b, o = p // 2, 4 * (p % 2)
        cols = {
            (t, i): jnp.broadcast_to(a[i][:, 4 * p + t:4 * p + t + 1], (8, CX)) for t in range(4) for i in range(b, 8)
        }
        cols = {key: v + nothing if key[1] == b else v for key, v in cols.items()}
        d = {
            (s, t): jnp.broadcast_to(cols[t, b][o + s:o + s + 1, :], (8, CX)) for s in range(4) for t in range(s + 1)
        }
        r = [jnp.broadcast_to(a[b][o + s:o + s + 1, :], (8, CX)) for s in range(4)]

        det = d[0, 0] * d[1, 1] - d[1, 0] * d[1, 0]
        inv = 1.0 / det
        f00 = d[1, 1] * d[2, 0] - d[1, 0] * d[2, 1]
        f10 = d[0, 0] * d[2, 1] - d[1, 0] * d[2, 0]
        f01 = d[1, 1] * d[3, 0] - d[1, 0] * d[3, 1]
        f11 = d[0, 0] * d[3, 1] - d[1, 0] * d[3, 0]
        g00 = det * d[2, 2] - (d[2, 0] * f00 + d[2, 1] * f10)
        g10 = det * d[3, 2] - (d[3, 0] * f00 + d[3, 1] * f10)
        g11 = det * d[3, 3] - (d[3, 0] * f01 + d[3, 1] * f11)
        det2 = g00 * g11 - g10 * g10
        i00, i10, i11 = d[1, 1] * inv, -d[1, 0] * inv, d[0, 0] * inv
        e00, e10, e01, e11 = f00 * inv, f10 * inv, f01 * inv, f11 * inv
        r2 = r[2] - (e00 * r[0] + e10 * r[1])
        r3 = r[3] - (e01 * r[0] + e11 * r[1])
        if p < 15:
            u0 = i00 * r[0] + i10 * r[1]
            u1 = i10 * r[0] + i11 * r[1]
            inv2 = det * (1.0 / det2)
            t2, t3 = g11 * r2 - g10 * r3, g00 * r3 - g10 * r2
            z2, z3 = t2 * inv2, t3 * inv2
            z0 = u0 - (e00 * z2 + e01 * z3)
            z1 = u1 - (e10 * z2 + e11 * z3)
            z = (z0, z1, z2, z3)
            for i in range(b if o == 0 else b + 1, 8):
                if i == (b if o == 0 else b + 1):
                    m2 = cols[2, i] - (cols[0, i] * e00 + cols[1, i] * e10)
                    m3 = cols[3, i] - (cols[0, i] * e01 + cols[1, i] * e11)
                    new = (a[i] - (cols[0, i] * u0 + cols[1, i] * u1)) - inv2 * (m2 * t2 + m3 * t3)
                else:
                    new = a[i] - ((cols[0, i] * z[0] + cols[1, i] * z[1]) + (cols[2, i] * z[2] + cols[3, i] * z[3]))
                a[i] = jnp.where(sub >= 4, new, a[i]) if i == b else new
        n0 = r[0] * lax.rsqrt(d[0, 0])
        n1 = (d[0, 0] * r[1] - d[1, 0] * r[0]) * lax.rsqrt(d[0, 0] * det)
        c00, c10 = g00 * inv, g10 * inv
        n2 = r2 * lax.rsqrt(c00)
        n3 = (c00 * r3 - c10 * r2) * lax.rsqrt(c00 * (det2 * inv * inv))
        rows = jnp.where(sub == o, n0, jnp.where(sub == o + 1, n1, jnp.where(sub == o + 2, n2, n3)))
        lower[b] = rows if o == 0 else jnp.where(sub >= 4, rows, lower[b])
        if o:
            lower[b] = jnp.where(lane >= M, lower[b], 0.0)
            heads.append(jnp.sum(lower[b] * target_high, axis=1, keepdims=True))
    weight = jnp.sum(functools.reduce(jnp.add, [v * h for v, h in zip(lower, heads)]), axis=0, keepdims=True)
    root = math.sqrt(M - 1.0)
    mix = jnp.concatenate([root * v + weight for v in lower], axis=0)
    mix = jnp.where(iota((M, CX), 1) < M, pltpu.roll(mix, M, 1), mix)
    high = mix.astype(BF16)
    pair, low_pair = high, (mix - high.astype(F32)).astype(BF16)
    left = jnp.concatenate([pair, low_pair], axis=1)
    for r in range(0, CY, 2):
        cols = pl.ds(r * CX, 2 * CX)
        block = hilo_ref[:, cols]
        right = jnp.concatenate([block, block], axis=0)
        res = jnp.dot(left, right, preferred_element_type=F32)
        for half in range(2):
            rows_out[r + half] = res[:, half * CX:(half + 1) * CX] + mean_ref[r + half:r + half + 1, :]
            pltpu.make_async_copy(rows_out.at[r + half], out_hbm.at[:, r + half, :], out_sem).start()
    pltpu.make_async_copy(rows_out, rows_out, out_sem).wait()


def near(array):
    return pltpu.with_memory_space_constraint(array, pltpu.VMEM)


def body(ngy, ngx, ensemble, flow, obs_cell, obs_value, obs_var):
    vmem = pl.BlockSpec(memory_space=pltpu.VMEM)
    hbm = pl.BlockSpec(memory_space=pl.ANY)
    dma = pltpu.SemaphoreType.DMA
    part, hilo, mean = pl.pallas_call(
        functools.partial(forecast_kernel, ngy, ngx),
        out_shape=(
            pltpu.VMEM((24, CX), F32),
            pltpu.VMEM((2 * M, CY * CX), BF16),
            pltpu.VMEM((CY, CX), F32),
        ),
        in_specs=[hbm] * 5,
        out_specs=(vmem,) * 3,
        scratch_shapes=[
            pltpu.VMEM((M, CY, CX), F32),
            pltpu.VMEM((CY + 2, M, CX), F32),
            pltpu.VMEM((CY + 2, M, CX), F32),
            pltpu.VMEM((CY, M, CX), F32),
            pltpu.VMEM((3, CY, CX), F32),
            pltpu.VMEM((5, CY, CX), F32),
            pltpu.SMEM((1, 1, 4), jnp.int32),
            pltpu.SMEM((2, 1, 1, 4), F32),
            pltpu.VMEM((16, CX), F32),
            pltpu.VMEM((2, 8, CX), F32),
            pltpu.VMEM((8, CX), F32),
            pltpu.VMEM((4, M, CX), F32),
            pltpu.VMEM((2, 16, CX), F32),
            pltpu.VMEM((4, 8, CX), F32),
            pltpu.VMEM((4, 8, CX), F32),
            pltpu.VMEM((2, 8, CX), F32),
            pltpu.VMEM((ngx, 2, CX), F32),
            dma((6,)), dma, dma((4,)), dma,
        ],
        compiler_params=pltpu.CompilerParams(collective_id=0, has_side_effects=True),
        name="forecast",
    )(ensemble, flow, obs_cell, obs_value, obs_var)
    gram = pl.pallas_call(
        functools.partial(sum_kernel, ngy),
        out_shape=pltpu.VMEM((24, CX), F32),
        in_specs=[vmem],
        out_specs=vmem,
        scratch_shapes=[
            pltpu.VMEM((ngy // NX4, 24, CX), F32),
            pltpu.VMEM((NX4, 24, CX), F32),
            dma, dma, dma, dma,
        ],
        compiler_params=pltpu.CompilerParams(collective_id=1, has_side_effects=True),
        name="sums",
    )(near(part))
    return pl.pallas_call(
        analysis_kernel,
        out_shape=jax.ShapeDtypeStruct((M, CY, CX), F32),
        in_specs=[vmem] * 3,
        out_specs=hbm,
        scratch_shapes=[pltpu.VMEM((CY, M, CX), F32), dma],
        name="analysis",
    )(near(gram), near(hilo), near(mean))


def solution(mesh):
    tile = P("gy", "gx", None)
    return jax.shard_map(
        functools.partial(body, mesh.shape["gy"], mesh.shape["gx"]),
        mesh=mesh,
        in_specs=(P(None, "gy", "gx"), P(None, "gy", "gx"), tile, tile, tile),
        out_specs=P(None, "gy", "gx"),
        check_vma=False,
    )
```

```python
import functools
import math

import jax
import jax.numpy as jnp
from jax import lax
from jax.experimental import pallas as pl
from jax.experimental.pallas import tpu as pltpu
from jax.sharding import PartitionSpec as P

MESH = pl.DeviceIdType.MESH
M = 64
CY = 8
CX = 128
F32 = jnp.float32
BF16 = jnp.bfloat16
NX4 = 4


def iota(shape, dim):
    return lax.broadcasted_iota(jnp.int32, shape, dim)


def step(x, n, s, w, e, k, hu, hv):
    return x + k * (n + s + w + e - 4.0 * x) - hu * (e - w) - hv * (s - n)


def forecast_kernel(
    ngy, ngx,
    x_hbm, flow_hbm, cell_hbm, val_hbm, var_hbm,
    gram_ref, hilo_ref, mean_ref,
    xb, xr, yr, zr, fl, cf, cells, obs, qs, fs, ct, h_rows, h_sides, h_corners, fh, zc, rf,
    load_sem, corner_send, halo_recv, gx_recv,
):
    gy = lax.axis_index("gy")
    gx = lax.axis_index("gx")
    up, down = gy - 1, gy + 1
    has_up, has_down = gy > 0, gy < ngy - 1
    left, right = lax.rem(gx + ngx - 1, ngx), lax.rem(gx + 1, ngx)
    gx_partners = [(gy, lax.rem(gx + i, ngx)) for i in sorted(range(1, ngx), key=lambda i: -min(i, ngx - i))]

    def load(src, dst, index):
        pltpu.make_async_copy(src, dst, load_sem.at[index]).start()

    def loaded(piece, index):
        pltpu.make_async_copy(piece, piece, load_sem.at[index]).wait()

    load(flow_hbm, fl, 0)
    for r in (0, 7, 1, 6):
        load(x_hbm.at[:, r, :], xr.at[r + 1], 1)
    load(x_hbm, xb, 2)
    for r in (2, 3, 4, 5):
        load(x_hbm.at[:, r, :], xr.at[r + 1], 3)
    load(cell_hbm, cells, 4)
    load(val_hbm, obs.at[0], 5)
    load(var_hbm, obs.at[1], 5)
    barrier = pltpu.get_barrier_semaphore()

    def greet(partners):
        for partner in partners:
            pl.semaphore_signal(barrier, inc=1, device_id=partner, device_id_type=MESH)

    @pl.when(has_up)
    def _():
        greet([(up, gx), (up, left), (up, right)])

    @pl.when(has_down)
    def _():
        greet([(down, gx), (down, left), (down, right)])

    greet(gx_partners)

    lane = iota((8, CX), 1)
    sub = iota((8, CX), 0)
    edge = (lane <= 1) | (lane >= CX - 2)
    s0, s7 = sub == 0, sub == 7
    l0, l127 = lane == 0, lane == CX - 1
    quad = lane & 3
    q0, q1, q3 = quad == 0, quad == 1, quad == 3
    west_side = quad >= 2

    sends = [load_sem.at[0], load_sem.at[2], load_sem.at[1], corner_send]
    gx_send = load_sem.at[3]

    def remote(src, dst, index, target):
        return pltpu.make_async_remote_copy(
            src_ref=src, dst_ref=dst, send_sem=sends[index], recv_sem=halo_recv.at[index],
            device_id=target, device_id_type=MESH,
        )

    def start(index, to_up, to_down, to_left=None, to_right=None):
        @pl.when(has_up)
        def _():
            for src, dst, target in to_up:
                remote(src, dst, index, (up, target)).start()

        @pl.when(has_down)
        def _():
            for src, dst, target in to_down:
                remote(src, dst, index, (down, target)).start()

        if to_left:
            remote(*to_left, index, (gy, left)).start()
            remote(*to_right, index, (gy, right)).start()

    both = has_up & has_down

    def settle(sem, buffer, most, least):
        def wait(count):
            piece = buffer.at[pl.ds(0, count)]
            pltpu.make_async_copy(piece, piece, sem).wait()

        if most == least:
            wait(most)
        else:
            pl.when(both)(lambda: wait(most))
            pl.when(jnp.logical_not(both))(lambda: wait(least))

    groups = [(fh, 4, 3), (h_sides, 2, 2), (h_rows, 4, 2), (h_corners, 4, 2)]

    def received(index):
        settle(halo_recv.at[index], *groups[index])

    loaded(fl, 0)
    qc = jnp.where(edge, fl[0], 0.0)
    for i in range(1, 3):
        qc = qc + pltpu.roll(jnp.where(edge, fl[i], 0.0), 4 * i, 1)
    fs[1] = qc
    for i in range(3):
        fs[0, pl.ds(i, 1), :] = fl[i, 0:1, :]
        fs[0, pl.ds(3 + i, 1), :] = fl[i, 7:8, :]
    loaded(xr.at[pl.ds(0, 4)], 1)

    ends = l0 | l127
    tile = jnp.zeros((8, CX), F32)
    for b in range(8):
        rows = pl.ds(8 * b, 8)
        tile = tile + pltpu.roll(jnp.where(ends, xr[1, rows, :], 0.0), 4 * b, 1)
        tile = tile + pltpu.roll(jnp.where(ends, xr[8, rows, :], 0.0), 4 * b + 2, 1)
    ct[...] = tile

    @pl.when(both)
    def _():
        pl.semaphore_wait(barrier, ngx + 5)

    @pl.when(jnp.logical_not(both))
    def _():
        pl.semaphore_wait(barrier, ngx + 2)

    start(
        3,
        [(ct, h_corners.at[3], left), (ct, h_corners.at[2], right)],
        [(ct, h_corners.at[1], left), (ct, h_corners.at[0], right)],
    )
    start(0, [(fs.at[0], fh.at[1], gx)], [(fs.at[0], fh.at[0], gx)], (fs.at[1], fh.at[2]), (fs.at[1], fh.at[3]))
    start(2, [(xr.at[pl.ds(1, 2)], h_rows.at[pl.ds(2, 2)], gx)], [(xr.at[pl.ds(7, 2)], h_rows.at[pl.ds(0, 2)], gx)])
    loaded(xb, 2)

    def pack(half):
        sums = [None] * 4
        for m in range(32):
            piece = pltpu.roll(jnp.where(edge, xb[half * 32 + m], 0.0), (CX - 4 * m) % CX, 1)
            sums[m % 4] = piece if m < 4 else sums[m % 4] + piece
        return (sums[0] + sums[1]) + (sums[2] + sums[3])

    qa, qb = pack(0), pack(1)
    qs[pl.ds(0, 8), :] = qa
    qs[pl.ds(8, 8), :] = qb
    start(1, [], [], (qs, h_sides.at[0]), (qs, h_sides.at[1]))
    loaded(xr.at[pl.ds(0, 4)], 3)
    loaded(cells, 4)
    loaded(obs, 5)

    def weights(f0, f1, f2):
        hu, hv = 0.5 * f1, 0.5 * f2
        return 1.0 - 4.0 * f0, f0 + hv, f0 - hv, f0 + hu, f0 - hu

    own = weights(fl[0], fl[1], fl[2])
    a0, an, as_, aw, ae = own
    aw_in, ae_in = jnp.where(l0, 0.0, aw), jnp.where(l127, 0.0, ae)
    for i, v in enumerate((a0, an, as_, aw_in, ae_in)):
        cf[i] = v

    blank = jnp.zeros((M, CX), F32)
    xr[0] = blank
    xr[9] = blank
    yr[0] = blank
    yr[9] = blank

    def inner(source, target, shift):
        def body(r, carry):
            c = [jnp.broadcast_to(cf[i, pl.ds(r, 1), :], (8, CX)) for i in range(5)]
            for b in range(8):
                rows = pl.ds(8 * b, 8)
                x = source[r + 1, rows, :]
                target[r + shift, rows, :] = (
                    (c[0] * x + c[1] * source[r, rows, :]) + (c[2] * source[r + 2, rows, :] + c[3] * pltpu.roll(x, 1, 1))
                    + c[4] * pltpu.roll(x, CX - 1, 1)
                )
            return carry
        lax.fori_loop(0, CY, body, 0)

    inner(xr, yr, 1)
    inner(yr, zr, 0)

    def col(v, l):
        return jnp.broadcast_to(v[:, l:l + 1], (8, CX))

    c_edge = jnp.where(q0, col(aw, 0), jnp.where(q3, col(ae, CX - 1), 0.0))
    a0_edge = jnp.where(q0, col(a0, 0), col(a0, CX - 1))
    an_edge = jnp.where(s0, 0.0, jnp.where(q0, col(an, 0), col(an, CX - 1)))
    as_edge = jnp.where(s7, 0.0, jnp.where(q0, col(as_, 0), col(as_, CX - 1)))
    c_next = jnp.where(q1, col(aw, 1), col(ae, CX - 2))

    has_left, has_right = gx > 0, gx < ngx - 1

    def on(flag):
        return jnp.full((8, CX), jnp.where(flag, 1, 0), jnp.int32) > 0

    cmask = (west_side & on(has_left)) | ((quad <= 1) & on(has_right))

    received(0)

    def flow_cols(i):
        west, east = col(fh[3], (4 * i - 1) % CX), col(fh[2], 4 * i)
        return jnp.where(cmask, jnp.where(west_side, west, east), 0.0)

    kc, uc, vc = flow_cols(0), 0.5 * flow_cols(1), 0.5 * flow_cols(2)

    def outer_row(tile, offset, flag):
        fields = [jnp.where(on(flag), jnp.broadcast_to(tile[offset + i:offset + i + 1, :], (8, CX)), 0.0) for i in range(3)]
        return weights(*fields)

    def line(v, r):
        return jnp.broadcast_to(v[r:r + 1, :], (8, CX))

    ends_in = (l0 & on(has_left)) | (l127 & on(has_right))

    def beside(i):
        return jnp.where(l0, pltpu.roll(fh[3], (1 - 4 * i) % CX, 1), pltpu.roll(fh[2], CX - 1 - 4 * i, 1))

    k_side, v_side = beside(0), 0.5 * beside(2)

    def outside(above):
        if above:
            t0, tn, ts, tw, te = outer_row(fh[0], 3, has_up)
            r, near, far, cross, toward = 0, line(an, 0), tn, ts, line(an, 1)
            side = line(k_side + v_side, 0)
        else:
            t0, tn, ts, tw, te = outer_row(fh[1], 0, has_down)
            r, near, far, cross, toward = 7, line(as_, 7), ts, tn, line(as_, 6)
            side = line(k_side - v_side, 7)
        west = near * jnp.where(l0, 0.0, tw) + line(aw_in, r) * pltpu.roll(near, 1, 1)
        east = near * jnp.where(l127, 0.0, te) + line(ae_in, r) * pltpu.roll(near, CX - 1, 1)
        corner = jnp.where(l0, near * tw + line(aw, r) * side, near * te + line(ae, r) * side)
        corner = jnp.where(ends_in, corner, 0.0)
        return near * (t0 + line(a0, r)), near * far, near * cross, west, east, toward * near, corner

    above = outside(True)
    below = outside(False)

    received(1)
    west_cell = q3
    for half in range(2):
        q = (qa, qb)[half]
        rows = pl.ds(8 * half, 8)
        ring = jnp.where(cmask, jnp.where(west_side, h_sides[1, rows, :], h_sides[0, rows, :]), 0.0)
        n = pltpu.roll(jnp.where(s7, 0.0, ring), 1, 0)
        s = pltpu.roll(jnp.where(s0, 0.0, ring), 7, 0)
        ring_w, ring_e = pltpu.roll(ring, 1, 1), pltpu.roll(ring, CX - 1, 1)
        w = jnp.where(west_cell, ring_w, pltpu.roll(q, 1, 1))
        e = jnp.where(west_cell, pltpu.roll(q, CX - 1, 1), ring_e)
        ring1 = step(ring, n, s, w, e, kc, uc, vc)
        x1 = jnp.where(q0, ring_w, ring_e)
        y1 = jnp.where(q0, pltpu.roll(ring1, 1, 1), pltpu.roll(ring1, CX - 1, 1))
        d = c_edge * x1
        at_edge = a0_edge * d + an_edge * pltpu.roll(d, 1, 0) + as_edge * pltpu.roll(d, 7, 0) + c_edge * y1
        inside = c_next * jnp.where(q1, pltpu.roll(d, 1, 1), pltpu.roll(d, CX - 1, 1))
        zc[half] = jnp.where(q0 | q3, at_edge, inside)

    received(2)
    received(3)

    def add_rows(flag, c, near_row, far_row, r, r_in, corners, first):
        @pl.when(flag)
        def _():
            merged = corners()
            for b in range(8):
                rows = pl.ds(8 * b, 8)
                p = h_rows[near_row, rows, :]
                zr[r, rows, :] = zr[r, rows, :] + (
                    (c[0] * p + c[1] * h_rows[far_row, rows, :]) + (c[2] * xr[r + 1, rows, :] + c[3] * pltpu.roll(p, 1, 1))
                    + (c[4] * pltpu.roll(p, CX - 1, 1) + c[6] * pltpu.roll(merged, (first - 4 * b) % CX, 1))
                )
                zr[r_in, rows, :] = zr[r_in, rows, :] + c[5] * p

    add_rows(has_up, above, 1, 0, 0, 1, lambda: jnp.where(q1, h_corners[0], pltpu.roll(h_corners[1], CX - 2, 1)), CX - 1)
    add_rows(has_down, below, 2, 3, 7, 6, lambda: jnp.where(q3, h_corners[2], pltpu.roll(h_corners[3], CX - 2, 1)), 1)

    def with_columns(r, b, lines):
        spread = pltpu.roll(lines[b // 4], 32 * (b % 4), 1, stride=4, stride_axis=0)
        return zr[r, 8 * b:8 * b + 8, :] + jnp.where(edge, spread, 0.0)

    def column_lines(r):
        return [jnp.broadcast_to(zc[half, pl.ds(r, 1), :], (8, CX)) for half in range(2)]

    lane64 = iota((M, CX), 1)
    diag64 = lane64 == iota((M, CX), 0)
    ones = jnp.zeros((1, CX), F32)
    picked = []
    for j in range(4):
        cell = cells[0, 0, j]
        row, place = lax.shift_right_logical(cell, 7), cell & (CX - 1)
        lines = column_lines(row)
        field = jnp.concatenate([with_columns(row, b, lines) for b in range(8)], axis=0)
        column = jnp.sum(jnp.where(lane64 == place, field, 0.0), axis=1, keepdims=True)
        column = jnp.broadcast_to(column, (M, CX))
        average = jnp.sum(column, axis=0, keepdims=True) * (1.0 / M)
        factor = lax.rsqrt(ones + obs[1, 0, 0, j])
        values = jnp.sum(jnp.where(diag64, column, 0.0), axis=0, keepdims=True)
        values = jnp.where(iota((1, CX), 1) < M - 1, values, ones + obs[0, 0, 0, j])
        picked.append(jnp.where(iota((1, CX), 1) < M, (values - average) * factor, 0.0))
    rf[gx] = jnp.concatenate(
        [picked[0] + pltpu.roll(picked[2], M, 1), picked[1] + pltpu.roll(picked[3], M, 1)], axis=0
    )

    gx_copies = [
        pltpu.make_async_remote_copy(
            src_ref=rf.at[gx], dst_ref=rf.at[gx], send_sem=gx_send, recv_sem=gx_recv,
            device_id=partner, device_id_type=MESH,
        )
        for partner in gx_partners
    ]
    for copy in gx_copies:
        copy.start()

    for r in range(CY):
        lines = column_lines(r)
        field = jnp.concatenate([with_columns(r, b, lines) for b in range(8)], axis=0)
        mean = jnp.sum(field, axis=0, keepdims=True) * (1.0 / M)
        mean_ref[pl.ds(r, 1), :] = mean
        field = field - mean
        high = field.astype(BF16)
        hilo_ref[pl.ds(0, M), pl.ds(r * CX, CX)] = high
        hilo_ref[pl.ds(M, M), pl.ds(r * CX, CX)] = (field - high.astype(F32)).astype(BF16)

    for index, group in enumerate(groups):
        settle(sends[index], *group)

    wait_all(rf, ngx - 1, gx_recv)
    gathered = jnp.concatenate([rf[i] for i in range(ngx)], axis=0)
    lane32 = iota((2 * ngx, CX), 1)
    rows = jnp.concatenate(
        [jnp.where(lane32 < M, gathered, 0.0), jnp.where(lane32 < M, pltpu.roll(gathered, M, 1), 0.0)], axis=0
    )
    gram = jnp.dot(rows.T[0:M], rows, precision=lax.Precision.HIGHEST, preferred_element_type=F32)
    high, low = gram[0:32], pltpu.roll(gram[32:64], CX - 32, 1)
    across, along = iota((32, CX), 1), iota((32, CX), 0)
    square = jnp.where((across < 32) & (across > along), low, high)
    gram_ref[pl.ds(0, 16), :] = square[0:16] + pltpu.roll(square[16:32], M, 1)
    diagonal = jnp.sum(jnp.where(across == along, low, 0.0), axis=0, keepdims=True)
    gram_ref[pl.ds(16, 8), :] = jnp.where(iota((8, CX), 0) == 0, diagonal, 0.0)

    wait_all(rf, ngx - 1, gx_send)


def wait_all(buffer, count, sem):
    piece = buffer.at[pl.ds(0, count)]
    pltpu.make_async_copy(piece, piece, sem).wait()


def sum_kernel(ngy, part_ref, gram_ref, rz, rx, z_send, z_recv, x_send, x_recv):
    gy = lax.axis_index("gy")
    gx = lax.axis_index("gx")
    nz = ngy // NX4
    zpos = gy // NX4
    xpos = lax.rem(gy, NX4)
    z_partners = [(lax.rem(gy + NX4 * i, ngy), gx) for i in sorted(range(1, nz), key=lambda i: -min(i, nz - i))]
    x_partners = [(zpos * NX4 + lax.rem(xpos + i, NX4), gx) for i in (2, 1, 3)]
    barrier = pltpu.get_barrier_semaphore()
    for partner in z_partners + x_partners:
        pl.semaphore_signal(barrier, inc=1, device_id=partner, device_id_type=MESH)
    pl.semaphore_wait(barrier, nz + NX4 - 2)

    def wait_rows(buffer, count, sem):
        piece = buffer.at[pl.ds(0, count), pl.ds(0, 17)]
        pltpu.make_async_copy(piece, piece, sem).wait()

    def spread(source, buffer, slot, partners, send, recv):
        for partner in partners:
            pltpu.make_async_remote_copy(
                src_ref=source.at[pl.ds(0, 17)], dst_ref=buffer.at[slot, pl.ds(0, 17)], send_sem=send, recv_sem=recv,
                device_id=partner, device_id_type=MESH,
            ).start()

    spread(part_ref, rz, zpos, z_partners, z_send, z_recv)
    rz[zpos] = part_ref[...]
    wait_rows(rz, nz - 1, z_recv)
    part = rz[0]
    for i in range(1, nz):
        part = part + rz[i]
    rx[xpos] = part
    spread(rx.at[xpos], rx, xpos, x_partners, x_send, x_recv)
    wait_rows(rx, NX4 - 1, x_recv)
    gram_ref[...] = (rx[0] + rx[1]) + (rx[2] + rx[3])
    wait_rows(rz, nz - 1, z_send)
    wait_rows(rx, NX4 - 1, x_send)


def analysis_kernel(gram_ref, hilo_ref, mean_ref, out_hbm, rows_out, out_sem):
    lane = iota((8, CX), 1)
    sub = iota((8, CX), 0)
    packed = gram_ref[pl.ds(0, 16), :]
    square = jnp.concatenate([packed, pltpu.roll(packed, M, 1)], axis=0)
    square = jnp.where(iota((32, CX), 1) < M, square, 0.0)
    turned = jnp.concatenate([square, jnp.zeros((CX - 32, CX), F32)], axis=0).T
    across, along = iota((32, CX), 1), iota((32, CX), 0)
    top = jnp.where((across < 32) & (across > along), turned[0:32], square)
    corner = jnp.where(across > along, square, jnp.where(across == along, gram_ref[pl.ds(16, 1), :], turned[0:32]))
    corner = pltpu.roll(jnp.where(across < 32, corner, 0.0), 32, 1)
    bottom = jnp.where(across < 32, turned[32:64], corner)
    blocks = [top[8 * i:8 * i + 8] for i in range(4)] + [bottom[8 * i:8 * i + 8] for i in range(4)]
    blocks = [jnp.where(lane < M - 1, b, 0.0) for b in blocks]
    row_sums = [jnp.sum(b, axis=1, keepdims=True) for b in blocks]
    eyes = [lane == sub + 8 * i for i in range(8)]
    diagonals = [jnp.where(e, b, 0.0) for e, b in zip(eyes, blocks)]
    last = sub == 7
    target_row = blocks[7][7:8] + jnp.where(lane[0:1] == M - 1, -row_sums[7][7:8], 0.0)
    blocks[7] = jnp.where(last, 0.0, blocks[7])
    row_sums[7] = jnp.where(last[:, 0:1], 0.0, row_sums[7])
    col_sum = functools.reduce(jnp.add, blocks)
    col_sum = jnp.sum(col_sum, axis=0, keepdims=True)
    all_sum = jnp.sum(functools.reduce(jnp.add, row_sums), axis=0, keepdims=True)
    blocks = [jnp.where(lane == M - 1, -r, b) for b, r in zip(blocks, row_sums)]
    blocks[7] = jnp.where(last, jnp.where(lane == M - 1, all_sum, -col_sum), blocks[7])
    scale_row = jnp.sum(functools.reduce(jnp.add, diagonals), axis=0, keepdims=True)
    scale_row = lax.rsqrt((M - 1.0) + jnp.where(lane[0:1] == M - 1, all_sum, scale_row))
    scale_col = [jnp.sum(d, axis=1, keepdims=True) for d in diagonals]
    scale_col[7] = jnp.where(last[:, 0:1], all_sum, scale_col[7])
    scale_col = [lax.rsqrt((M - 1.0) + c) for c in scale_col]
    blocks = [jnp.where(e, b + (M - 1.0), b) for e, b in zip(eyes, blocks)]
    a = [
        jnp.where(lane == sub + (M + 8 * i), scale_col[i], jnp.where(lane < M, blocks[i] * scale_col[i] * scale_row, 0.0))
        for i in range(8)
    ]

    lower = [None] * 8
    heads = []
    target_high = pltpu.roll(jnp.broadcast_to(target_row, (8, CX)), M, 1)
    nothing = 0.0 * packed[0:8]
    for p in range(16):
        b, o = p // 2, 4 * (p % 2)
        cols = {
            (t, i): jnp.broadcast_to(a[i][:, 4 * p + t:4 * p + t + 1], (8, CX)) for t in range(4) for i in range(b, 8)
        }
        cols = {key: v + nothing if key[1] == b else v for key, v in cols.items()}
        d = {
            (s, t): jnp.broadcast_to(cols[t, b][o + s:o + s + 1, :], (8, CX)) for s in range(4) for t in range(s + 1)
        }
        r = [jnp.broadcast_to(a[b][o + s:o + s + 1, :], (8, CX)) for s in range(4)]

        det = d[0, 0] * d[1, 1] - d[1, 0] * d[1, 0]
        inv = 1.0 / det
        f00 = d[1, 1] * d[2, 0] - d[1, 0] * d[2, 1]
        f10 = d[0, 0] * d[2, 1] - d[1, 0] * d[2, 0]
        f01 = d[1, 1] * d[3, 0] - d[1, 0] * d[3, 1]
        f11 = d[0, 0] * d[3, 1] - d[1, 0] * d[3, 0]
        g00 = det * d[2, 2] - (d[2, 0] * f00 + d[2, 1] * f10)
        g10 = det * d[3, 2] - (d[3, 0] * f00 + d[3, 1] * f10)
        g11 = det * d[3, 3] - (d[3, 0] * f01 + d[3, 1] * f11)
        det2 = g00 * g11 - g10 * g10
        i00, i10, i11 = d[1, 1] * inv, -d[1, 0] * inv, d[0, 0] * inv
        e00, e10, e01, e11 = f00 * inv, f10 * inv, f01 * inv, f11 * inv
        r2 = r[2] - (e00 * r[0] + e10 * r[1])
        r3 = r[3] - (e01 * r[0] + e11 * r[1])
        if p < 15:
            u0 = i00 * r[0] + i10 * r[1]
            u1 = i10 * r[0] + i11 * r[1]
            inv2 = det * (1.0 / det2)
            t2, t3 = g11 * r2 - g10 * r3, g00 * r3 - g10 * r2
            z2, z3 = t2 * inv2, t3 * inv2
            z0 = u0 - (e00 * z2 + e01 * z3)
            z1 = u1 - (e10 * z2 + e11 * z3)
            z = (z0, z1, z2, z3)
            for i in range(b if o == 0 else b + 1, 8):
                if i == (b if o == 0 else b + 1):
                    m2 = cols[2, i] - (cols[0, i] * e00 + cols[1, i] * e10)
                    m3 = cols[3, i] - (cols[0, i] * e01 + cols[1, i] * e11)
                    new = (a[i] - (cols[0, i] * u0 + cols[1, i] * u1)) - inv2 * (m2 * t2 + m3 * t3)
                else:
                    new = a[i] - ((cols[0, i] * z[0] + cols[1, i] * z[1]) + (cols[2, i] * z[2] + cols[3, i] * z[3]))
                a[i] = jnp.where(sub >= 4, new, a[i]) if i == b else new
        n0 = r[0] * lax.rsqrt(d[0, 0])
        n1 = (d[0, 0] * r[1] - d[1, 0] * r[0]) * lax.rsqrt(d[0, 0] * det)
        c00, c10 = g00 * inv, g10 * inv
        n2 = r2 * lax.rsqrt(c00)
        n3 = (c00 * r3 - c10 * r2) * lax.rsqrt(c00 * (det2 * inv * inv))
        rows = jnp.where(sub == o, n0, jnp.where(sub == o + 1, n1, jnp.where(sub == o + 2, n2, n3)))
        lower[b] = rows if o == 0 else jnp.where(sub >= 4, rows, lower[b])
        if o:
            lower[b] = jnp.where(lane >= M, lower[b], 0.0)
            heads.append(jnp.sum(lower[b] * target_high, axis=1, keepdims=True))
    weight = jnp.sum(functools.reduce(jnp.add, [v * h for v, h in zip(lower, heads)]), axis=0, keepdims=True)
    root = math.sqrt(M - 1.0)
    mix = jnp.concatenate([root * v + weight for v in lower], axis=0)
    mix = jnp.where(iota((M, CX), 1) < M, pltpu.roll(mix, M, 1), mix)
    high = mix.astype(BF16)
    pair, low_pair = high, (mix - high.astype(F32)).astype(BF16)
    left = jnp.concatenate([pair, low_pair], axis=1)
    for r in range(0, CY, 2):
        cols = pl.ds(r * CX, 2 * CX)
        block = hilo_ref[:, cols]
        right = jnp.concatenate([block, block], axis=0)
        res = jnp.dot(left, right, preferred_element_type=F32)
        for half in range(2):
            rows_out[r + half] = res[:, half * CX:(half + 1) * CX] + mean_ref[r + half:r + half + 1, :]
            pltpu.make_async_copy(rows_out.at[r + half], out_hbm.at[:, r + half, :], out_sem).start()
    pltpu.make_async_copy(rows_out, rows_out, out_sem).wait()


def near(array):
    return pltpu.with_memory_space_constraint(array, pltpu.VMEM)


def body(ngy, ngx, ensemble, flow, obs_cell, obs_value, obs_var):
    vmem = pl.BlockSpec(memory_space=pltpu.VMEM)
    hbm = pl.BlockSpec(memory_space=pl.ANY)
    dma = pltpu.SemaphoreType.DMA
    part, hilo, mean = pl.pallas_call(
        functools.partial(forecast_kernel, ngy, ngx),
        out_shape=(
            pltpu.VMEM((24, CX), F32),
            pltpu.VMEM((2 * M, CY * CX), BF16),
            pltpu.VMEM((CY, CX), F32),
        ),
        in_specs=[hbm] * 5,
        out_specs=(vmem,) * 3,
        scratch_shapes=[
            pltpu.VMEM((M, CY, CX), F32),
            pltpu.VMEM((CY + 2, M, CX), F32),
            pltpu.VMEM((CY + 2, M, CX), F32),
            pltpu.VMEM((CY, M, CX), F32),
            pltpu.VMEM((3, CY, CX), F32),
            pltpu.VMEM((5, CY, CX), F32),
            pltpu.SMEM((1, 1, 4), jnp.int32),
            pltpu.SMEM((2, 1, 1, 4), F32),
            pltpu.VMEM((16, CX), F32),
            pltpu.VMEM((2, 8, CX), F32),
            pltpu.VMEM((8, CX), F32),
            pltpu.VMEM((4, M, CX), F32),
            pltpu.VMEM((2, 16, CX), F32),
            pltpu.VMEM((4, 8, CX), F32),
            pltpu.VMEM((4, 8, CX), F32),
            pltpu.VMEM((2, 8, CX), F32),
            pltpu.VMEM((ngx, 2, CX), F32),
            dma((6,)), dma, dma((4,)), dma,
        ],
        compiler_params=pltpu.CompilerParams(collective_id=0, has_side_effects=True),
        name="forecast",
    )(ensemble, flow, obs_cell, obs_value, obs_var)
    gram = pl.pallas_call(
        functools.partial(sum_kernel, ngy),
        out_shape=pltpu.VMEM((24, CX), F32),
        in_specs=[vmem],
        out_specs=vmem,
        scratch_shapes=[
            pltpu.VMEM((ngy // NX4, 24, CX), F32),
            pltpu.VMEM((NX4, 24, CX), F32),
            dma, dma, dma, dma,
        ],
        compiler_params=pltpu.CompilerParams(collective_id=1, has_side_effects=True),
        name="sums",
    )(near(part))
    return pl.pallas_call(
        analysis_kernel,
        out_shape=jax.ShapeDtypeStruct((M, CY, CX), F32),
        in_specs=[vmem] * 3,
        out_specs=hbm,
        scratch_shapes=[pltpu.VMEM((CY, M, CX), F32), dma],
        name="analysis",
    )(near(gram), near(hilo), near(mean))


def solution(mesh):
    tile = P("gy", "gx", None)
    return jax.shard_map(
        functools.partial(body, mesh.shape["gy"], mesh.shape["gx"]),
        mesh=mesh,
        in_specs=(P(None, "gy", "gx"), P(None, "gy", "gx"), tile, tile, tile),
        out_specs=P(None, "gy", "gx"),
        check_vma=False,
    )
```

```python
import functools
import math

import jax
import jax.numpy as jnp
from jax import lax
from jax.experimental import pallas as pl
from jax.experimental.pallas import tpu as pltpu
from jax.sharding import PartitionSpec as P

MESH = pl.DeviceIdType.MESH
M = 64
CY = 8
CX = 128
F32 = jnp.float32
BF16 = jnp.bfloat16
NX4 = 4


def iota(shape, dim):
    return lax.broadcasted_iota(jnp.int32, shape, dim)


def step(x, n, s, w, e, k, hu, hv):
    return x + k * (n + s + w + e - 4.0 * x) - hu * (e - w) - hv * (s - n)


def forecast_kernel(
    ngy, ngx,
    x_hbm, flow_hbm, cell_hbm, val_hbm, var_hbm,
    gram_ref, hilo_ref, mean_ref,
    xb, xr, yr, zr, fl, cf, cells, obs, qs, fs, ct, h_rows, h_sides, h_corners, fh, zc, rf,
    load_sem, corner_send, halo_recv, gx_recv,
):
    gy = lax.axis_index("gy")
    gx = lax.axis_index("gx")
    up, down = gy - 1, gy + 1
    has_up, has_down = gy > 0, gy < ngy - 1
    left, right = lax.rem(gx + ngx - 1, ngx), lax.rem(gx + 1, ngx)
    gx_partners = [(gy, lax.rem(gx + i, ngx)) for i in sorted(range(1, ngx), key=lambda i: -min(i, ngx - i))]

    def load(src, dst, index):
        pltpu.make_async_copy(src, dst, load_sem.at[index]).start()

    def loaded(piece, index):
        pltpu.make_async_copy(piece, piece, load_sem.at[index]).wait()

    load(flow_hbm, fl, 0)
    for r in (0, 7, 1, 6):
        load(x_hbm.at[:, r, :], xr.at[r + 1], 1)
    load(x_hbm, xb, 2)
    for r in (2, 3, 4, 5):
        load(x_hbm.at[:, r, :], xr.at[r + 1], 3)
    load(cell_hbm, cells, 4)
    load(val_hbm, obs.at[0], 5)
    load(var_hbm, obs.at[1], 5)
    barrier = pltpu.get_barrier_semaphore()

    def greet(partners):
        for partner in partners:
            pl.semaphore_signal(barrier, inc=1, device_id=partner, device_id_type=MESH)

    @pl.when(has_up)
    def _():
        greet([(up, gx), (up, left), (up, right)])

    @pl.when(has_down)
    def _():
        greet([(down, gx), (down, left), (down, right)])

    greet(gx_partners)

    lane = iota((8, CX), 1)
    sub = iota((8, CX), 0)
    edge = (lane <= 1) | (lane >= CX - 2)
    s0, s7 = sub == 0, sub == 7
    l0, l127 = lane == 0, lane == CX - 1
    quad = lane & 3
    q0, q1, q3 = quad == 0, quad == 1, quad == 3
    west_side = quad >= 2

    sends = [load_sem.at[0], load_sem.at[2], load_sem.at[1], corner_send]
    gx_send = load_sem.at[3]

    def remote(src, dst, index, target):
        return pltpu.make_async_remote_copy(
            src_ref=src, dst_ref=dst, send_sem=sends[index], recv_sem=halo_recv.at[index],
            device_id=target, device_id_type=MESH,
        )

    def start(index, to_up, to_down, to_left=None, to_right=None):
        @pl.when(has_up)
        def _():
            for src, dst, target in to_up:
                remote(src, dst, index, (up, target)).start()

        @pl.when(has_down)
        def _():
            for src, dst, target in to_down:
                remote(src, dst, index, (down, target)).start()

        if to_left:
            remote(*to_left, index, (gy, left)).start()
            remote(*to_right, index, (gy, right)).start()

    both = has_up & has_down

    def settle(sem, buffer, most, least):
        def wait(count):
            piece = buffer.at[pl.ds(0, count)]
            pltpu.make_async_copy(piece, piece, sem).wait()

        if most == least:
            wait(most)
        else:
            pl.when(both)(lambda: wait(most))
            pl.when(jnp.logical_not(both))(lambda: wait(least))

    groups = [(fh, 4, 3), (h_sides, 2, 2), (h_rows, 4, 2), (h_corners, 4, 2)]

    def received(index):
        settle(halo_recv.at[index], *groups[index])

    loaded(fl, 0)
    qc = jnp.where(edge, fl[0], 0.0)
    for i in range(1, 3):
        qc = qc + pltpu.roll(jnp.where(edge, fl[i], 0.0), 4 * i, 1)
    fs[1] = qc
    for i in range(3):
        fs[0, pl.ds(i, 1), :] = fl[i, 0:1, :]
        fs[0, pl.ds(3 + i, 1), :] = fl[i, 7:8, :]
    loaded(xr.at[pl.ds(0, 4)], 1)

    ends = l0 | l127
    tile = jnp.zeros((8, CX), F32)
    for b in range(8):
        rows = pl.ds(8 * b, 8)
        tile = tile + pltpu.roll(jnp.where(ends, xr[1, rows, :], 0.0), 4 * b, 1)
        tile = tile + pltpu.roll(jnp.where(ends, xr[8, rows, :], 0.0), 4 * b + 2, 1)
    ct[...] = tile

    @pl.when(both)
    def _():
        pl.semaphore_wait(barrier, ngx + 5)

    @pl.when(jnp.logical_not(both))
    def _():
        pl.semaphore_wait(barrier, ngx + 2)

    start(
        3,
        [(ct, h_corners.at[3], left), (ct, h_corners.at[2], right)],
        [(ct, h_corners.at[1], left), (ct, h_corners.at[0], right)],
    )
    start(0, [(fs.at[0], fh.at[1], gx)], [(fs.at[0], fh.at[0], gx)], (fs.at[1], fh.at[2]), (fs.at[1], fh.at[3]))
    start(2, [(xr.at[pl.ds(1, 2)], h_rows.at[pl.ds(2, 2)], gx)], [(xr.at[pl.ds(7, 2)], h_rows.at[pl.ds(0, 2)], gx)])
    loaded(xb, 2)

    def pack(half):
        sums = [None] * 4
        for m in range(32):
            piece = pltpu.roll(jnp.where(edge, xb[half * 32 + m], 0.0), (CX - 4 * m) % CX, 1)
            sums[m % 4] = piece if m < 4 else sums[m % 4] + piece
        return (sums[0] + sums[1]) + (sums[2] + sums[3])

    qa, qb = pack(0), pack(1)
    qs[pl.ds(0, 8), :] = qa
    qs[pl.ds(8, 8), :] = qb
    start(1, [], [], (qs, h_sides.at[0]), (qs, h_sides.at[1]))
    loaded(xr.at[pl.ds(0, 4)], 3)
    loaded(cells, 4)
    loaded(obs, 5)

    def weights(f0, f1, f2):
        hu, hv = 0.5 * f1, 0.5 * f2
        return 1.0 - 4.0 * f0, f0 + hv, f0 - hv, f0 + hu, f0 - hu

    own = weights(fl[0], fl[1], fl[2])
    a0, an, as_, aw, ae = own
    aw_in, ae_in = jnp.where(l0, 0.0, aw), jnp.where(l127, 0.0, ae)
    for i, v in enumerate((a0, an, as_, aw_in, ae_in)):
        cf[i] = v

    blank = jnp.zeros((M, CX), F32)
    xr[0] = blank
    xr[9] = blank
    yr[0] = blank
    yr[9] = blank

    def inner(source, target, shift):
        def body(r, carry):
            c = [jnp.broadcast_to(cf[i, pl.ds(r, 1), :], (8, CX)) for i in range(5)]
            for b in range(8):
                rows = pl.ds(8 * b, 8)
                x = source[r + 1, rows, :]
                target[r + shift, rows, :] = (
                    (c[0] * x + c[1] * source[r, rows, :]) + (c[2] * source[r + 2, rows, :] + c[3] * pltpu.roll(x, 1, 1))
                    + c[4] * pltpu.roll(x, CX - 1, 1)
                )
            return carry
        lax.fori_loop(0, CY, body, 0)

    inner(xr, yr, 1)
    inner(yr, zr, 0)

    def col(v, l):
        return jnp.broadcast_to(v[:, l:l + 1], (8, CX))

    c_edge = jnp.where(q0, col(aw, 0), jnp.where(q3, col(ae, CX - 1), 0.0))
    a0_edge = jnp.where(q0, col(a0, 0), col(a0, CX - 1))
    an_edge = jnp.where(s0, 0.0, jnp.where(q0, col(an, 0), col(an, CX - 1)))
    as_edge = jnp.where(s7, 0.0, jnp.where(q0, col(as_, 0), col(as_, CX - 1)))
    c_next = jnp.where(q1, col(aw, 1), col(ae, CX - 2))

    has_left, has_right = gx > 0, gx < ngx - 1

    def on(flag):
        return jnp.full((8, CX), jnp.where(flag, 1, 0), jnp.int32) > 0

    cmask = (west_side & on(has_left)) | ((quad <= 1) & on(has_right))

    received(0)

    def flow_cols(i):
        west, east = col(fh[3], (4 * i - 1) % CX), col(fh[2], 4 * i)
        return jnp.where(cmask, jnp.where(west_side, west, east), 0.0)

    kc, uc, vc = flow_cols(0), 0.5 * flow_cols(1), 0.5 * flow_cols(2)

    def outer_row(tile, offset, flag):
        fields = [jnp.where(on(flag), jnp.broadcast_to(tile[offset + i:offset + i + 1, :], (8, CX)), 0.0) for i in range(3)]
        return weights(*fields)

    def line(v, r):
        return jnp.broadcast_to(v[r:r + 1, :], (8, CX))

    ends_in = (l0 & on(has_left)) | (l127 & on(has_right))

    def beside(i):
        return jnp.where(l0, pltpu.roll(fh[3], (1 - 4 * i) % CX, 1), pltpu.roll(fh[2], CX - 1 - 4 * i, 1))

    k_side, v_side = beside(0), 0.5 * beside(2)

    def outside(above):
        if above:
            t0, tn, ts, tw, te = outer_row(fh[0], 3, has_up)
            r, near, far, cross, toward = 0, line(an, 0), tn, ts, line(an, 1)
            side = line(k_side + v_side, 0)
        else:
            t0, tn, ts, tw, te = outer_row(fh[1], 0, has_down)
            r, near, far, cross, toward = 7, line(as_, 7), ts, tn, line(as_, 6)
            side = line(k_side - v_side, 7)
        west = near * jnp.where(l0, 0.0, tw) + line(aw_in, r) * pltpu.roll(near, 1, 1)
        east = near * jnp.where(l127, 0.0, te) + line(ae_in, r) * pltpu.roll(near, CX - 1, 1)
        corner = jnp.where(l0, near * tw + line(aw, r) * side, near * te + line(ae, r) * side)
        corner = jnp.where(ends_in, corner, 0.0)
        return near * (t0 + line(a0, r)), near * far, near * cross, west, east, toward * near, corner

    above = outside(True)
    below = outside(False)

    received(1)
    west_cell = q3
    for half in range(2):
        q = (qa, qb)[half]
        rows = pl.ds(8 * half, 8)
        ring = jnp.where(cmask, jnp.where(west_side, h_sides[1, rows, :], h_sides[0, rows, :]), 0.0)
        n = pltpu.roll(jnp.where(s7, 0.0, ring), 1, 0)
        s = pltpu.roll(jnp.where(s0, 0.0, ring), 7, 0)
        ring_w, ring_e = pltpu.roll(ring, 1, 1), pltpu.roll(ring, CX - 1, 1)
        w = jnp.where(west_cell, ring_w, pltpu.roll(q, 1, 1))
        e = jnp.where(west_cell, pltpu.roll(q, CX - 1, 1), ring_e)
        ring1 = step(ring, n, s, w, e, kc, uc, vc)
        x1 = jnp.where(q0, ring_w, ring_e)
        y1 = jnp.where(q0, pltpu.roll(ring1, 1, 1), pltpu.roll(ring1, CX - 1, 1))
        d = c_edge * x1
        at_edge = a0_edge * d + an_edge * pltpu.roll(d, 1, 0) + as_edge * pltpu.roll(d, 7, 0) + c_edge * y1
        inside = c_next * jnp.where(q1, pltpu.roll(d, 1, 1), pltpu.roll(d, CX - 1, 1))
        zc[half] = jnp.where(q0 | q3, at_edge, inside)

    received(2)
    received(3)

    def add_rows(flag, c, near_row, far_row, r, r_in, corners, first):
        @pl.when(flag)
        def _():
            merged = corners()
            for b in range(8):
                rows = pl.ds(8 * b, 8)
                p = h_rows[near_row, rows, :]
                zr[r, rows, :] = zr[r, rows, :] + (
                    (c[0] * p + c[1] * h_rows[far_row, rows, :]) + (c[2] * xr[r + 1, rows, :] + c[3] * pltpu.roll(p, 1, 1))
                    + (c[4] * pltpu.roll(p, CX - 1, 1) + c[6] * pltpu.roll(merged, (first - 4 * b) % CX, 1))
                )
                zr[r_in, rows, :] = zr[r_in, rows, :] + c[5] * p

    add_rows(has_up, above, 1, 0, 0, 1, lambda: jnp.where(q1, h_corners[0], pltpu.roll(h_corners[1], CX - 2, 1)), CX - 1)
    add_rows(has_down, below, 2, 3, 7, 6, lambda: jnp.where(q3, h_corners[2], pltpu.roll(h_corners[3], CX - 2, 1)), 1)

    def with_columns(r, b, lines):
        spread = pltpu.roll(lines[b // 4], 32 * (b % 4), 1, stride=4, stride_axis=0)
        return zr[r, 8 * b:8 * b + 8, :] + jnp.where(edge, spread, 0.0)

    def column_lines(r):
        return [jnp.broadcast_to(zc[half, pl.ds(r, 1), :], (8, CX)) for half in range(2)]

    lane64 = iota((M, CX), 1)
    diag64 = lane64 == iota((M, CX), 0)
    ones = jnp.zeros((1, CX), F32)
    picked = []
    for j in range(4):
        cell = cells[0, 0, j]
        row, place = lax.shift_right_logical(cell, 7), cell & (CX - 1)
        lines = column_lines(row)
        field = jnp.concatenate([with_columns(row, b, lines) for b in range(8)], axis=0)
        column = jnp.sum(jnp.where(lane64 == place, field, 0.0), axis=1, keepdims=True)
        column = jnp.broadcast_to(column, (M, CX))
        average = jnp.sum(column, axis=0, keepdims=True) * (1.0 / M)
        factor = lax.rsqrt(ones + obs[1, 0, 0, j])
        values = jnp.sum(jnp.where(diag64, column, 0.0), axis=0, keepdims=True)
        values = jnp.where(iota((1, CX), 1) < M - 1, values, ones + obs[0, 0, 0, j])
        picked.append(jnp.where(iota((1, CX), 1) < M, (values - average) * factor, 0.0))
    rf[gx] = jnp.concatenate(
        [picked[0] + pltpu.roll(picked[2], M, 1), picked[1] + pltpu.roll(picked[3], M, 1)], axis=0
    )

    gx_copies = [
        pltpu.make_async_remote_copy(
            src_ref=rf.at[gx], dst_ref=rf.at[gx], send_sem=gx_send, recv_sem=gx_recv,
            device_id=partner, device_id_type=MESH,
        )
        for partner in gx_partners
    ]
    for copy in gx_copies:
        copy.start()

    for r in range(CY):
        lines = column_lines(r)
        field = jnp.concatenate([with_columns(r, b, lines) for b in range(8)], axis=0)
        mean = jnp.sum(field, axis=0, keepdims=True) * (1.0 / M)
        mean_ref[pl.ds(r, 1), :] = mean
        field = field - mean
        high = field.astype(BF16)
        hilo_ref[pl.ds(0, M), pl.ds(r * CX, CX)] = high
        hilo_ref[pl.ds(M, M), pl.ds(r * CX, CX)] = (field - high.astype(F32)).astype(BF16)

    for index, group in enumerate(groups):
        settle(sends[index], *group)

    wait_all(rf, ngx - 1, gx_send)
    wait_all(rf, ngx - 1, gx_recv)
    gathered = jnp.concatenate([rf[i] for i in range(ngx)], axis=0)
    lane32 = iota((2 * ngx, CX), 1)
    rows = jnp.concatenate(
        [jnp.where(lane32 < M, gathered, 0.0), jnp.where(lane32 < M, pltpu.roll(gathered, M, 1), 0.0)], axis=0
    )
    gram = jnp.dot(rows.T[0:M], rows, precision=lax.Precision.HIGHEST, preferred_element_type=F32)
    high, low = gram[0:32], pltpu.roll(gram[32:64], CX - 32, 1)
    across, along = iota((32, CX), 1), iota((32, CX), 0)
    square = jnp.where((across < 32) & (across > along), low, high)
    gram_ref[pl.ds(0, 16), :] = square[0:16] + pltpu.roll(square[16:32], M, 1)
    diagonal = jnp.sum(jnp.where(across == along, low, 0.0), axis=0, keepdims=True)
    gram_ref[pl.ds(16, 8), :] = jnp.where(iota((8, CX), 0) == 0, diagonal, 0.0)


def wait_all(buffer, count, sem):
    piece = buffer.at[pl.ds(0, count)]
    pltpu.make_async_copy(piece, piece, sem).wait()


def sum_kernel(ngy, part_ref, gram_ref, rz, rx, z_send, z_recv, x_send, x_recv):
    gy = lax.axis_index("gy")
    gx = lax.axis_index("gx")
    nz = ngy // NX4
    zpos = gy // NX4
    xpos = lax.rem(gy, NX4)
    z_partners = [(lax.rem(gy + NX4 * i, ngy), gx) for i in sorted(range(1, nz), key=lambda i: -min(i, nz - i))]
    x_partners = [(zpos * NX4 + lax.rem(xpos + i, NX4), gx) for i in (2, 1, 3)]
    barrier = pltpu.get_barrier_semaphore()
    for partner in z_partners + x_partners:
        pl.semaphore_signal(barrier, inc=1, device_id=partner, device_id_type=MESH)
    pl.semaphore_wait(barrier, nz + NX4 - 2)

    def wait_rows(buffer, count, sem):
        piece = buffer.at[pl.ds(0, count), pl.ds(0, 17)]
        pltpu.make_async_copy(piece, piece, sem).wait()

    def spread(source, buffer, slot, partners, send, recv):
        for partner in partners:
            pltpu.make_async_remote_copy(
                src_ref=source.at[pl.ds(0, 17)], dst_ref=buffer.at[slot, pl.ds(0, 17)], send_sem=send, recv_sem=recv,
                device_id=partner, device_id_type=MESH,
            ).start()

    spread(part_ref, rz, zpos, z_partners, z_send, z_recv)
    rz[zpos] = part_ref[...]
    wait_rows(rz, nz - 1, z_recv)
    part = rz[0]
    for i in range(1, nz):
        part = part + rz[i]
    rx[xpos] = part
    spread(rx.at[xpos], rx, xpos, x_partners, x_send, x_recv)
    wait_rows(rz, nz - 1, z_send)
    wait_rows(rx, NX4 - 1, x_recv)
    gram_ref[...] = (rx[0] + rx[1]) + (rx[2] + rx[3])
    wait_rows(rx, NX4 - 1, x_send)


def analysis_kernel(gram_ref, hilo_ref, mean_ref, out_hbm, rows_out, out_sem):
    lane = iota((8, CX), 1)
    sub = iota((8, CX), 0)
    packed = gram_ref[pl.ds(0, 16), :]
    square = jnp.concatenate([packed, pltpu.roll(packed, M, 1)], axis=0)
    square = jnp.where(iota((32, CX), 1) < M, square, 0.0)
    turned = jnp.concatenate([square, jnp.zeros((CX - 32, CX), F32)], axis=0).T
    across, along = iota((32, CX), 1), iota((32, CX), 0)
    top = jnp.where((across < 32) & (across > along), turned[0:32], square)
    corner = jnp.where(across > along, square, jnp.where(across == along, gram_ref[pl.ds(16, 1), :], turned[0:32]))
    corner = pltpu.roll(jnp.where(across < 32, corner, 0.0), 32, 1)
    bottom = jnp.where(across < 32, turned[32:64], corner)
    blocks = [top[8 * i:8 * i + 8] for i in range(4)] + [bottom[8 * i:8 * i + 8] for i in range(4)]
    blocks = [jnp.where(lane < M - 1, b, 0.0) for b in blocks]
    row_sums = [jnp.sum(b, axis=1, keepdims=True) for b in blocks]
    eyes = [lane == sub + 8 * i for i in range(8)]
    diagonals = [jnp.where(e, b, 0.0) for e, b in zip(eyes, blocks)]
    last = sub == 7
    target_row = blocks[7][7:8] + jnp.where(lane[0:1] == M - 1, -row_sums[7][7:8], 0.0)
    blocks[7] = jnp.where(last, 0.0, blocks[7])
    row_sums[7] = jnp.where(last[:, 0:1], 0.0, row_sums[7])
    col_sum = functools.reduce(jnp.add, blocks)
    col_sum = jnp.sum(col_sum, axis=0, keepdims=True)
    all_sum = jnp.sum(functools.reduce(jnp.add, row_sums), axis=0, keepdims=True)
    blocks = [jnp.where(lane == M - 1, -r, b) for b, r in zip(blocks, row_sums)]
    blocks[7] = jnp.where(last, jnp.where(lane == M - 1, all_sum, -col_sum), blocks[7])
    scale_row = jnp.sum(functools.reduce(jnp.add, diagonals), axis=0, keepdims=True)
    scale_row = lax.rsqrt((M - 1.0) + jnp.where(lane[0:1] == M - 1, all_sum, scale_row))
    scale_col = [jnp.sum(d, axis=1, keepdims=True) for d in diagonals]
    scale_col[7] = jnp.where(last[:, 0:1], all_sum, scale_col[7])
    scale_col = [lax.rsqrt((M - 1.0) + c) for c in scale_col]
    blocks = [jnp.where(e, b + (M - 1.0), b) for e, b in zip(eyes, blocks)]
    a = [
        jnp.where(lane == sub + (M + 8 * i), scale_col[i], jnp.where(lane < M, blocks[i] * scale_col[i] * scale_row, 0.0))
        for i in range(8)
    ]

    lower = [None] * 8
    heads = []
    target_high = pltpu.roll(jnp.broadcast_to(target_row, (8, CX)), M, 1)
    nothing = 0.0 * packed[0:8]
    for p in range(16):
        b, o = p // 2, 4 * (p % 2)
        cols = {
            (t, i): jnp.broadcast_to(a[i][:, 4 * p + t:4 * p + t + 1], (8, CX)) for t in range(4) for i in range(b, 8)
        }
        cols = {key: v + nothing if key[1] == b else v for key, v in cols.items()}
        d = {
            (s, t): jnp.broadcast_to(cols[t, b][o + s:o + s + 1, :], (8, CX)) for s in range(4) for t in range(s + 1)
        }
        r = [jnp.broadcast_to(a[b][o + s:o + s + 1, :], (8, CX)) for s in range(4)]

        det = d[0, 0] * d[1, 1] - d[1, 0] * d[1, 0]
        inv = 1.0 / det
        f00 = d[1, 1] * d[2, 0] - d[1, 0] * d[2, 1]
        f10 = d[0, 0] * d[2, 1] - d[1, 0] * d[2, 0]
        f01 = d[1, 1] * d[3, 0] - d[1, 0] * d[3, 1]
        f11 = d[0, 0] * d[3, 1] - d[1, 0] * d[3, 0]
        g00 = det * d[2, 2] - (d[2, 0] * f00 + d[2, 1] * f10)
        g10 = det * d[3, 2] - (d[3, 0] * f00 + d[3, 1] * f10)
        g11 = det * d[3, 3] - (d[3, 0] * f01 + d[3, 1] * f11)
        det2 = g00 * g11 - g10 * g10
        i00, i10, i11 = d[1, 1] * inv, -d[1, 0] * inv, d[0, 0] * inv
        e00, e10, e01, e11 = f00 * inv, f10 * inv, f01 * inv, f11 * inv
        r2 = r[2] - (e00 * r[0] + e10 * r[1])
        r3 = r[3] - (e01 * r[0] + e11 * r[1])
        if p < 15:
            u0 = i00 * r[0] + i10 * r[1]
            u1 = i10 * r[0] + i11 * r[1]
            inv2 = det * (1.0 / det2)
            t2, t3 = g11 * r2 - g10 * r3, g00 * r3 - g10 * r2
            z2, z3 = t2 * inv2, t3 * inv2
            z0 = u0 - (e00 * z2 + e01 * z3)
            z1 = u1 - (e10 * z2 + e11 * z3)
            z = (z0, z1, z2, z3)
            for i in range(b if o == 0 else b + 1, 8):
                if i == (b if o == 0 else b + 1):
                    m2 = cols[2, i] - (cols[0, i] * e00 + cols[1, i] * e10)
                    m3 = cols[3, i] - (cols[0, i] * e01 + cols[1, i] * e11)
                    new = (a[i] - (cols[0, i] * u0 + cols[1, i] * u1)) - inv2 * (m2 * t2 + m3 * t3)
                else:
                    new = a[i] - ((cols[0, i] * z[0] + cols[1, i] * z[1]) + (cols[2, i] * z[2] + cols[3, i] * z[3]))
                a[i] = jnp.where(sub >= 4, new, a[i]) if i == b else new
        n0 = r[0] * lax.rsqrt(d[0, 0])
        n1 = (d[0, 0] * r[1] - d[1, 0] * r[0]) * lax.rsqrt(d[0, 0] * det)
        c00, c10 = g00 * inv, g10 * inv
        n2 = r2 * lax.rsqrt(c00)
        n3 = (c00 * r3 - c10 * r2) * lax.rsqrt(c00 * (det2 * inv * inv))
        rows = jnp.where(sub == o, n0, jnp.where(sub == o + 1, n1, jnp.where(sub == o + 2, n2, n3)))
        lower[b] = rows if o == 0 else jnp.where(sub >= 4, rows, lower[b])
        if o:
            lower[b] = jnp.where(lane >= M, lower[b], 0.0)
            heads.append(jnp.sum(lower[b] * target_high, axis=1, keepdims=True))
    weight = jnp.sum(functools.reduce(jnp.add, [v * h for v, h in zip(lower, heads)]), axis=0, keepdims=True)
    root = math.sqrt(M - 1.0)
    mix = jnp.concatenate([root * v + weight for v in lower], axis=0)
    mix = jnp.where(iota((M, CX), 1) < M, pltpu.roll(mix, M, 1), mix)
    high = mix.astype(BF16)
    pair, low_pair = high, (mix - high.astype(F32)).astype(BF16)
    left = jnp.concatenate([pair, low_pair], axis=1)
    for r in range(0, CY, 2):
        cols = pl.ds(r * CX, 2 * CX)
        block = hilo_ref[:, cols]
        right = jnp.concatenate([block, block], axis=0)
        res = jnp.dot(left, right, preferred_element_type=F32)
        for half in range(2):
            rows_out[r + half] = res[:, half * CX:(half + 1) * CX] + mean_ref[r + half:r + half + 1, :]
            pltpu.make_async_copy(rows_out.at[r + half], out_hbm.at[:, r + half, :], out_sem).start()
    pltpu.make_async_copy(rows_out, rows_out, out_sem).wait()


def near(array):
    return pltpu.with_memory_space_constraint(array, pltpu.VMEM)


def body(ngy, ngx, ensemble, flow, obs_cell, obs_value, obs_var):
    vmem = pl.BlockSpec(memory_space=pltpu.VMEM)
    hbm = pl.BlockSpec(memory_space=pl.ANY)
    dma = pltpu.SemaphoreType.DMA
    part, hilo, mean = pl.pallas_call(
        functools.partial(forecast_kernel, ngy, ngx),
        out_shape=(
            pltpu.VMEM((24, CX), F32),
            pltpu.VMEM((2 * M, CY * CX), BF16),
            pltpu.VMEM((CY, CX), F32),
        ),
        in_specs=[hbm] * 5,
        out_specs=(vmem,) * 3,
        scratch_shapes=[
            pltpu.VMEM((M, CY, CX), F32),
            pltpu.VMEM((CY + 2, M, CX), F32),
            pltpu.VMEM((CY + 2, M, CX), F32),
            pltpu.VMEM((CY, M, CX), F32),
            pltpu.VMEM((3, CY, CX), F32),
            pltpu.VMEM((5, CY, CX), F32),
            pltpu.SMEM((1, 1, 4), jnp.int32),
            pltpu.SMEM((2, 1, 1, 4), F32),
            pltpu.VMEM((16, CX), F32),
            pltpu.VMEM((2, 8, CX), F32),
            pltpu.VMEM((8, CX), F32),
            pltpu.VMEM((4, M, CX), F32),
            pltpu.VMEM((2, 16, CX), F32),
            pltpu.VMEM((4, 8, CX), F32),
            pltpu.VMEM((4, 8, CX), F32),
            pltpu.VMEM((2, 8, CX), F32),
            pltpu.VMEM((ngx, 2, CX), F32),
            dma((6,)), dma, dma((4,)), dma,
        ],
        compiler_params=pltpu.CompilerParams(collective_id=0, has_side_effects=True),
        name="forecast",
    )(ensemble, flow, obs_cell, obs_value, obs_var)
    gram = pl.pallas_call(
        functools.partial(sum_kernel, ngy),
        out_shape=pltpu.VMEM((24, CX), F32),
        in_specs=[vmem],
        out_specs=vmem,
        scratch_shapes=[
            pltpu.VMEM((ngy // NX4, 24, CX), F32),
            pltpu.VMEM((NX4, 24, CX), F32),
            dma, dma, dma, dma,
        ],
        compiler_params=pltpu.CompilerParams(collective_id=1, has_side_effects=True),
        name="sums",
    )(near(part))
    return pl.pallas_call(
        analysis_kernel,
        out_shape=jax.ShapeDtypeStruct((M, CY, CX), F32),
        in_specs=[vmem] * 3,
        out_specs=hbm,
        scratch_shapes=[pltpu.VMEM((CY, M, CX), F32), dma],
        name="analysis",
    )(near(gram), near(hilo), near(mean))


def solution(mesh):
    tile = P("gy", "gx", None)
    return jax.shard_map(
        functools.partial(body, mesh.shape["gy"], mesh.shape["gx"]),
        mesh=mesh,
        in_specs=(P(None, "gy", "gx"), P(None, "gy", "gx"), tile, tile, tile),
        out_specs=P(None, "gy", "gx"),
        check_vma=False,
    )
```

```python
import functools
import math

import jax
import jax.numpy as jnp
from jax import lax
from jax.experimental import pallas as pl
from jax.experimental.pallas import tpu as pltpu
from jax.sharding import PartitionSpec as P

MESH = pl.DeviceIdType.MESH
M = 64
CY = 8
CX = 128
F32 = jnp.float32
BF16 = jnp.bfloat16
NX4 = 4


def iota(shape, dim):
    return lax.broadcasted_iota(jnp.int32, shape, dim)


def step(x, n, s, w, e, k, hu, hv):
    return x + k * (n + s + w + e - 4.0 * x) - hu * (e - w) - hv * (s - n)


def forecast_kernel(
    ngy, ngx,
    x_hbm, flow_hbm, cell_hbm, val_hbm, var_hbm,
    gram_ref, hilo_ref, mean_ref,
    xb, xr, yr, zr, fl, cf, cells, obs, qs, fs, ct, h_rows, h_sides, h_corners, fh, zc, rf,
    load_sem, corner_send, halo_recv, gx_recv,
):
    gy = lax.axis_index("gy")
    gx = lax.axis_index("gx")
    up, down = gy - 1, gy + 1
    has_up, has_down = gy > 0, gy < ngy - 1
    left, right = lax.rem(gx + ngx - 1, ngx), lax.rem(gx + 1, ngx)
    gx_partners = [(gy, lax.rem(gx + i, ngx)) for i in sorted(range(1, ngx), key=lambda i: -min(i, ngx - i))]

    def load(src, dst, index):
        pltpu.make_async_copy(src, dst, load_sem.at[index]).start()

    def loaded(piece, index):
        pltpu.make_async_copy(piece, piece, load_sem.at[index]).wait()

    for r in (0, 7, 1, 6):
        load(x_hbm.at[:, r, :], xr.at[r + 1], 1)
    load(flow_hbm, fl, 0)
    load(x_hbm, xb, 2)
    for r in (2, 3, 4, 5):
        load(x_hbm.at[:, r, :], xr.at[r + 1], 3)
    load(cell_hbm, cells, 4)
    load(val_hbm, obs.at[0], 5)
    load(var_hbm, obs.at[1], 5)
    barrier = pltpu.get_barrier_semaphore()

    def greet(partners):
        for partner in partners:
            pl.semaphore_signal(barrier, inc=1, device_id=partner, device_id_type=MESH)

    @pl.when(has_up)
    def _():
        greet([(up, gx), (up, left), (up, right)])

    @pl.when(has_down)
    def _():
        greet([(down, gx), (down, left), (down, right)])

    greet(gx_partners)

    lane = iota((8, CX), 1)
    sub = iota((8, CX), 0)
    edge = (lane <= 1) | (lane >= CX - 2)
    s0, s7 = sub == 0, sub == 7
    l0, l127 = lane == 0, lane == CX - 1
    quad = lane & 3
    q0, q1, q3 = quad == 0, quad == 1, quad == 3
    west_side = quad >= 2

    sends = [load_sem.at[0], load_sem.at[2], load_sem.at[1], corner_send]
    gx_send = load_sem.at[3]

    def remote(src, dst, index, target):
        return pltpu.make_async_remote_copy(
            src_ref=src, dst_ref=dst, send_sem=sends[index], recv_sem=halo_recv.at[index],
            device_id=target, device_id_type=MESH,
        )

    def start(index, to_up, to_down, to_left=None, to_right=None):
        @pl.when(has_up)
        def _():
            for src, dst, target in to_up:
                remote(src, dst, index, (up, target)).start()

        @pl.when(has_down)
        def _():
            for src, dst, target in to_down:
                remote(src, dst, index, (down, target)).start()

        if to_left:
            remote(*to_left, index, (gy, left)).start()
            remote(*to_right, index, (gy, right)).start()

    both = has_up & has_down

    def settle(sem, buffer, most, least):
        def wait(count):
            piece = buffer.at[pl.ds(0, count)]
            pltpu.make_async_copy(piece, piece, sem).wait()

        if most == least:
            wait(most)
        else:
            pl.when(both)(lambda: wait(most))
            pl.when(jnp.logical_not(both))(lambda: wait(least))

    groups = [(fh, 4, 3), (h_sides, 2, 2), (h_rows, 4, 2), (h_corners, 4, 2)]

    def received(index):
        settle(halo_recv.at[index], *groups[index])

    loaded(fl, 0)
    qc = jnp.where(edge, fl[0], 0.0)
    for i in range(1, 3):
        qc = qc + pltpu.roll(jnp.where(edge, fl[i], 0.0), 4 * i, 1)
    fs[1] = qc
    for i in range(3):
        fs[0, pl.ds(i, 1), :] = fl[i, 0:1, :]
        fs[0, pl.ds(3 + i, 1), :] = fl[i, 7:8, :]
    loaded(xr.at[pl.ds(0, 4)], 1)

    ends = l0 | l127
    tile = jnp.zeros((8, CX), F32)
    for b in range(8):
        rows = pl.ds(8 * b, 8)
        tile = tile + pltpu.roll(jnp.where(ends, xr[1, rows, :], 0.0), 4 * b, 1)
        tile = tile + pltpu.roll(jnp.where(ends, xr[8, rows, :], 0.0), 4 * b + 2, 1)
    ct[...] = tile

    @pl.when(both)
    def _():
        pl.semaphore_wait(barrier, ngx + 5)

    @pl.when(jnp.logical_not(both))
    def _():
        pl.semaphore_wait(barrier, ngx + 2)

    start(
        3,
        [(ct, h_corners.at[3], left), (ct, h_corners.at[2], right)],
        [(ct, h_corners.at[1], left), (ct, h_corners.at[0], right)],
    )
    start(0, [(fs.at[0], fh.at[1], gx)], [(fs.at[0], fh.at[0], gx)], (fs.at[1], fh.at[2]), (fs.at[1], fh.at[3]))
    start(2, [(xr.at[pl.ds(1, 2)], h_rows.at[pl.ds(2, 2)], gx)], [(xr.at[pl.ds(7, 2)], h_rows.at[pl.ds(0, 2)], gx)])
    loaded(xb, 2)

    def pack(half):
        sums = [None] * 4
        for m in range(32):
            piece = pltpu.roll(jnp.where(edge, xb[half * 32 + m], 0.0), (CX - 4 * m) % CX, 1)
            sums[m % 4] = piece if m < 4 else sums[m % 4] + piece
        return (sums[0] + sums[1]) + (sums[2] + sums[3])

    qa, qb = pack(0), pack(1)
    qs[pl.ds(0, 8), :] = qa
    qs[pl.ds(8, 8), :] = qb
    start(1, [], [], (qs, h_sides.at[0]), (qs, h_sides.at[1]))
    loaded(xr.at[pl.ds(0, 4)], 3)
    loaded(cells, 4)
    loaded(obs, 5)

    def weights(f0, f1, f2):
        hu, hv = 0.5 * f1, 0.5 * f2
        return 1.0 - 4.0 * f0, f0 + hv, f0 - hv, f0 + hu, f0 - hu

    own = weights(fl[0], fl[1], fl[2])
    a0, an, as_, aw, ae = own
    aw_in, ae_in = jnp.where(l0, 0.0, aw), jnp.where(l127, 0.0, ae)
    for i, v in enumerate((a0, an, as_, aw_in, ae_in)):
        cf[i] = v

    blank = jnp.zeros((M, CX), F32)
    xr[0] = blank
    xr[9] = blank
    yr[0] = blank
    yr[9] = blank

    def inner(source, target, shift):
        def body(r, carry):
            c = [jnp.broadcast_to(cf[i, pl.ds(r, 1), :], (8, CX)) for i in range(5)]
            for b in range(8):
                rows = pl.ds(8 * b, 8)
                x = source[r + 1, rows, :]
                target[r + shift, rows, :] = (
                    (c[0] * x + c[1] * source[r, rows, :]) + (c[2] * source[r + 2, rows, :] + c[3] * pltpu.roll(x, 1, 1))
                    + c[4] * pltpu.roll(x, CX - 1, 1)
                )
            return carry
        lax.fori_loop(0, CY, body, 0)

    inner(xr, yr, 1)
    inner(yr, zr, 0)

    def col(v, l):
        return jnp.broadcast_to(v[:, l:l + 1], (8, CX))

    c_edge = jnp.where(q0, col(aw, 0), jnp.where(q3, col(ae, CX - 1), 0.0))
    a0_edge = jnp.where(q0, col(a0, 0), col(a0, CX - 1))
    an_edge = jnp.where(s0, 0.0, jnp.where(q0, col(an, 0), col(an, CX - 1)))
    as_edge = jnp.where(s7, 0.0, jnp.where(q0, col(as_, 0), col(as_, CX - 1)))
    c_next = jnp.where(q1, col(aw, 1), col(ae, CX - 2))

    has_left, has_right = gx > 0, gx < ngx - 1

    def on(flag):
        return jnp.full((8, CX), jnp.where(flag, 1, 0), jnp.int32) > 0

    cmask = (west_side & on(has_left)) | ((quad <= 1) & on(has_right))

    received(0)

    def flow_cols(i):
        west, east = col(fh[3], (4 * i - 1) % CX), col(fh[2], 4 * i)
        return jnp.where(cmask, jnp.where(west_side, west, east), 0.0)

    kc, uc, vc = flow_cols(0), 0.5 * flow_cols(1), 0.5 * flow_cols(2)

    def outer_row(tile, offset, flag):
        fields = [jnp.where(on(flag), jnp.broadcast_to(tile[offset + i:offset + i + 1, :], (8, CX)), 0.0) for i in range(3)]
        return weights(*fields)

    def line(v, r):
        return jnp.broadcast_to(v[r:r + 1, :], (8, CX))

    ends_in = (l0 & on(has_left)) | (l127 & on(has_right))

    def beside(i):
        return jnp.where(l0, pltpu.roll(fh[3], (1 - 4 * i) % CX, 1), pltpu.roll(fh[2], CX - 1 - 4 * i, 1))

    k_side, v_side = beside(0), 0.5 * beside(2)

    def outside(above):
        if above:
            t0, tn, ts, tw, te = outer_row(fh[0], 3, has_up)
            r, near, far, cross, toward = 0, line(an, 0), tn, ts, line(an, 1)
            side = line(k_side + v_side, 0)
        else:
            t0, tn, ts, tw, te = outer_row(fh[1], 0, has_down)
            r, near, far, cross, toward = 7, line(as_, 7), ts, tn, line(as_, 6)
            side = line(k_side - v_side, 7)
        west = near * jnp.where(l0, 0.0, tw) + line(aw_in, r) * pltpu.roll(near, 1, 1)
        east = near * jnp.where(l127, 0.0, te) + line(ae_in, r) * pltpu.roll(near, CX - 1, 1)
        corner = jnp.where(l0, near * tw + line(aw, r) * side, near * te + line(ae, r) * side)
        corner = jnp.where(ends_in, corner, 0.0)
        return near * (t0 + line(a0, r)), near * far, near * cross, west, east, toward * near, corner

    above = outside(True)
    below = outside(False)

    received(1)
    west_cell = q3
    for half in range(2):
        q = (qa, qb)[half]
        rows = pl.ds(8 * half, 8)
        ring = jnp.where(cmask, jnp.where(west_side, h_sides[1, rows, :], h_sides[0, rows, :]), 0.0)
        n = pltpu.roll(jnp.where(s7, 0.0, ring), 1, 0)
        s = pltpu.roll(jnp.where(s0, 0.0, ring), 7, 0)
        ring_w, ring_e = pltpu.roll(ring, 1, 1), pltpu.roll(ring, CX - 1, 1)
        w = jnp.where(west_cell, ring_w, pltpu.roll(q, 1, 1))
        e = jnp.where(west_cell, pltpu.roll(q, CX - 1, 1), ring_e)
        ring1 = step(ring, n, s, w, e, kc, uc, vc)
        x1 = jnp.where(q0, ring_w, ring_e)
        y1 = jnp.where(q0, pltpu.roll(ring1, 1, 1), pltpu.roll(ring1, CX - 1, 1))
        d = c_edge * x1
        at_edge = a0_edge * d + an_edge * pltpu.roll(d, 1, 0) + as_edge * pltpu.roll(d, 7, 0) + c_edge * y1
        inside = c_next * jnp.where(q1, pltpu.roll(d, 1, 1), pltpu.roll(d, CX - 1, 1))
        zc[half] = jnp.where(q0 | q3, at_edge, inside)

    received(2)
    received(3)

    def add_rows(flag, c, near_row, far_row, r, r_in, corners, first):
        @pl.when(flag)
        def _():
            merged = corners()
            for b in range(8):
                rows = pl.ds(8 * b, 8)
                p = h_rows[near_row, rows, :]
                zr[r, rows, :] = zr[r, rows, :] + (
                    (c[0] * p + c[1] * h_rows[far_row, rows, :]) + (c[2] * xr[r + 1, rows, :] + c[3] * pltpu.roll(p, 1, 1))
                    + (c[4] * pltpu.roll(p, CX - 1, 1) + c[6] * pltpu.roll(merged, (first - 4 * b) % CX, 1))
                )
                zr[r_in, rows, :] = zr[r_in, rows, :] + c[5] * p

    add_rows(has_up, above, 1, 0, 0, 1, lambda: jnp.where(q1, h_corners[0], pltpu.roll(h_corners[1], CX - 2, 1)), CX - 1)
    add_rows(has_down, below, 2, 3, 7, 6, lambda: jnp.where(q3, h_corners[2], pltpu.roll(h_corners[3], CX - 2, 1)), 1)

    def with_columns(r, b, lines):
        spread = pltpu.roll(lines[b // 4], 32 * (b % 4), 1, stride=4, stride_axis=0)
        return zr[r, 8 * b:8 * b + 8, :] + jnp.where(edge, spread, 0.0)

    def column_lines(r):
        return [jnp.broadcast_to(zc[half, pl.ds(r, 1), :], (8, CX)) for half in range(2)]

    lane64 = iota((M, CX), 1)
    diag64 = lane64 == iota((M, CX), 0)
    ones = jnp.zeros((1, CX), F32)
    picked = []
    for j in range(4):
        cell = cells[0, 0, j]
        row, place = lax.shift_right_logical(cell, 7), cell & (CX - 1)
        lines = column_lines(row)
        field = jnp.concatenate([with_columns(row, b, lines) for b in range(8)], axis=0)
        column = jnp.sum(jnp.where(lane64 == place, field, 0.0), axis=1, keepdims=True)
        column = jnp.broadcast_to(column, (M, CX))
        average = jnp.sum(column, axis=0, keepdims=True) * (1.0 / M)
        factor = lax.rsqrt(ones + obs[1, 0, 0, j])
        values = jnp.sum(jnp.where(diag64, column, 0.0), axis=0, keepdims=True)
        values = jnp.where(iota((1, CX), 1) < M - 1, values, ones + obs[0, 0, 0, j])
        picked.append(jnp.where(iota((1, CX), 1) < M, (values - average) * factor, 0.0))
    rf[gx] = jnp.concatenate(
        [picked[0] + pltpu.roll(picked[2], M, 1), picked[1] + pltpu.roll(picked[3], M, 1)], axis=0
    )

    gx_copies = [
        pltpu.make_async_remote_copy(
            src_ref=rf.at[gx], dst_ref=rf.at[gx], send_sem=gx_send, recv_sem=gx_recv,
            device_id=partner, device_id_type=MESH,
        )
        for partner in gx_partners
    ]
    for copy in gx_copies:
        copy.start()

    for r in range(CY):
        lines = column_lines(r)
        field = jnp.concatenate([with_columns(r, b, lines) for b in range(8)], axis=0)
        mean = jnp.sum(field, axis=0, keepdims=True) * (1.0 / M)
        mean_ref[pl.ds(r, 1), :] = mean
        field = field - mean
        high = field.astype(BF16)
        hilo_ref[pl.ds(0, M), pl.ds(r * CX, CX)] = high
        hilo_ref[pl.ds(M, M), pl.ds(r * CX, CX)] = (field - high.astype(F32)).astype(BF16)

    for index, group in enumerate(groups):
        settle(sends[index], *group)

    wait_all(rf, ngx - 1, gx_send)
    wait_all(rf, ngx - 1, gx_recv)
    gathered = jnp.concatenate([rf[i] for i in range(ngx)], axis=0)
    lane32 = iota((2 * ngx, CX), 1)
    rows = jnp.concatenate(
        [jnp.where(lane32 < M, gathered, 0.0), jnp.where(lane32 < M, pltpu.roll(gathered, M, 1), 0.0)], axis=0
    )
    gram = jnp.dot(rows.T[0:M], rows, precision=lax.Precision.HIGHEST, preferred_element_type=F32)
    high, low = gram[0:32], pltpu.roll(gram[32:64], CX - 32, 1)
    across, along = iota((32, CX), 1), iota((32, CX), 0)
    square = jnp.where((across < 32) & (across > along), low, high)
    gram_ref[pl.ds(0, 16), :] = square[0:16] + pltpu.roll(square[16:32], M, 1)
    diagonal = jnp.sum(jnp.where(across == along, low, 0.0), axis=0, keepdims=True)
    gram_ref[pl.ds(16, 8), :] = jnp.where(iota((8, CX), 0) == 0, diagonal, 0.0)


def wait_all(buffer, count, sem):
    piece = buffer.at[pl.ds(0, count)]
    pltpu.make_async_copy(piece, piece, sem).wait()


def sum_kernel(ngy, part_ref, gram_ref, rz, rx, z_send, z_recv, x_send, x_recv):
    gy = lax.axis_index("gy")
    gx = lax.axis_index("gx")
    nz = ngy // NX4
    zpos = gy // NX4
    xpos = lax.rem(gy, NX4)
    z_partners = [(lax.rem(gy + NX4 * i, ngy), gx) for i in sorted(range(1, nz), key=lambda i: -min(i, nz - i))]
    x_partners = [(zpos * NX4 + lax.rem(xpos + i, NX4), gx) for i in (2, 1, 3)]
    barrier = pltpu.get_barrier_semaphore()
    for partner in z_partners + x_partners:
        pl.semaphore_signal(barrier, inc=1, device_id=partner, device_id_type=MESH)
    pl.semaphore_wait(barrier, nz + NX4 - 2)

    def wait_rows(buffer, count, sem):
        piece = buffer.at[pl.ds(0, count), pl.ds(0, 17)]
        pltpu.make_async_copy(piece, piece, sem).wait()

    def spread(source, buffer, slot, partners, send, recv):
        for partner in partners:
            pltpu.make_async_remote_copy(
                src_ref=source.at[pl.ds(0, 17)], dst_ref=buffer.at[slot, pl.ds(0, 17)], send_sem=send, recv_sem=recv,
                device_id=partner, device_id_type=MESH,
            ).start()

    spread(part_ref, rz, zpos, z_partners, z_send, z_recv)
    rz[zpos] = part_ref[...]
    wait_rows(rz, nz - 1, z_recv)
    part = rz[0]
    for i in range(1, nz):
        part = part + rz[i]
    rx[xpos] = part
    spread(rx.at[xpos], rx, xpos, x_partners, x_send, x_recv)
    wait_rows(rz, nz - 1, z_send)
    wait_rows(rx, NX4 - 1, x_recv)
    gram_ref[...] = (rx[0] + rx[1]) + (rx[2] + rx[3])
    wait_rows(rx, NX4 - 1, x_send)


def analysis_kernel(gram_ref, hilo_ref, mean_ref, out_hbm, rows_out, out_sem):
    lane = iota((8, CX), 1)
    sub = iota((8, CX), 0)
    packed = gram_ref[pl.ds(0, 16), :]
    square = jnp.concatenate([packed, pltpu.roll(packed, M, 1)], axis=0)
    square = jnp.where(iota((32, CX), 1) < M, square, 0.0)
    turned = jnp.concatenate([square, jnp.zeros((CX - 32, CX), F32)], axis=0).T
    across, along = iota((32, CX), 1), iota((32, CX), 0)
    top = jnp.where((across < 32) & (across > along), turned[0:32], square)
    corner = jnp.where(across > along, square, jnp.where(across == along, gram_ref[pl.ds(16, 1), :], turned[0:32]))
    corner = pltpu.roll(jnp.where(across < 32, corner, 0.0), 32, 1)
    bottom = jnp.where(across < 32, turned[32:64], corner)
    blocks = [top[8 * i:8 * i + 8] for i in range(4)] + [bottom[8 * i:8 * i + 8] for i in range(4)]
    blocks = [jnp.where(lane < M - 1, b, 0.0) for b in blocks]
    row_sums = [jnp.sum(b, axis=1, keepdims=True) for b in blocks]
    eyes = [lane == sub + 8 * i for i in range(8)]
    diagonals = [jnp.where(e, b, 0.0) for e, b in zip(eyes, blocks)]
    last = sub == 7
    target_row = blocks[7][7:8] + jnp.where(lane[0:1] == M - 1, -row_sums[7][7:8], 0.0)
    blocks[7] = jnp.where(last, 0.0, blocks[7])
    row_sums[7] = jnp.where(last[:, 0:1], 0.0, row_sums[7])
    col_sum = functools.reduce(jnp.add, blocks)
    col_sum = jnp.sum(col_sum, axis=0, keepdims=True)
    all_sum = jnp.sum(functools.reduce(jnp.add, row_sums), axis=0, keepdims=True)
    blocks = [jnp.where(lane == M - 1, -r, b) for b, r in zip(blocks, row_sums)]
    blocks[7] = jnp.where(last, jnp.where(lane == M - 1, all_sum, -col_sum), blocks[7])
    scale_row = jnp.sum(functools.reduce(jnp.add, diagonals), axis=0, keepdims=True)
    scale_row = lax.rsqrt((M - 1.0) + jnp.where(lane[0:1] == M - 1, all_sum, scale_row))
    scale_col = [jnp.sum(d, axis=1, keepdims=True) for d in diagonals]
    scale_col[7] = jnp.where(last[:, 0:1], all_sum, scale_col[7])
    scale_col = [lax.rsqrt((M - 1.0) + c) for c in scale_col]
    blocks = [jnp.where(e, b + (M - 1.0), b) for e, b in zip(eyes, blocks)]
    a = [
        jnp.where(lane == sub + (M + 8 * i), scale_col[i], jnp.where(lane < M, blocks[i] * scale_col[i] * scale_row, 0.0))
        for i in range(8)
    ]

    lower = [None] * 8
    heads = []
    target_high = pltpu.roll(jnp.broadcast_to(target_row, (8, CX)), M, 1)
    nothing = 0.0 * packed[0:8]
    for p in range(16):
        b, o = p // 2, 4 * (p % 2)
        cols = {
            (t, i): jnp.broadcast_to(a[i][:, 4 * p + t:4 * p + t + 1], (8, CX)) for t in range(4) for i in range(b, 8)
        }
        cols = {key: v + nothing if key[1] == b else v for key, v in cols.items()}
        d = {
            (s, t): jnp.broadcast_to(cols[t, b][o + s:o + s + 1, :], (8, CX)) for s in range(4) for t in range(s + 1)
        }
        r = [jnp.broadcast_to(a[b][o + s:o + s + 1, :], (8, CX)) for s in range(4)]

        det = d[0, 0] * d[1, 1] - d[1, 0] * d[1, 0]
        inv = 1.0 / det
        f00 = d[1, 1] * d[2, 0] - d[1, 0] * d[2, 1]
        f10 = d[0, 0] * d[2, 1] - d[1, 0] * d[2, 0]
        f01 = d[1, 1] * d[3, 0] - d[1, 0] * d[3, 1]
        f11 = d[0, 0] * d[3, 1] - d[1, 0] * d[3, 0]
        g00 = det * d[2, 2] - (d[2, 0] * f00 + d[2, 1] * f10)
        g10 = det * d[3, 2] - (d[3, 0] * f00 + d[3, 1] * f10)
        g11 = det * d[3, 3] - (d[3, 0] * f01 + d[3, 1] * f11)
        det2 = g00 * g11 - g10 * g10
        i00, i10, i11 = d[1, 1] * inv, -d[1, 0] * inv, d[0, 0] * inv
        e00, e10, e01, e11 = f00 * inv, f10 * inv, f01 * inv, f11 * inv
        r2 = r[2] - (e00 * r[0] + e10 * r[1])
        r3 = r[3] - (e01 * r[0] + e11 * r[1])
        if p < 15:
            u0 = i00 * r[0] + i10 * r[1]
            u1 = i10 * r[0] + i11 * r[1]
            inv2 = det * (1.0 / det2)
            t2, t3 = g11 * r2 - g10 * r3, g00 * r3 - g10 * r2
            z2, z3 = t2 * inv2, t3 * inv2
            z0 = u0 - (e00 * z2 + e01 * z3)
            z1 = u1 - (e10 * z2 + e11 * z3)
            z = (z0, z1, z2, z3)
            for i in range(b if o == 0 else b + 1, 8):
                if i == (b if o == 0 else b + 1):
                    m2 = cols[2, i] - (cols[0, i] * e00 + cols[1, i] * e10)
                    m3 = cols[3, i] - (cols[0, i] * e01 + cols[1, i] * e11)
                    new = (a[i] - (cols[0, i] * u0 + cols[1, i] * u1)) - inv2 * (m2 * t2 + m3 * t3)
                else:
                    new = a[i] - ((cols[0, i] * z[0] + cols[1, i] * z[1]) + (cols[2, i] * z[2] + cols[3, i] * z[3]))
                a[i] = jnp.where(sub >= 4, new, a[i]) if i == b else new
        n0 = r[0] * lax.rsqrt(d[0, 0])
        n1 = (d[0, 0] * r[1] - d[1, 0] * r[0]) * lax.rsqrt(d[0, 0] * det)
        c00, c10 = g00 * inv, g10 * inv
        n2 = r2 * lax.rsqrt(c00)
        n3 = (c00 * r3 - c10 * r2) * lax.rsqrt(c00 * (det2 * inv * inv))
        rows = jnp.where(sub == o, n0, jnp.where(sub == o + 1, n1, jnp.where(sub == o + 2, n2, n3)))
        lower[b] = rows if o == 0 else jnp.where(sub >= 4, rows, lower[b])
        if o:
            lower[b] = jnp.where(lane >= M, lower[b], 0.0)
            heads.append(jnp.sum(lower[b] * target_high, axis=1, keepdims=True))
    weight = jnp.sum(functools.reduce(jnp.add, [v * h for v, h in zip(lower, heads)]), axis=0, keepdims=True)
    root = math.sqrt(M - 1.0)
    mix = jnp.concatenate([root * v + weight for v in lower], axis=0)
    mix = jnp.where(iota((M, CX), 1) < M, pltpu.roll(mix, M, 1), mix)
    high = mix.astype(BF16)
    pair, low_pair = high, (mix - high.astype(F32)).astype(BF16)
    left = jnp.concatenate([pair, low_pair], axis=1)
    for r in range(0, CY, 2):
        cols = pl.ds(r * CX, 2 * CX)
        block = hilo_ref[:, cols]
        right = jnp.concatenate([block, block], axis=0)
        res = jnp.dot(left, right, preferred_element_type=F32)
        for half in range(2):
            rows_out[r + half] = res[:, half * CX:(half + 1) * CX] + mean_ref[r + half:r + half + 1, :]
            pltpu.make_async_copy(rows_out.at[r + half], out_hbm.at[:, r + half, :], out_sem).start()
    pltpu.make_async_copy(rows_out, rows_out, out_sem).wait()


def near(array):
    return pltpu.with_memory_space_constraint(array, pltpu.VMEM)


def body(ngy, ngx, ensemble, flow, obs_cell, obs_value, obs_var):
    vmem = pl.BlockSpec(memory_space=pltpu.VMEM)
    hbm = pl.BlockSpec(memory_space=pl.ANY)
    dma = pltpu.SemaphoreType.DMA
    part, hilo, mean = pl.pallas_call(
        functools.partial(forecast_kernel, ngy, ngx),
        out_shape=(
            pltpu.VMEM((24, CX), F32),
            pltpu.VMEM((2 * M, CY * CX), BF16),
            pltpu.VMEM((CY, CX), F32),
        ),
        in_specs=[hbm] * 5,
        out_specs=(vmem,) * 3,
        scratch_shapes=[
            pltpu.VMEM((M, CY, CX), F32),
            pltpu.VMEM((CY + 2, M, CX), F32),
            pltpu.VMEM((CY + 2, M, CX), F32),
            pltpu.VMEM((CY, M, CX), F32),
            pltpu.VMEM((3, CY, CX), F32),
            pltpu.VMEM((5, CY, CX), F32),
            pltpu.SMEM((1, 1, 4), jnp.int32),
            pltpu.SMEM((2, 1, 1, 4), F32),
            pltpu.VMEM((16, CX), F32),
            pltpu.VMEM((2, 8, CX), F32),
            pltpu.VMEM((8, CX), F32),
            pltpu.VMEM((4, M, CX), F32),
            pltpu.VMEM((2, 16, CX), F32),
            pltpu.VMEM((4, 8, CX), F32),
            pltpu.VMEM((4, 8, CX), F32),
            pltpu.VMEM((2, 8, CX), F32),
            pltpu.VMEM((ngx, 2, CX), F32),
            dma((6,)), dma, dma((4,)), dma,
        ],
        compiler_params=pltpu.CompilerParams(collective_id=0, has_side_effects=True),
        name="forecast",
    )(ensemble, flow, obs_cell, obs_value, obs_var)
    gram = pl.pallas_call(
        functools.partial(sum_kernel, ngy),
        out_shape=pltpu.VMEM((24, CX), F32),
        in_specs=[vmem],
        out_specs=vmem,
        scratch_shapes=[
            pltpu.VMEM((ngy // NX4, 24, CX), F32),
            pltpu.VMEM((NX4, 24, CX), F32),
            dma, dma, dma, dma,
        ],
        compiler_params=pltpu.CompilerParams(collective_id=1, has_side_effects=True),
        name="sums",
    )(near(part))
    return pl.pallas_call(
        analysis_kernel,
        out_shape=jax.ShapeDtypeStruct((M, CY, CX), F32),
        in_specs=[vmem] * 3,
        out_specs=hbm,
        scratch_shapes=[pltpu.VMEM((CY, M, CX), F32), dma],
        name="analysis",
    )(near(gram), near(hilo), near(mean))


def solution(mesh):
    tile = P("gy", "gx", None)
    return jax.shard_map(
        functools.partial(body, mesh.shape["gy"], mesh.shape["gx"]),
        mesh=mesh,
        in_specs=(P(None, "gy", "gx"), P(None, "gy", "gx"), tile, tile, tile),
        out_specs=P(None, "gy", "gx"),
        check_vma=False,
    )
```
